128 devices in a mesh: row: 8 (over x_hi, y), col: 16 (over x_lo, z, core).
Axes of the slice: x: 4 (x_hi: 2, x_lo: 2; x = x_hi * 2 + x_lo), y: 4, z: 4, core: 2. Of those that a mesh axis runs over, the one named last changes fastest.
Arguments:
- trailing: bfloat16 [8192, 16384], P('row', 'col'), may hold values from -6 to 6
- raw_l: bfloat16 [8, 16, 1024, 1024], P('row', None, 'col'), may hold values from -1.1953125 to 1.1953125
- raw_u: bfloat16 [16, 16, 1024, 1024], P(None, 'col', 'row'), may hold values from -1.1953125 to 1.1953125
- sketch: bfloat16 [8, 16, 1024, 192], P('row', 'col'), may hold values from -0.1875 to 0.1875
- helper_l: int32 [8, 16], P('row'), may hold values from 0 to 15, as said below
- helper_u: int32 [16, 16], P(None, 'col'), may hold values from 0 to 7, as said below
- ranks_l: int32 [8, 16], P('row'), may hold values from 64 to 192, as said below
- ranks_u: int32 [16, 16], P(None, 'col'), may hold values from 64 to 192, as said below
Outputs:
- updated: float32 [8192, 16384], P('row', 'col')
The draws below stay inside these ranges and needn't reach their ends.
Inputs may be any that keep to these rules, and one draw needn't show every extreme that they name: `helper_l`: in every grid row no value occurs more than 2 times, and some value occurs exactly 2 times. `helper_u`: in every grid column no value occurs more than 4 times, and some value occurs exactly 4 times. `ranks_l`: some tile has rank 64 and some tile rank 192. `ranks_u`: some tile has rank 64 and some tile rank 192.
All inputs are finite; a program needn't handle non-finite values.
Results may differ from the reference program's by a relative error of at most 0.0068.
Values may be sent and summed in bfloat16 or wider, within the bound.
A program may use at most 192 MiB of HBM per device.

```python
import jax
import jax.numpy as jnp
from jax import lax

B = 1024
RMAX = 192
RLO = 64
KD = 16
CAP_L = 2
CAP_U = 4
N_ROW = 8
N_COL = 16


def spread_helpers(key, groups, count, owners, capacity):

    def one_group(group):
        group_key = jax.random.fold_in(key, group)
        order = jax.random.permutation(group_key, owners * capacity).astype(jnp.int32)
        chosen = order[0] // capacity
        for place in range(capacity):
            partner = chosen * capacity + place
            where_at = jnp.argmax(order == partner)
            moved = order[place]
            order = order.at[where_at].set(moved).at[place].set(partner)
        return order[:count] // capacity
    return jax.vmap(one_group)(jnp.arange(groups, dtype=jnp.int32))


def pick_ranks(key, shape):
    values = jax.random.randint(key, shape, RLO, RMAX + 1, dtype=jnp.int32).reshape(-1)
    total = values.shape[0]
    first = jax.random.randint(jax.random.fold_in(key, 1), (), 0, total, dtype=jnp.int32)
    offset = jax.random.randint(jax.random.fold_in(key, 2), (), 0, total - 1, dtype=jnp.int32)
    second = (first + 1 + offset) % total
    values = values.at[first].set(RMAX).at[second].set(RLO)
    return values.reshape(shape)


def draw_helper_l(key, part):
    return spread_helpers(jax.random.fold_in(key, 11), N_ROW, KD, N_COL, CAP_L)


def draw_helper_u(key, part):
    return spread_helpers(jax.random.fold_in(key, 13), N_COL, KD, N_ROW, CAP_U).T


def draw_ranks_l(key, part):
    return pick_ranks(jax.random.fold_in(key, 17), (N_ROW, KD))


def draw_ranks_u(key, part):
    return pick_ranks(jax.random.fold_in(key, 19), (KD, N_COL))


def shard_levels(rng, extent, split, least, largest):
    def one(position, shards_of):
        heights = jax.random.uniform(jax.random.fold_in(jax.random.fold_in(rng, 6), position), (shards_of,), jnp.float32, least / len(split), largest / len(split))
        return jnp.repeat(jnp.exp(heights), extent[position] // shards_of).reshape((-1,) + (1,) * (len(extent) - position - 1))

    factor_of = one(*split[0])
    for cut in split[1:]:
        factor_of = factor_of * one(*cut)
    return factor_of


def gaussian(key, dims, width, limit, cuts=(), kind=jnp.bfloat16):
    values = jax.random.normal(key, dims, jnp.float32) * width
    if len(cuts) > 0:
        values = shard_levels(key, dims, cuts, -0.22, 0.18) * values
    return jnp.clip(values, min=-limit, max=limit).astype(kind)


def setup_inputs(seed: int = 0) -> dict:
    key_list = jax.random.split(jax.random.key(seed), 9)
    return {
        "trailing": gaussian(key_list[0], (N_ROW * B, N_COL * B), 1.0, 6.0, ((0, 8), (1, 16))),
        "raw_l": gaussian(key_list[1], (N_ROW, KD, B, B), 0.2, 1.1953125, ((0, 8), (2, 16))),
        "raw_u": gaussian(key_list[2], (KD, N_COL, B, B), 0.2, 1.1953125, ((1, 16), (2, 8))),
        "sketch": gaussian(key_list[3], (N_ROW, N_COL, B, RMAX), B ** -0.5, 0.1875, ((0, 8), (1, 16))),
        "helper_l": draw_helper_l(jax.random.fold_in(key_list[8], 71), 0),
        "helper_u": draw_helper_u(jax.random.fold_in(key_list[8], 71), 0),
        "ranks_l": draw_ranks_l(jax.random.fold_in(key_list[8], 71), 0),
        "ranks_u": draw_ranks_u(jax.random.fold_in(key_list[8], 71), 0),
    }


def compress_tile(panel_tile, tile_rank, sketch_cols):
    keep_cols = jnp.arange(sketch_cols.shape[1]) < tile_rank
    masked = jnp.where(keep_cols[None, :], sketch_cols, jnp.zeros_like(sketch_cols))
    sketched = jnp.dot(panel_tile.astype(jnp.float32), masked.astype(jnp.float32), preferred_element_type=jnp.float32)
    padding = jnp.where(keep_cols, 1.0, 1.0) - jnp.where(keep_cols, 1.0, 0.0)
    gram = jnp.dot(sketched.T, sketched, precision=lax.Precision.HIGHEST) + jnp.diag(padding.astype(jnp.float32))
    lower_factor = jnp.linalg.cholesky(gram)
    basis = jax.scipy.linalg.solve_triangular(lower_factor, sketched.T, lower=True).T.astype(jnp.bfloat16)
    coeffs = lax.dot_general(panel_tile.astype(jnp.float32), basis.astype(jnp.float32), (((0,), (0,)), ((), ())), preferred_element_type=jnp.float32).astype(jnp.bfloat16)
    return jnp.concatenate([basis, coeffs], axis=1)

def reference(trailing, raw_l, raw_u, sketch, helper_l, helper_u, ranks_l, ranks_u):
    width_r = sketch.shape[3]
    grid_rows = jnp.repeat(jnp.arange(N_ROW, dtype=jnp.int32), KD)
    grid_cols = jnp.tile(jnp.arange(N_COL, dtype=jnp.int32), KD)

    def make_row(item):
        panel_tile, tile_rank, grid_row, helper = item
        return compress_tile(panel_tile, tile_rank, sketch[grid_row, helper])

    def make_col(item):
        panel_tile, tile_rank, grid_col, helper = item
        return compress_tile(panel_tile, tile_rank, sketch[helper, grid_col])
    made_row = lax.map(make_row, (raw_l.reshape(N_ROW * KD, B, B), ranks_l.reshape(-1), grid_rows, helper_l.reshape(-1)))
    made_row = made_row.reshape(N_ROW, KD, B, 2 * width_r)
    made_col = lax.map(make_col, (raw_u.reshape(KD * N_COL, B, B), ranks_u.reshape(-1), grid_cols, helper_u.reshape(-1)))
    made_col = made_col.reshape(KD, N_COL, B, 2 * width_r)

    def update_tile(pair):
        grid_row = (pair // N_COL).astype(jnp.int32)
        grid_col = (pair % N_COL).astype(jnp.int32)
        full_row = made_row[grid_row].astype(jnp.float32)
        full_col = made_col[:, grid_col].astype(jnp.float32)
        middle = jnp.einsum('kbr,kbs->krs', full_row[:, :, width_r:], full_col[:, :, :width_r])
        middle = lax.optimization_barrier(middle.astype(jnp.bfloat16)).astype(jnp.float32)
        left = jnp.einsum('kbr,krs->kbs', full_row[:, :, :width_r], middle)
        left = lax.optimization_barrier(left.astype(jnp.bfloat16)).astype(jnp.float32)
        update = jnp.einsum('kbs,kcs->bc', left, full_col[:, :, width_r:])
        start = lax.dynamic_slice(trailing, ((grid_row * B).astype(jnp.int32), (grid_col * B).astype(jnp.int32)), (B, B))
        return start.astype(jnp.float32) - update
    tiles = lax.map(update_tile, jnp.arange(N_ROW * N_COL, dtype=jnp.int32))
    return tiles.reshape(N_ROW, N_COL, B, B).transpose(0, 2, 1, 3).reshape(N_ROW * B, N_COL * B)
```

```python
import jax
import jax.numpy as jnp
from jax import lax
from jax.sharding import Mesh
from jax.sharding import PartitionSpec as P
from jax.experimental import pallas as pl
from jax.experimental.pallas import tpu as pltpu

HI = lax.Precision.HIGHEST


def _eliminate(a, n):
    rows = lax.broadcasted_iota(jnp.int32, (1, n, 1), 1)
    cols = lax.broadcasted_iota(jnp.int32, (1, 1, n), 2)
    ident = jnp.broadcast_to((rows == cols).astype(jnp.float32), a.shape)

    def step(j, carry):
        xa, xb = carry
        at_row = rows == j
        at_col = cols == j
        row_a = jnp.sum(jnp.where(at_row, xa, 0.0), axis=1, keepdims=True)
        row_b = jnp.sum(jnp.where(at_row, xb, 0.0), axis=1, keepdims=True)
        col = jnp.sum(jnp.where(at_col, xa, 0.0), axis=2, keepdims=True)
        pivot = jnp.sum(jnp.where(at_col, row_a, 0.0), axis=2, keepdims=True)
        scale = 1.0 / jnp.sqrt(pivot)
        ra = row_a * scale
        rb = row_b * scale
        mult = jnp.where(rows > j, col * scale, 0.0)
        xa = jnp.where(at_row, ra, xa - mult * ra)
        xb = jnp.where(at_row, rb, xb - mult * rb)
        return xa, xb

    _, xb = lax.fori_loop(0, n, step, (a, ident))
    return xb


def _chol_inv_kernel(g_ref, e_ref):
    count, m, _ = g_ref.shape
    h = 128
    e0 = _eliminate(g_ref[:, :h, :h], h)
    for t in range(count):
        g21 = g_ref[t, h:, :h]
        v = lax.dot_general(g21, e0[t], (((1,), (1,)), ((), ())), precision=HI,
                            preferred_element_type=jnp.float32)
        s = g_ref[t, h:, h:] - lax.dot_general(v, v, (((1,), (1,)), ((), ())), precision=HI,
                                               preferred_element_type=jnp.float32)
        e_ref[t, h:, h:] = s
        e_ref[t, :h, :h] = e0[t]
        e_ref[t, :h, h:] = jnp.zeros((h, m - h), jnp.float32)
        e_ref[t, h:, :h] = jnp.dot(v, e0[t], precision=HI, preferred_element_type=jnp.float32)
    e1 = _eliminate(e_ref[:, h:, h:], m - h)
    for t in range(count):
        e_ref[t, h:, h:] = e1[t]
        e_ref[t, h:, :h] = -jnp.dot(e1[t], e_ref[t, h:, :h], precision=HI,
                                    preferred_element_type=jnp.float32)


def chol_inv(gram):
    return pl.pallas_call(
        _chol_inv_kernel,
        out_shape=jax.ShapeDtypeStruct(gram.shape, jnp.float32),
        in_specs=[pl.BlockSpec(memory_space=pltpu.VMEM)],
        out_specs=pl.BlockSpec(memory_space=pltpu.VMEM),
    )(gram)

COL = ("col_0", "col_1", "col_2")


def cut_along(value, dim, size):
    before, after = (value.shape[:dim], value.shape[dim + 1 :])
    return jnp.moveaxis(value.reshape(*before, size, -1, *after), dim, 0)


def laid_out(tiles, dim):
    tiles = jnp.moveaxis(tiles, 0, dim)
    lengths = tiles.shape
    return tiles.reshape(*lengths[:dim], lengths[dim] * lengths[dim + 1], *lengths[dim + 2 :])


def turned_blocks(tiles, axes, turns):
    inside = tiles.shape[1:]
    result = tiles.reshape(*(lax.axis_size(a) for a in axes), *inside)
    for k in turns:
        result = lax.all_to_all(result, axes[k], k, k, tiled=True)
    return result.reshape(-1, *inside)


def exchange_by_chip(value, groups, turns, split_dim, concat_dim):
    size = lax.axis_size(groups[0]) * lax.axis_size(groups[1])
    tiles = cut_along(value, split_dim, size)
    return laid_out(turned_blocks(tiles, groups, turns), concat_dim)


def piece_ends(length, count):
    unit = 8 if length >= 8 * count else 1
    return [length // unit * k // count * unit for k in range(1, count)]


def cut_exchange(value, axis, pieces, split_dim, concat_dim):
    tiles = cut_along(value, split_dim, lax.axis_size(axis))
    cut = max(range(1, max(2, tiles.ndim - 1)), key=lambda d: tiles.shape[d])
    gathered = []
    for share in jnp.split(tiles, piece_ends(tiles.shape[cut], pieces), axis=cut):
        if share.size:
            gathered.append(lax.all_to_all(share, axis, split_axis=0, concat_axis=0, tiled=True))
    return laid_out(jnp.concatenate(gathered, axis=cut), concat_dim)


def compress_batch(panel_tiles, tile_ranks, sketch_cols):
    keep_cols = jnp.arange(sketch_cols.shape[1])[None, :] < tile_ranks[:, None]
    masked = jnp.where(keep_cols[:, None, :], sketch_cols[None], jnp.zeros_like(sketch_cols)[None])
    sketched = jnp.einsum("bij,bjk->bik", panel_tiles, masked, preferred_element_type=jnp.float32)
    padding = jnp.where(keep_cols, 0.0, 1.0).astype(jnp.float32)
    gram = jnp.einsum("bij,bik->bjk", sketched, sketched, precision=HI)
    gram = gram + padding[:, :, None] * jnp.eye(gram.shape[1], dtype=jnp.float32)[None]
    gram = (gram + jnp.swapaxes(gram, 1, 2)) * 0.5
    inverse = chol_inv(gram)
    basis = jnp.einsum(
        "bij,bkj->bik", sketched, inverse, precision=HI, preferred_element_type=jnp.float32
    ).astype(jnp.bfloat16)
    coeffs = jnp.einsum(
        "bij,bik->bjk", panel_tiles, basis, preferred_element_type=jnp.float32
    ).astype(jnp.bfloat16)
    return jnp.concatenate([basis, coeffs], axis=2)


def slot_numbers(helpers):
    total = helpers.shape[0]
    same_helper = helpers[:, None] == helpers[None, :]
    earlier = jnp.arange(total)[None, :] < jnp.arange(total)[:, None]
    return jnp.sum(jnp.logical_and(same_helper, earlier).astype(jnp.int32), axis=1)


def pack_slabs(slabs, helpers, slots, owners, capacity):
    target = slots * owners + helpers
    table = (jnp.arange(capacity * owners)[:, None] == target[None, :]).astype(jnp.bfloat16)
    packed = jnp.einsum("sk,kab->sab", table, slabs, preferred_element_type=jnp.float32).astype(
        jnp.bfloat16
    )
    return packed.reshape(capacity, owners * slabs.shape[1], slabs.shape[2])


def slot_ranks(ranks, helpers, slots, myself, capacity):
    chosen = jnp.logical_and(
        helpers[None, :] == myself, slots[None, :] == jnp.arange(capacity)[:, None]
    )
    return jnp.sum(jnp.where(chosen, ranks[None, :], 0), axis=1)


def pick_mine(returned, helpers, slots, capacity):
    target = helpers * capacity + slots
    table = (target[:, None] == jnp.arange(returned.shape[0])[None, :]).astype(jnp.bfloat16)
    return jnp.einsum("kn,nab->kab", table, returned, preferred_element_type=jnp.float32).astype(
        jnp.bfloat16
    )


def local(trailing, raw_l, raw_u, sketch, helper_l, helper_u, ranks_l, ranks_u):
    depth = raw_l.shape[1]
    width_r = sketch.shape[3]
    own_sketch = sketch[0, 0]
    compress_all = compress_batch
    col_count = lax.axis_size(COL)
    row_count = lax.axis_size("row")
    cap_row = 2 * depth // col_count
    cap_col = 2 * depth // row_count
    helpers_row = helper_l[0]
    slots_row = slot_numbers(helpers_row)
    sent_row = pack_slabs(raw_l[0], helpers_row, slots_row, col_count, cap_row)
    tiles_row = exchange_by_chip(sent_row, (("col_0", "col_1"), "col_2"), (1, 0), 1, 1)
    made_row = compress_all(
        tiles_row,
        slot_ranks(ranks_l[0], helpers_row, slots_row, lax.axis_index(COL), cap_row),
        own_sketch,
    )
    helpers_col = helper_u[:, 0]
    slots_col = slot_numbers(helpers_col)
    sent_col = pack_slabs(raw_u[:, 0], helpers_col, slots_col, row_count, cap_col)
    tiles_col = cut_exchange(sent_col, "row", 2, 1, 1)
    made_col = compress_all(
        tiles_col,
        slot_ranks(ranks_u[:, 0], helpers_col, slots_col, lax.axis_index("row"), cap_col),
        own_sketch,
    )
    back_row = lax.all_to_all(made_row, COL, split_axis=1, concat_axis=0, tiled=True)
    full_row = lax.all_gather(
        pick_mine(back_row, helpers_row, slots_row, cap_row), COL, axis=1, tiled=True
    )
    back_col = cut_exchange(made_col, "row", 2, 1, 0)
    full_col = lax.all_gather(
        pick_mine(back_col, helpers_col, slots_col, cap_col), "row", axis=1, tiled=True
    )
    basis_row = full_row[:, :, :width_r]
    coeff_row = full_row[:, :, width_r:]
    basis_col = full_col[:, :, :width_r]
    coeff_col = full_col[:, :, width_r:]
    middle = jnp.einsum(
        "kbr,kbs->krs", coeff_row, basis_col, preferred_element_type=jnp.float32
    ).astype(jnp.bfloat16)
    left = jnp.einsum("kbr,krs->kbs", basis_row, middle, preferred_element_type=jnp.float32).astype(
        jnp.bfloat16
    )
    update = jnp.einsum("kbs,kcs->bc", left, coeff_col, preferred_element_type=jnp.float32)
    return trailing.astype(jnp.float32) - update


def solution(mesh):
    torus = Mesh(
        mesh.devices.reshape(mesh.shape["row"], 2, 4, 2), ("row", "col_0", "col_1", "col_2")
    )
    in_specs = (
        P("row", COL),
        P("row", None, COL, None),
        P(None, COL, "row", None),
        P("row", COL, None, None),
        P("row", None),
        P(None, COL),
        P("row", None),
        P(None, COL),
    )
    out_specs = P("row", COL)
    return jax.shard_map(local, mesh=torus, in_specs=in_specs, out_specs=out_specs, check_vma=False)
```

```python
import jax
import jax.numpy as jnp
from jax import lax
from jax.sharding import Mesh
from jax.sharding import PartitionSpec as P
from jax.experimental import pallas as pl
from jax.experimental.pallas import tpu as pltpu

HI = lax.Precision.HIGHEST


def _eliminate(a, n):
    rows = lax.broadcasted_iota(jnp.int32, (1, n, 1), 1)
    cols = lax.broadcasted_iota(jnp.int32, (1, 1, n), 2)
    ident = jnp.broadcast_to((rows == cols).astype(jnp.float32), a.shape)

    def step(j, carry):
        xa, xb = carry
        at_row = rows == j
        at_col = cols == j
        row_a = jnp.sum(jnp.where(at_row, xa, 0.0), axis=1, keepdims=True)
        row_b = jnp.sum(jnp.where(at_row, xb, 0.0), axis=1, keepdims=True)
        col = jnp.sum(jnp.where(at_col, xa, 0.0), axis=2, keepdims=True)
        pivot = jnp.sum(jnp.where(at_col, row_a, 0.0), axis=2, keepdims=True)
        scale = 1.0 / jnp.sqrt(pivot)
        ra = row_a * scale
        rb = row_b * scale
        mult = jnp.where(rows > j, col * scale, 0.0)
        xa = jnp.where(at_row, ra, xa - mult * ra)
        xb = jnp.where(at_row, rb, xb - mult * rb)
        return xa, xb

    _, xb = lax.fori_loop(0, n, step, (a, ident))
    return xb


def _chol_inv_kernel(g_ref, e_ref):
    count, m, _ = g_ref.shape
    h = 128
    e0 = _eliminate(g_ref[:, :h, :h], h)
    for t in range(count):
        g21 = g_ref[t, h:, :h]
        v = lax.dot_general(g21, e0[t], (((1,), (1,)), ((), ())), precision=HI,
                            preferred_element_type=jnp.float32)
        s = g_ref[t, h:, h:] - lax.dot_general(v, v, (((1,), (1,)), ((), ())), precision=HI,
                                               preferred_element_type=jnp.float32)
        e_ref[t, h:, h:] = s
        e_ref[t, :h, :h] = e0[t]
        e_ref[t, :h, h:] = jnp.zeros((h, m - h), jnp.float32)
        e_ref[t, h:, :h] = jnp.dot(v, e0[t], precision=HI, preferred_element_type=jnp.float32)
    e1 = _eliminate(e_ref[:, h:, h:], m - h)
    for t in range(count):
        e_ref[t, h:, h:] = e1[t]
        e_ref[t, h:, :h] = -jnp.dot(e1[t], e_ref[t, h:, :h], precision=HI,
                                    preferred_element_type=jnp.float32)


def chol_inv(gram):
    return pl.pallas_call(
        _chol_inv_kernel,
        out_shape=jax.ShapeDtypeStruct(gram.shape, jnp.float32),
        in_specs=[pl.BlockSpec(memory_space=pltpu.VMEM)],
        out_specs=pl.BlockSpec(memory_space=pltpu.VMEM),
    )(gram)


MESH_ID = pl.DeviceIdType.MESH


def _exchange_kernel(sl_ref, su_ref, ol_ref, ou_ref, sem_l, sem_u, sem_own):
    n_row = lax.axis_size("row")
    n1 = lax.axis_size("col_1")
    n2 = lax.axis_size("col_2")
    n_col = lax.axis_size("col_0") * n1 * n2
    rl = ol_ref.shape[2]
    ru = ou_ref.shape[2]
    me_r = lax.axis_index("row")
    c0 = lax.axis_index("col_0")
    c1 = lax.axis_index("col_1")
    c2 = lax.axis_index("col_2")
    me_c = (c0 * n1 + c1) * n2 + c2

    def col_dev(d):
        return (me_r, d // (n1 * n2), (d // n2) % n1, d % n2)

    def row_dev(o):
        return (o, c0, c1, c2)

    barrier = pltpu.get_barrier_semaphore()
    for step in range(1, n_col):
        pl.semaphore_signal(barrier, 1, device_id=col_dev(lax.rem(me_c + step, n_col)),
                            device_id_type=MESH_ID)
    for step in range(1, n_row):
        pl.semaphore_signal(barrier, 1, device_id=row_dev(lax.rem(me_r + step, n_row)),
                            device_id_type=MESH_ID)
    pl.semaphore_wait(barrier, n_col - 1 + n_row - 1)
    copies = []
    for step in range(1, n_row):
        o = lax.rem(me_r + step, n_row)
        copies.append(pltpu.make_async_remote_copy(
            src_ref=su_ref.at[:, pl.ds(o * ru, ru)], dst_ref=ou_ref.at[:, me_r],
            send_sem=sem_u.at[0, step], recv_sem=sem_u.at[1, step],
            device_id=row_dev(o), device_id_type=MESH_ID))
    for step in range(1, n_col):
        d = lax.rem(me_c + step, n_col)
        copies.append(pltpu.make_async_remote_copy(
            src_ref=sl_ref.at[:, pl.ds(d * rl, rl)], dst_ref=ol_ref.at[:, me_c],
            send_sem=sem_l.at[0, step], recv_sem=sem_l.at[1, step],
            device_id=col_dev(d), device_id_type=MESH_ID))
    for cp in copies:
        cp.start()
    own = [
        pltpu.make_async_copy(su_ref.at[:, pl.ds(me_r * ru, ru)], ou_ref.at[:, me_r], sem_own.at[0]),
        pltpu.make_async_copy(sl_ref.at[:, pl.ds(me_c * rl, rl)], ol_ref.at[:, me_c], sem_own.at[1]),
    ]
    for cp in own:
        cp.start()
    for cp in own:
        cp.wait()
    for cp in copies:
        cp.wait()


def exchange_tiles(sent_l, sent_u, n_col, n_row):
    cap_l, rows_l, width = sent_l.shape
    cap_u, rows_u, _ = sent_u.shape
    rl = rows_l // n_col
    ru = rows_u // n_row
    out_l, out_u = pl.pallas_call(
        _exchange_kernel,
        out_shape=(
            jax.ShapeDtypeStruct((cap_l, n_col, rl, width), sent_l.dtype),
            jax.ShapeDtypeStruct((cap_u, n_row, ru, width), sent_u.dtype),
        ),
        in_specs=[pl.BlockSpec(memory_space=pl.ANY)] * 2,
        out_specs=(pl.BlockSpec(memory_space=pl.ANY), pl.BlockSpec(memory_space=pl.ANY)),
        scratch_shapes=[
            pltpu.SemaphoreType.DMA((2, n_col)),
            pltpu.SemaphoreType.DMA((2, n_row)),
            pltpu.SemaphoreType.DMA((2,)),
        ],
        compiler_params=pltpu.CompilerParams(collective_id=0, has_side_effects=True),
    )(sent_l, sent_u)
    return out_l.reshape(cap_l, n_col * rl, width), out_u.reshape(cap_u, n_row * ru, width)


COL = ("col_0", "col_1", "col_2")


def cut_along(value, dim, size):
    before, after = (value.shape[:dim], value.shape[dim + 1 :])
    return jnp.moveaxis(value.reshape(*before, size, -1, *after), dim, 0)


def laid_out(tiles, dim):
    tiles = jnp.moveaxis(tiles, 0, dim)
    lengths = tiles.shape
    return tiles.reshape(*lengths[:dim], lengths[dim] * lengths[dim + 1], *lengths[dim + 2 :])


def turned_blocks(tiles, axes, turns):
    inside = tiles.shape[1:]
    result = tiles.reshape(*(lax.axis_size(a) for a in axes), *inside)
    for k in turns:
        result = lax.all_to_all(result, axes[k], k, k, tiled=True)
    return result.reshape(-1, *inside)


def exchange_by_chip(value, groups, turns, split_dim, concat_dim):
    size = lax.axis_size(groups[0]) * lax.axis_size(groups[1])
    tiles = cut_along(value, split_dim, size)
    return laid_out(turned_blocks(tiles, groups, turns), concat_dim)


def piece_ends(length, count):
    unit = 8 if length >= 8 * count else 1
    return [length // unit * k // count * unit for k in range(1, count)]


def cut_exchange(value, axis, pieces, split_dim, concat_dim):
    tiles = cut_along(value, split_dim, lax.axis_size(axis))
    cut = max(range(1, max(2, tiles.ndim - 1)), key=lambda d: tiles.shape[d])
    gathered = []
    for share in jnp.split(tiles, piece_ends(tiles.shape[cut], pieces), axis=cut):
        if share.size:
            gathered.append(lax.all_to_all(share, axis, split_axis=0, concat_axis=0, tiled=True))
    return laid_out(jnp.concatenate(gathered, axis=cut), concat_dim)


def sketch_gram(panel_tiles, tile_ranks, sketch_cols):
    keep_cols = jnp.arange(sketch_cols.shape[1])[None, :] < tile_ranks[:, None]
    masked = jnp.where(keep_cols[:, None, :], sketch_cols[None], jnp.zeros_like(sketch_cols)[None])
    sketched = jnp.einsum("bij,bjk->bik", panel_tiles, masked, preferred_element_type=jnp.float32)
    padding = jnp.where(keep_cols, 0.0, 1.0).astype(jnp.float32)
    gram = jnp.einsum("bij,bik->bjk", sketched, sketched, precision=HI)
    gram = gram + padding[:, :, None] * jnp.eye(gram.shape[1], dtype=jnp.float32)[None]
    return sketched, (gram + jnp.swapaxes(gram, 1, 2)) * 0.5


def finish_batch(panel_tiles, sketched, inverse):
    basis = jnp.einsum(
        "bij,bkj->bik", sketched, inverse, precision=HI, preferred_element_type=jnp.float32
    ).astype(jnp.bfloat16)
    coeffs = jnp.einsum(
        "bij,bik->bjk", panel_tiles, basis, preferred_element_type=jnp.float32
    ).astype(jnp.bfloat16)
    return jnp.concatenate([basis, coeffs], axis=2)


def slot_numbers(helpers):
    total = helpers.shape[0]
    same_helper = helpers[:, None] == helpers[None, :]
    earlier = jnp.arange(total)[None, :] < jnp.arange(total)[:, None]
    return jnp.sum(jnp.logical_and(same_helper, earlier).astype(jnp.int32), axis=1)


def pack_slabs(slabs, helpers, slots, owners, capacity):
    target = slots * owners + helpers
    table = (jnp.arange(capacity * owners)[:, None] == target[None, :]).astype(jnp.bfloat16)
    packed = jnp.einsum("sk,kab->sab", table, slabs, preferred_element_type=jnp.float32).astype(
        jnp.bfloat16
    )
    return packed.reshape(capacity, owners * slabs.shape[1], slabs.shape[2])


def slot_ranks(ranks, helpers, slots, myself, capacity):
    chosen = jnp.logical_and(
        helpers[None, :] == myself, slots[None, :] == jnp.arange(capacity)[:, None]
    )
    return jnp.sum(jnp.where(chosen, ranks[None, :], 0), axis=1)


def pick_mine(returned, helpers, slots, capacity):
    target = helpers * capacity + slots
    table = (target[:, None] == jnp.arange(returned.shape[0])[None, :]).astype(jnp.bfloat16)
    return jnp.einsum("kn,nab->kab", table, returned, preferred_element_type=jnp.float32).astype(
        jnp.bfloat16
    )


def local(trailing, raw_l, raw_u, sketch, helper_l, helper_u, ranks_l, ranks_u):
    depth = raw_l.shape[1]
    width_r = sketch.shape[3]
    own_sketch = sketch[0, 0]
    col_count = lax.axis_size(COL)
    row_count = lax.axis_size("row")
    cap_row = 2 * depth // col_count
    cap_col = 2 * depth // row_count
    helpers_row = helper_l[0]
    slots_row = slot_numbers(helpers_row)
    sent_row = pack_slabs(raw_l[0], helpers_row, slots_row, col_count, cap_row)
    helpers_col = helper_u[:, 0]
    slots_col = slot_numbers(helpers_col)
    sent_col = pack_slabs(raw_u[:, 0], helpers_col, slots_col, row_count, cap_col)
    tiles_row, tiles_col = exchange_tiles(sent_row, sent_col, col_count, row_count)
    sketched_row, gram_row = sketch_gram(
        tiles_row,
        slot_ranks(ranks_l[0], helpers_row, slots_row, lax.axis_index(COL), cap_row),
        own_sketch,
    )
    sketched_col, gram_col = sketch_gram(
        tiles_col,
        slot_ranks(ranks_u[:, 0], helpers_col, slots_col, lax.axis_index("row"), cap_col),
        own_sketch,
    )
    inverse = chol_inv(jnp.concatenate([gram_row, gram_col], axis=0))
    made_row = finish_batch(tiles_row, sketched_row, inverse[:cap_row])
    made_col = finish_batch(tiles_col, sketched_col, inverse[cap_row:])
    back_row = lax.all_to_all(made_row, COL, split_axis=1, concat_axis=0, tiled=True)
    full_row = lax.all_gather(
        pick_mine(back_row, helpers_row, slots_row, cap_row), COL, axis=1, tiled=True
    )
    back_col = cut_exchange(made_col, "row", 2, 1, 0)
    full_col = lax.all_gather(
        pick_mine(back_col, helpers_col, slots_col, cap_col), "row", axis=1, tiled=True
    )
    basis_row = full_row[:, :, :width_r]
    coeff_row = full_row[:, :, width_r:]
    basis_col = full_col[:, :, :width_r]
    coeff_col = full_col[:, :, width_r:]
    middle = jnp.einsum(
        "kbr,kbs->krs", coeff_row, basis_col, preferred_element_type=jnp.float32
    ).astype(jnp.bfloat16)
    left = jnp.einsum("kbr,krs->kbs", basis_row, middle, preferred_element_type=jnp.float32).astype(
        jnp.bfloat16
    )
    update = jnp.einsum("kbs,kcs->bc", left, coeff_col, preferred_element_type=jnp.float32)
    return trailing.astype(jnp.float32) - update


def solution(mesh):
    torus = Mesh(
        mesh.devices.reshape(mesh.shape["row"], 2, 4, 2), ("row", "col_0", "col_1", "col_2")
    )
    in_specs = (
        P("row", COL),
        P("row", None, COL, None),
        P(None, COL, "row", None),
        P("row", COL, None, None),
        P("row", None),
        P(None, COL),
        P("row", None),
        P(None, COL),
    )
    out_specs = P("row", COL)
    return jax.shard_map(local, mesh=torus, in_specs=in_specs, out_specs=out_specs, check_vma=False)
```

```python
import jax
import jax.numpy as jnp
from jax import lax
from jax.sharding import Mesh
from jax.sharding import PartitionSpec as P
from jax.experimental import pallas as pl
from jax.experimental.pallas import tpu as pltpu

HI = lax.Precision.HIGHEST


def _eliminate(a, n):
    rows = lax.broadcasted_iota(jnp.int32, (1, n, 1), 1)
    cols = lax.broadcasted_iota(jnp.int32, (1, 1, n), 2)
    ident = jnp.broadcast_to((rows == cols).astype(jnp.float32), a.shape)

    def step(j, carry):
        xa, xb = carry
        at_row = rows == j
        at_col = cols == j
        row_a = jnp.sum(jnp.where(at_row, xa, 0.0), axis=1, keepdims=True)
        row_b = jnp.sum(jnp.where(at_row, xb, 0.0), axis=1, keepdims=True)
        col = jnp.sum(jnp.where(at_col, xa, 0.0), axis=2, keepdims=True)
        pivot = jnp.sum(jnp.where(at_col, row_a, 0.0), axis=2, keepdims=True)
        scale = 1.0 / jnp.sqrt(pivot)
        ra = row_a * scale
        rb = row_b * scale
        mult = jnp.where(rows > j, col * scale, 0.0)
        xa = jnp.where(at_row, ra, xa - mult * ra)
        xb = jnp.where(at_row, rb, xb - mult * rb)
        return xa, xb

    _, xb = lax.fori_loop(0, n, step, (a, ident))
    return xb


def _chol_inv_kernel(g_ref, e_ref):
    count, m, _ = g_ref.shape
    h = 128
    e0 = _eliminate(g_ref[:, :h, :h], h)
    for t in range(count):
        g21 = g_ref[t, h:, :h]
        v = lax.dot_general(g21, e0[t], (((1,), (1,)), ((), ())), precision=HI,
                            preferred_element_type=jnp.float32)
        s = g_ref[t, h:, h:] - lax.dot_general(v, v, (((1,), (1,)), ((), ())), precision=HI,
                                               preferred_element_type=jnp.float32)
        e_ref[t, h:, h:] = s
        e_ref[t, :h, :h] = e0[t]
        e_ref[t, :h, h:] = jnp.zeros((h, m - h), jnp.float32)
        e_ref[t, h:, :h] = jnp.dot(v, e0[t], precision=HI, preferred_element_type=jnp.float32)
    e1 = _eliminate(e_ref[:, h:, h:], m - h)
    for t in range(count):
        e_ref[t, h:, h:] = e1[t]
        e_ref[t, h:, :h] = -jnp.dot(e1[t], e_ref[t, h:, :h], precision=HI,
                                    preferred_element_type=jnp.float32)


def chol_inv(gram):
    return pl.pallas_call(
        _chol_inv_kernel,
        out_shape=jax.ShapeDtypeStruct(gram.shape, jnp.float32),
        in_specs=[pl.BlockSpec(memory_space=pltpu.VMEM)],
        out_specs=pl.BlockSpec(memory_space=pltpu.VMEM),
    )(gram)

COL = ("col_0", "col_1", "col_2")


def cut_along(value, dim, size):
    before, after = (value.shape[:dim], value.shape[dim + 1 :])
    return jnp.moveaxis(value.reshape(*before, size, -1, *after), dim, 0)


def laid_out(tiles, dim):
    tiles = jnp.moveaxis(tiles, 0, dim)
    lengths = tiles.shape
    return tiles.reshape(*lengths[:dim], lengths[dim] * lengths[dim + 1], *lengths[dim + 2 :])


def turned_blocks(tiles, axes, turns):
    inside = tiles.shape[1:]
    result = tiles.reshape(*(lax.axis_size(a) for a in axes), *inside)
    for k in turns:
        result = lax.all_to_all(result, axes[k], k, k, tiled=True)
    return result.reshape(-1, *inside)


def exchange_by_chip(value, groups, turns, split_dim, concat_dim):
    size = lax.axis_size(groups[0]) * lax.axis_size(groups[1])
    tiles = cut_along(value, split_dim, size)
    return laid_out(turned_blocks(tiles, groups, turns), concat_dim)


def piece_ends(length, count):
    unit = 8 if length >= 8 * count else 1
    return [length // unit * k // count * unit for k in range(1, count)]


def cut_exchange(value, axis, pieces, split_dim, concat_dim):
    tiles = cut_along(value, split_dim, lax.axis_size(axis))
    cut = max(range(1, max(2, tiles.ndim - 1)), key=lambda d: tiles.shape[d])
    gathered = []
    for share in jnp.split(tiles, piece_ends(tiles.shape[cut], pieces), axis=cut):
        if share.size:
            gathered.append(lax.all_to_all(share, axis, split_axis=0, concat_axis=0, tiled=True))
    return laid_out(jnp.concatenate(gathered, axis=cut), concat_dim)


def compress_batch(panel_tiles, tile_ranks, sketch_cols):
    keep_cols = jnp.arange(sketch_cols.shape[1])[None, :] < tile_ranks[:, None]
    masked = jnp.where(keep_cols[:, None, :], sketch_cols[None], jnp.zeros_like(sketch_cols)[None])
    sketched = jnp.einsum("bij,bjk->bik", panel_tiles, masked, preferred_element_type=jnp.float32)
    padding = jnp.where(keep_cols, 0.0, 1.0).astype(jnp.float32)
    gram = jnp.einsum("bij,bik->bjk", sketched, sketched, precision=HI)
    gram = gram + padding[:, :, None] * jnp.eye(gram.shape[1], dtype=jnp.float32)[None]
    gram = (gram + jnp.swapaxes(gram, 1, 2)) * 0.5
    inverse = chol_inv(gram)
    basis = jnp.einsum(
        "bij,bkj->bik", sketched, inverse, precision=HI, preferred_element_type=jnp.float32
    ).astype(jnp.bfloat16)
    coeffs = jnp.einsum(
        "bij,bik->bjk", panel_tiles, basis, preferred_element_type=jnp.float32
    ).astype(jnp.bfloat16)
    return jnp.concatenate([basis, coeffs], axis=2)


def slot_numbers(helpers):
    total = helpers.shape[0]
    same_helper = helpers[:, None] == helpers[None, :]
    earlier = jnp.arange(total)[None, :] < jnp.arange(total)[:, None]
    return jnp.sum(jnp.logical_and(same_helper, earlier).astype(jnp.int32), axis=1)


def pack_slabs(slabs, helpers, slots, owners, capacity):
    target = slots * owners + helpers
    table = (jnp.arange(capacity * owners)[:, None] == target[None, :]).astype(jnp.bfloat16)
    packed = jnp.einsum("sk,kab->sab", table, slabs, preferred_element_type=jnp.float32).astype(
        jnp.bfloat16
    )
    return packed.reshape(capacity, owners * slabs.shape[1], slabs.shape[2])


def slot_ranks(ranks, helpers, slots, myself, capacity):
    chosen = jnp.logical_and(
        helpers[None, :] == myself, slots[None, :] == jnp.arange(capacity)[:, None]
    )
    return jnp.sum(jnp.where(chosen, ranks[None, :], 0), axis=1)


def pick_mine(returned, helpers, slots, capacity):
    target = helpers * capacity + slots
    table = (target[:, None] == jnp.arange(returned.shape[0])[None, :]).astype(jnp.bfloat16)
    return jnp.einsum("kn,nab->kab", table, returned, preferred_element_type=jnp.float32).astype(
        jnp.bfloat16
    )


def local(trailing, raw_l, raw_u, sketch, helper_l, helper_u, ranks_l, ranks_u):
    depth = raw_l.shape[1]
    width_r = sketch.shape[3]
    own_sketch = sketch[0, 0]
    compress_all = compress_batch
    col_count = lax.axis_size(COL)
    row_count = lax.axis_size("row")
    cap_row = 2 * depth // col_count
    cap_col = 2 * depth // row_count
    helpers_row = helper_l[0]
    slots_row = slot_numbers(helpers_row)
    sent_row = pack_slabs(raw_l[0], helpers_row, slots_row, col_count, cap_row)
    tiles_row = exchange_by_chip(sent_row, (("col_0", "col_1"), "col_2"), (1, 0), 1, 1)
    made_row = compress_all(
        tiles_row,
        slot_ranks(ranks_l[0], helpers_row, slots_row, lax.axis_index(COL), cap_row),
        own_sketch,
    )
    back_row = lax.all_to_all(made_row, COL, split_axis=1, concat_axis=0, tiled=True)
    mine_row = pick_mine(back_row, helpers_row, slots_row, cap_row)
    full_row = lax.all_gather(mine_row, COL, axis=1, tiled=True)
    helpers_col = helper_u[:, 0]
    slots_col = slot_numbers(helpers_col)
    panel_col, mine_row = lax.optimization_barrier((raw_u[:, 0], mine_row))
    sent_col = pack_slabs(panel_col, helpers_col, slots_col, row_count, cap_col)
    tiles_col = cut_exchange(sent_col, "row", 2, 1, 1)
    made_col = compress_all(
        tiles_col,
        slot_ranks(ranks_u[:, 0], helpers_col, slots_col, lax.axis_index("row"), cap_col),
        own_sketch,
    )
    back_col = cut_exchange(made_col, "row", 2, 1, 0)
    full_col = lax.all_gather(
        pick_mine(back_col, helpers_col, slots_col, cap_col), "row", axis=1, tiled=True
    )
    basis_row = full_row[:, :, :width_r]
    coeff_row = full_row[:, :, width_r:]
    basis_col = full_col[:, :, :width_r]
    coeff_col = full_col[:, :, width_r:]
    middle = jnp.einsum(
        "kbr,kbs->krs", coeff_row, basis_col, preferred_element_type=jnp.float32
    ).astype(jnp.bfloat16)
    left = jnp.einsum("kbr,krs->kbs", basis_row, middle, preferred_element_type=jnp.float32).astype(
        jnp.bfloat16
    )
    update = jnp.einsum("kbs,kcs->bc", left, coeff_col, preferred_element_type=jnp.float32)
    return trailing.astype(jnp.float32) - update


def solution(mesh):
    torus = Mesh(
        mesh.devices.reshape(mesh.shape["row"], 2, 4, 2), ("row", "col_0", "col_1", "col_2")
    )
    in_specs = (
        P("row", COL),
        P("row", None, COL, None),
        P(None, COL, "row", None),
        P("row", COL, None, None),
        P("row", None),
        P(None, COL),
        P("row", None),
        P(None, COL),
    )
    out_specs = P("row", COL)
    return jax.shard_map(local, mesh=torus, in_specs=in_specs, out_specs=out_specs, check_vma=False)
```

```python
import jax
import jax.numpy as jnp
from jax import lax
from jax.sharding import Mesh
from jax.sharding import PartitionSpec as P
from jax.experimental import pallas as pl
from jax.experimental.pallas import tpu as pltpu

HI = lax.Precision.HIGHEST


def _eliminate(a, n):
    rows = lax.broadcasted_iota(jnp.int32, (1, n, 1), 1)
    cols = lax.broadcasted_iota(jnp.int32, (1, 1, n), 2)
    ident = jnp.broadcast_to((rows == cols).astype(jnp.float32), a.shape)

    def step(j, carry):
        xa, xb = carry
        at_row = rows == j
        at_col = cols == j
        row_a = jnp.sum(jnp.where(at_row, xa, 0.0), axis=1, keepdims=True)
        row_b = jnp.sum(jnp.where(at_row, xb, 0.0), axis=1, keepdims=True)
        col = jnp.sum(jnp.where(at_col, xa, 0.0), axis=2, keepdims=True)
        pivot = jnp.sum(jnp.where(at_col, row_a, 0.0), axis=2, keepdims=True)
        scale = 1.0 / jnp.sqrt(pivot)
        ra = row_a * scale
        rb = row_b * scale
        mult = jnp.where(rows > j, col * scale, 0.0)
        xa = jnp.where(at_row, ra, xa - mult * ra)
        xb = jnp.where(at_row, rb, xb - mult * rb)
        return xa, xb

    _, xb = lax.fori_loop(0, n, step, (a, ident))
    return xb


def _chol_inv_kernel(g_ref, e_ref):
    count, m, _ = g_ref.shape
    h = 128
    e0 = _eliminate(g_ref[:, :h, :h], h)
    for t in range(count):
        g21 = g_ref[t, h:, :h]
        v = lax.dot_general(g21, e0[t], (((1,), (1,)), ((), ())), precision=HI,
                            preferred_element_type=jnp.float32)
        s = g_ref[t, h:, h:] - lax.dot_general(v, v, (((1,), (1,)), ((), ())), precision=HI,
                                               preferred_element_type=jnp.float32)
        e_ref[t, h:, h:] = s
        e_ref[t, :h, :h] = e0[t]
        e_ref[t, :h, h:] = jnp.zeros((h, m - h), jnp.float32)
        e_ref[t, h:, :h] = jnp.dot(v, e0[t], precision=HI, preferred_element_type=jnp.float32)
    e1 = _eliminate(e_ref[:, h:, h:], m - h)
    for t in range(count):
        e_ref[t, h:, h:] = e1[t]
        e_ref[t, h:, :h] = -jnp.dot(e1[t], e_ref[t, h:, :h], precision=HI,
                                    preferred_element_type=jnp.float32)


def chol_inv(gram):
    return pl.pallas_call(
        _chol_inv_kernel,
        out_shape=jax.ShapeDtypeStruct(gram.shape, jnp.float32),
        in_specs=[pl.BlockSpec(memory_space=pltpu.VMEM)],
        out_specs=pl.BlockSpec(memory_space=pltpu.VMEM),
    )(gram)


def _update_kernel(row_ref, col_ref, t_ref, o_ref):
    k = pl.program_id(0)
    width = row_ref.shape[2] // 2
    x = row_ref[0]
    y = col_ref[0]
    middle = lax.dot_general(x[:, width:], y[:, :width], (((0,), (0,)), ((), ())),
                             preferred_element_type=jnp.float32).astype(jnp.bfloat16)
    left = jnp.dot(x[:, :width], middle, preferred_element_type=jnp.float32).astype(jnp.bfloat16)
    term = lax.dot_general(left, y[:, width:], (((1,), (1,)), ((), ())),
                           preferred_element_type=jnp.float32)

    @pl.when(k == 0)
    def _():
        o_ref[...] = t_ref[...].astype(jnp.float32) - term

    @pl.when(k > 0)
    def _():
        o_ref[...] -= term


def trailing_update(full_row, full_col, trailing):
    depth, rows, both = full_row.shape
    cols = full_col.shape[1]
    return pl.pallas_call(
        _update_kernel,
        out_shape=jax.ShapeDtypeStruct((rows, cols), jnp.float32),
        grid=(depth,),
        in_specs=[
            pl.BlockSpec((1, rows, both), lambda k: (k, 0, 0)),
            pl.BlockSpec((1, cols, both), lambda k: (k, 0, 0)),
            pl.BlockSpec((rows, cols), lambda k: (0, 0)),
        ],
        out_specs=pl.BlockSpec((rows, cols), lambda k: (0, 0)),
        compiler_params=pltpu.CompilerParams(
            dimension_semantics=("arbitrary",), vmem_limit_bytes=48 * 1024 * 1024
        ),
    )(full_row, full_col, trailing)


COL = ("col_0", "col_1", "col_2")


def cut_along(value, dim, size):
    before, after = (value.shape[:dim], value.shape[dim + 1 :])
    return jnp.moveaxis(value.reshape(*before, size, -1, *after), dim, 0)


def laid_out(tiles, dim):
    tiles = jnp.moveaxis(tiles, 0, dim)
    lengths = tiles.shape
    return tiles.reshape(*lengths[:dim], lengths[dim] * lengths[dim + 1], *lengths[dim + 2 :])


def turned_blocks(tiles, axes, turns):
    inside = tiles.shape[1:]
    result = tiles.reshape(*(lax.axis_size(a) for a in axes), *inside)
    for k in turns:
        result = lax.all_to_all(result, axes[k], k, k, tiled=True)
    return result.reshape(-1, *inside)


def exchange_by_chip(value, groups, turns, split_dim, concat_dim):
    size = lax.axis_size(groups[0]) * lax.axis_size(groups[1])
    tiles = cut_along(value, split_dim, size)
    return laid_out(turned_blocks(tiles, groups, turns), concat_dim)


def piece_ends(length, count):
    unit = 8 if length >= 8 * count else 1
    return [length // unit * k // count * unit for k in range(1, count)]


def cut_exchange(value, axis, pieces, split_dim, concat_dim):
    tiles = cut_along(value, split_dim, lax.axis_size(axis))
    cut = max(range(1, max(2, tiles.ndim - 1)), key=lambda d: tiles.shape[d])
    gathered = []
    for share in jnp.split(tiles, piece_ends(tiles.shape[cut], pieces), axis=cut):
        if share.size:
            gathered.append(lax.all_to_all(share, axis, split_axis=0, concat_axis=0, tiled=True))
    return laid_out(jnp.concatenate(gathered, axis=cut), concat_dim)


def compress_batch(panel_tiles, tile_ranks, sketch_cols):
    keep_cols = jnp.arange(sketch_cols.shape[1])[None, :] < tile_ranks[:, None]
    masked = jnp.where(keep_cols[:, None, :], sketch_cols[None], jnp.zeros_like(sketch_cols)[None])
    sketched = jnp.einsum("bij,bjk->bik", panel_tiles, masked, preferred_element_type=jnp.float32)
    padding = jnp.where(keep_cols, 0.0, 1.0).astype(jnp.float32)
    gram = jnp.einsum("bij,bik->bjk", sketched, sketched, precision=HI)
    gram = gram + padding[:, :, None] * jnp.eye(gram.shape[1], dtype=jnp.float32)[None]
    gram = (gram + jnp.swapaxes(gram, 1, 2)) * 0.5
    inverse = chol_inv(gram)
    basis = jnp.einsum(
        "bij,bkj->bik", sketched, inverse, precision=HI, preferred_element_type=jnp.float32
    ).astype(jnp.bfloat16)
    coeffs = jnp.einsum(
        "bij,bik->bjk", panel_tiles, basis, preferred_element_type=jnp.float32
    ).astype(jnp.bfloat16)
    return jnp.concatenate([basis, coeffs], axis=2)


def slot_numbers(helpers):
    total = helpers.shape[0]
    same_helper = helpers[:, None] == helpers[None, :]
    earlier = jnp.arange(total)[None, :] < jnp.arange(total)[:, None]
    return jnp.sum(jnp.logical_and(same_helper, earlier).astype(jnp.int32), axis=1)


def pack_slabs(slabs, helpers, slots, owners, capacity):
    target = slots * owners + helpers
    table = (jnp.arange(capacity * owners)[:, None] == target[None, :]).astype(jnp.bfloat16)
    packed = jnp.einsum("sk,kab->sab", table, slabs, preferred_element_type=jnp.float32).astype(
        jnp.bfloat16
    )
    return packed.reshape(capacity, owners * slabs.shape[1], slabs.shape[2])


def slot_ranks(ranks, helpers, slots, myself, capacity):
    chosen = jnp.logical_and(
        helpers[None, :] == myself, slots[None, :] == jnp.arange(capacity)[:, None]
    )
    return jnp.sum(jnp.where(chosen, ranks[None, :], 0), axis=1)


def pick_mine(returned, helpers, slots, capacity):
    target = helpers * capacity + slots
    table = (target[:, None] == jnp.arange(returned.shape[0])[None, :]).astype(jnp.bfloat16)
    return jnp.einsum("kn,nab->kab", table, returned, preferred_element_type=jnp.float32).astype(
        jnp.bfloat16
    )


def local(trailing, raw_l, raw_u, sketch, helper_l, helper_u, ranks_l, ranks_u):
    depth = raw_l.shape[1]
    width_r = sketch.shape[3]
    own_sketch = sketch[0, 0]
    compress_all = compress_batch
    col_count = lax.axis_size(COL)
    row_count = lax.axis_size("row")
    cap_row = 2 * depth // col_count
    cap_col = 2 * depth // row_count
    helpers_row = helper_l[0]
    slots_row = slot_numbers(helpers_row)
    sent_row = pack_slabs(raw_l[0], helpers_row, slots_row, col_count, cap_row)
    tiles_row = exchange_by_chip(sent_row, (("col_0", "col_1"), "col_2"), (1, 0), 1, 1)
    made_row = compress_all(
        tiles_row,
        slot_ranks(ranks_l[0], helpers_row, slots_row, lax.axis_index(COL), cap_row),
        own_sketch,
    )
    helpers_col = helper_u[:, 0]
    slots_col = slot_numbers(helpers_col)
    sent_col = pack_slabs(raw_u[:, 0], helpers_col, slots_col, row_count, cap_col)
    tiles_col = cut_exchange(sent_col, "row", 2, 1, 1)
    made_col = compress_all(
        tiles_col,
        slot_ranks(ranks_u[:, 0], helpers_col, slots_col, lax.axis_index("row"), cap_col),
        own_sketch,
    )
    back_row = lax.all_to_all(made_row, COL, split_axis=1, concat_axis=0, tiled=True)
    full_row = lax.all_gather(
        pick_mine(back_row, helpers_row, slots_row, cap_row), COL, axis=1, tiled=True
    )
    back_col = cut_exchange(made_col, "row", 2, 1, 0)
    full_col = lax.all_gather(
        pick_mine(back_col, helpers_col, slots_col, cap_col), "row", axis=1, tiled=True
    )
    return trailing_update(full_row, full_col, trailing)


def solution(mesh):
    torus = Mesh(
        mesh.devices.reshape(mesh.shape["row"], 2, 4, 2), ("row", "col_0", "col_1", "col_2")
    )
    in_specs = (
        P("row", COL),
        P("row", None, COL, None),
        P(None, COL, "row", None),
        P("row", COL, None, None),
        P("row", None),
        P(None, COL),
        P("row", None),
        P(None, COL),
    )
    out_specs = P("row", COL)
    return jax.shard_map(local, mesh=torus, in_specs=in_specs, out_specs=out_specs, check_vma=False)
```

```python
import jax
import jax.numpy as jnp
from jax import lax
from jax.sharding import Mesh
from jax.sharding import PartitionSpec as P
from jax.experimental import pallas as pl
from jax.experimental.pallas import tpu as pltpu

HI = lax.Precision.HIGHEST


def _eliminate(a, n):
    rows = lax.broadcasted_iota(jnp.int32, (1, n, 1), 1)
    cols = lax.broadcasted_iota(jnp.int32, (1, 1, n), 2)
    ident = jnp.broadcast_to((rows == cols).astype(jnp.float32), a.shape)

    def step(j, carry):
        xa, xb = carry
        at_row = rows == j
        at_col = cols == j
        row_a = jnp.sum(jnp.where(at_row, xa, 0.0), axis=1, keepdims=True)
        row_b = jnp.sum(jnp.where(at_row, xb, 0.0), axis=1, keepdims=True)
        col = jnp.sum(jnp.where(at_col, xa, 0.0), axis=2, keepdims=True)
        pivot = jnp.sum(jnp.where(at_col, row_a, 0.0), axis=2, keepdims=True)
        scale = 1.0 / jnp.sqrt(pivot)
        ra = row_a * scale
        rb = row_b * scale
        mult = jnp.where(rows > j, col * scale, 0.0)
        xa = jnp.where(at_row, ra, xa - mult * ra)
        xb = jnp.where(at_row, rb, xb - mult * rb)
        return xa, xb

    _, xb = lax.fori_loop(0, n, step, (a, ident), unroll=4)
    return xb


def _chol_inv_kernel(g_ref, e_ref):
    count, m, _ = g_ref.shape
    h = 128
    e0 = _eliminate(g_ref[:, :h, :h], h)
    for t in range(count):
        g21 = g_ref[t, h:, :h]
        v = lax.dot_general(g21, e0[t], (((1,), (1,)), ((), ())), precision=HI,
                            preferred_element_type=jnp.float32)
        s = g_ref[t, h:, h:] - lax.dot_general(v, v, (((1,), (1,)), ((), ())), precision=HI,
                                               preferred_element_type=jnp.float32)
        e_ref[t, h:, h:] = s
        e_ref[t, :h, :h] = e0[t]
        e_ref[t, :h, h:] = jnp.zeros((h, m - h), jnp.float32)
        e_ref[t, h:, :h] = jnp.dot(v, e0[t], precision=HI, preferred_element_type=jnp.float32)
    e1 = _eliminate(e_ref[:, h:, h:], m - h)
    for t in range(count):
        e_ref[t, h:, h:] = e1[t]
        e_ref[t, h:, :h] = -jnp.dot(e1[t], e_ref[t, h:, :h], precision=HI,
                                    preferred_element_type=jnp.float32)


def chol_inv(gram):
    return pl.pallas_call(
        _chol_inv_kernel,
        out_shape=jax.ShapeDtypeStruct(gram.shape, jnp.float32),
        in_specs=[pl.BlockSpec(memory_space=pltpu.VMEM)],
        out_specs=pl.BlockSpec(memory_space=pltpu.VMEM),
    )(gram)


def _update_kernel(row_ref, col_ref, t_ref, o_ref):
    k = pl.program_id(0)
    width = row_ref.shape[2] // 2
    term = None
    for part in range(row_ref.shape[0]):
        x = row_ref[part]
        y = col_ref[part]
        middle = lax.dot_general(x[:, width:], y[:, :width], (((0,), (0,)), ((), ())),
                                 preferred_element_type=jnp.float32).astype(jnp.bfloat16)
        left = jnp.dot(x[:, :width], middle, preferred_element_type=jnp.float32).astype(jnp.bfloat16)
        piece = lax.dot_general(left, y[:, width:], (((1,), (1,)), ((), ())),
                                preferred_element_type=jnp.float32)
        term = piece if term is None else term + piece

    @pl.when(k == 0)
    def _():
        o_ref[...] = t_ref[...].astype(jnp.float32) - term

    @pl.when(k > 0)
    def _():
        o_ref[...] -= term


def trailing_update(full_row, full_col, trailing):
    depth, rows, both = full_row.shape
    cols = full_col.shape[1]
    return pl.pallas_call(
        _update_kernel,
        out_shape=jax.ShapeDtypeStruct((rows, cols), jnp.float32),
        grid=(depth // 2,),
        in_specs=[
            pl.BlockSpec((2, rows, both), lambda k: (k, 0, 0)),
            pl.BlockSpec((2, cols, both), lambda k: (k, 0, 0)),
            pl.BlockSpec((rows, cols), lambda k: (0, 0)),
        ],
        out_specs=pl.BlockSpec((rows, cols), lambda k: (0, 0)),
        compiler_params=pltpu.CompilerParams(
            dimension_semantics=("arbitrary",), vmem_limit_bytes=48 * 1024 * 1024
        ),
    )(full_row, full_col, trailing)


COL = ("col_0", "col_1", "col_2")


def cut_along(value, dim, size):
    before, after = (value.shape[:dim], value.shape[dim + 1 :])
    return jnp.moveaxis(value.reshape(*before, size, -1, *after), dim, 0)


def laid_out(tiles, dim):
    tiles = jnp.moveaxis(tiles, 0, dim)
    lengths = tiles.shape
    return tiles.reshape(*lengths[:dim], lengths[dim] * lengths[dim + 1], *lengths[dim + 2 :])


def turned_blocks(tiles, axes, turns):
    inside = tiles.shape[1:]
    result = tiles.reshape(*(lax.axis_size(a) for a in axes), *inside)
    for k in turns:
        result = lax.all_to_all(result, axes[k], k, k, tiled=True)
    return result.reshape(-1, *inside)


def exchange_by_chip(value, groups, turns, split_dim, concat_dim):
    size = lax.axis_size(groups[0]) * lax.axis_size(groups[1])
    tiles = cut_along(value, split_dim, size)
    return laid_out(turned_blocks(tiles, groups, turns), concat_dim)


def piece_ends(length, count):
    unit = 8 if length >= 8 * count else 1
    return [length // unit * k // count * unit for k in range(1, count)]


def cut_exchange(value, axis, pieces, split_dim, concat_dim):
    tiles = cut_along(value, split_dim, lax.axis_size(axis))
    cut = max(range(1, max(2, tiles.ndim - 1)), key=lambda d: tiles.shape[d])
    gathered = []
    for share in jnp.split(tiles, piece_ends(tiles.shape[cut], pieces), axis=cut):
        if share.size:
            gathered.append(lax.all_to_all(share, axis, split_axis=0, concat_axis=0, tiled=True))
    return laid_out(jnp.concatenate(gathered, axis=cut), concat_dim)


def compress_batch(panel_tiles, tile_ranks, sketch_cols):
    keep_cols = jnp.arange(sketch_cols.shape[1])[None, :] < tile_ranks[:, None]
    masked = jnp.where(keep_cols[:, None, :], sketch_cols[None], jnp.zeros_like(sketch_cols)[None])
    sketched = jnp.einsum("bij,bjk->bik", panel_tiles, masked, preferred_element_type=jnp.float32)
    padding = jnp.where(keep_cols, 0.0, 1.0).astype(jnp.float32)
    gram = jnp.einsum("bij,bik->bjk", sketched, sketched, precision=HI)
    gram = gram + padding[:, :, None] * jnp.eye(gram.shape[1], dtype=jnp.float32)[None]
    gram = (gram + jnp.swapaxes(gram, 1, 2)) * 0.5
    inverse = chol_inv(gram)
    basis = jnp.einsum(
        "bij,bkj->bik", sketched, inverse, precision=HI, preferred_element_type=jnp.float32
    ).astype(jnp.bfloat16)
    coeffs = jnp.einsum(
        "bij,bik->bjk", panel_tiles, basis, preferred_element_type=jnp.float32
    ).astype(jnp.bfloat16)
    return jnp.concatenate([basis, coeffs], axis=2)


def slot_numbers(helpers):
    total = helpers.shape[0]
    same_helper = helpers[:, None] == helpers[None, :]
    earlier = jnp.arange(total)[None, :] < jnp.arange(total)[:, None]
    return jnp.sum(jnp.logical_and(same_helper, earlier).astype(jnp.int32), axis=1)


def pack_slabs(slabs, helpers, slots, owners, capacity):
    target = slots * owners + helpers
    table = (jnp.arange(capacity * owners)[:, None] == target[None, :]).astype(jnp.bfloat16)
    packed = jnp.einsum("sk,kab->sab", table, slabs, preferred_element_type=jnp.float32).astype(
        jnp.bfloat16
    )
    return packed.reshape(capacity, owners * slabs.shape[1], slabs.shape[2])


def slot_ranks(ranks, helpers, slots, myself, capacity):
    chosen = jnp.logical_and(
        helpers[None, :] == myself, slots[None, :] == jnp.arange(capacity)[:, None]
    )
    return jnp.sum(jnp.where(chosen, ranks[None, :], 0), axis=1)


def pick_mine(returned, helpers, slots, capacity):
    target = helpers * capacity + slots
    table = (target[:, None] == jnp.arange(returned.shape[0])[None, :]).astype(jnp.bfloat16)
    return jnp.einsum("kn,nab->kab", table, returned, preferred_element_type=jnp.float32).astype(
        jnp.bfloat16
    )


def local(trailing, raw_l, raw_u, sketch, helper_l, helper_u, ranks_l, ranks_u):
    depth = raw_l.shape[1]
    width_r = sketch.shape[3]
    own_sketch = sketch[0, 0]
    compress_all = compress_batch
    col_count = lax.axis_size(COL)
    row_count = lax.axis_size("row")
    cap_row = 2 * depth // col_count
    cap_col = 2 * depth // row_count
    helpers_row = helper_l[0]
    slots_row = slot_numbers(helpers_row)
    sent_row = pack_slabs(raw_l[0], helpers_row, slots_row, col_count, cap_row)
    tiles_row = exchange_by_chip(sent_row, (("col_0", "col_1"), "col_2"), (1, 0), 1, 1)
    made_row = compress_all(
        tiles_row,
        slot_ranks(ranks_l[0], helpers_row, slots_row, lax.axis_index(COL), cap_row),
        own_sketch,
    )
    helpers_col = helper_u[:, 0]
    slots_col = slot_numbers(helpers_col)
    sent_col = pack_slabs(raw_u[:, 0], helpers_col, slots_col, row_count, cap_col)
    tiles_col = cut_exchange(sent_col, "row", 2, 1, 1)
    made_col = compress_all(
        tiles_col,
        slot_ranks(ranks_u[:, 0], helpers_col, slots_col, lax.axis_index("row"), cap_col),
        own_sketch,
    )
    back_row = lax.all_to_all(made_row, COL, split_axis=1, concat_axis=0, tiled=True)
    full_row = lax.all_gather(
        pick_mine(back_row, helpers_row, slots_row, cap_row), COL, axis=1, tiled=True
    )
    back_col = cut_exchange(made_col, "row", 2, 1, 0)
    full_col = lax.all_gather(
        pick_mine(back_col, helpers_col, slots_col, cap_col), "row", axis=1, tiled=True
    )
    return trailing_update(full_row, full_col, trailing)


def solution(mesh):
    torus = Mesh(
        mesh.devices.reshape(mesh.shape["row"], 2, 4, 2), ("row", "col_0", "col_1", "col_2")
    )
    in_specs = (
        P("row", COL),
        P("row", None, COL, None),
        P(None, COL, "row", None),
        P("row", COL, None, None),
        P("row", None),
        P(None, COL),
        P("row", None),
        P(None, COL),
    )
    out_specs = P("row", COL)
    return jax.shard_map(local, mesh=torus, in_specs=in_specs, out_specs=out_specs, check_vma=False)
```

```python
import jax
import jax.numpy as jnp
from jax import lax
from jax.sharding import Mesh
from jax.sharding import PartitionSpec as P
from jax.experimental import pallas as pl
from jax.experimental.pallas import tpu as pltpu

HI = lax.Precision.HIGHEST


def _eliminate(a, n):
    rows = lax.broadcasted_iota(jnp.int32, (1, n, 1), 1)
    cols = lax.broadcasted_iota(jnp.int32, (1, 1, n), 2)
    ident = jnp.broadcast_to((rows == cols).astype(jnp.float32), a.shape)

    def step(j, carry):
        xa, xb = carry
        at_row = rows == j
        at_col = cols == j
        row_a = jnp.sum(jnp.where(at_row, xa, 0.0), axis=1, keepdims=True)
        row_b = jnp.sum(jnp.where(at_row, xb, 0.0), axis=1, keepdims=True)
        col = jnp.sum(jnp.where(at_col, xa, 0.0), axis=2, keepdims=True)
        pivot = jnp.sum(jnp.where(at_col, row_a, 0.0), axis=2, keepdims=True)
        scale = 1.0 / jnp.sqrt(pivot)
        ra = row_a * scale
        rb = row_b * scale
        mult = jnp.where(rows > j, col * scale, 0.0)
        xa = jnp.where(at_row, ra, xa - mult * ra)
        xb = jnp.where(at_row, rb, xb - mult * rb)
        return xa, xb

    _, xb = lax.fori_loop(0, n, step, (a, ident), unroll=4)
    return xb


def _chol_inv_kernel(g_ref, e_ref):
    count, m, _ = g_ref.shape
    h = 128
    e0 = _eliminate(g_ref[:, :h, :h], h)
    for t in range(count):
        g21 = g_ref[t, h:, :h]
        v = lax.dot_general(g21, e0[t], (((1,), (1,)), ((), ())), precision=HI,
                            preferred_element_type=jnp.float32)
        s = g_ref[t, h:, h:] - lax.dot_general(v, v, (((1,), (1,)), ((), ())), precision=HI,
                                               preferred_element_type=jnp.float32)
        e_ref[t, h:, h:] = s
        e_ref[t, :h, :h] = e0[t]
        e_ref[t, :h, h:] = jnp.zeros((h, m - h), jnp.float32)
        e_ref[t, h:, :h] = jnp.dot(v, e0[t], precision=HI, preferred_element_type=jnp.float32)
    e1 = _eliminate(e_ref[:, h:, h:], m - h)
    for t in range(count):
        e_ref[t, h:, h:] = e1[t]
        e_ref[t, h:, :h] = -jnp.dot(e1[t], e_ref[t, h:, :h], precision=HI,
                                    preferred_element_type=jnp.float32)


def chol_inv(gram):
    return pl.pallas_call(
        _chol_inv_kernel,
        out_shape=jax.ShapeDtypeStruct(gram.shape, jnp.float32),
        in_specs=[pl.BlockSpec(memory_space=pltpu.VMEM)],
        out_specs=pl.BlockSpec(memory_space=pltpu.VMEM),
    )(gram)


def _update_kernel(row_ref, col_ref, t_ref, o_ref):
    k = pl.program_id(0)
    width = row_ref.shape[2] // 2
    term = None
    for part in range(row_ref.shape[0]):
        x = row_ref[part]
        y = col_ref[part]
        middle = lax.dot_general(x[:, width:], y[:, :width], (((0,), (0,)), ((), ())),
                                 preferred_element_type=jnp.float32).astype(jnp.bfloat16)
        left = jnp.dot(x[:, :width], middle, preferred_element_type=jnp.float32).astype(jnp.bfloat16)
        piece = lax.dot_general(left, y[:, width:], (((1,), (1,)), ((), ())),
                                preferred_element_type=jnp.float32)
        term = piece if term is None else term + piece

    @pl.when(k == 0)
    def _():
        o_ref[...] = t_ref[...].astype(jnp.float32) - term

    @pl.when(k > 0)
    def _():
        o_ref[...] -= term


def trailing_update(full_row, full_col, trailing):
    depth, rows, both = full_row.shape
    cols = full_col.shape[1]
    return pl.pallas_call(
        _update_kernel,
        out_shape=jax.ShapeDtypeStruct((rows, cols), jnp.float32),
        grid=(depth // 2,),
        in_specs=[
            pl.BlockSpec((2, rows, both), lambda k: (k, 0, 0)),
            pl.BlockSpec((2, cols, both), lambda k: (k, 0, 0)),
            pl.BlockSpec((rows, cols), lambda k: (0, 0)),
        ],
        out_specs=pl.BlockSpec((rows, cols), lambda k: (0, 0)),
        compiler_params=pltpu.CompilerParams(
            dimension_semantics=("arbitrary",), vmem_limit_bytes=48 * 1024 * 1024
        ),
    )(full_row, full_col, trailing)


MESH_ID = pl.DeviceIdType.MESH


def _row_exchange_kernel(s_ref, o_ref, sems, own_sem):
    n_row = lax.axis_size("row")
    rows = o_ref.shape[2]
    me = lax.axis_index("row")
    c0 = lax.axis_index("col_0")
    c1 = lax.axis_index("col_1")
    c2 = lax.axis_index("col_2")

    def row_dev(o):
        return (o, c0, c1, c2)

    barrier = pltpu.get_barrier_semaphore()
    for step in range(1, n_row):
        pl.semaphore_signal(barrier, 1, device_id=row_dev(lax.rem(me + step, n_row)),
                            device_id_type=MESH_ID)
    pl.semaphore_wait(barrier, n_row - 1)
    copies = []
    for step in range(1, n_row):
        target = lax.rem(me + step, n_row)
        copies.append(pltpu.make_async_remote_copy(
            src_ref=s_ref.at[:, pl.ds(target * rows, rows)], dst_ref=o_ref.at[:, me],
            send_sem=sems.at[0, step], recv_sem=sems.at[1, step],
            device_id=row_dev(target), device_id_type=MESH_ID))
    for cp in copies:
        cp.start()
    own = pltpu.make_async_copy(s_ref.at[:, pl.ds(me * rows, rows)], o_ref.at[:, me], own_sem.at[0])
    own.start()
    own.wait()
    for cp in copies:
        cp.wait()


def exchange_rows(sent, n_row):
    cap, total, width = sent.shape
    rows = total // n_row
    out = pl.pallas_call(
        _row_exchange_kernel,
        out_shape=jax.ShapeDtypeStruct((cap, n_row, rows, width), sent.dtype),
        in_specs=[pl.BlockSpec(memory_space=pl.ANY)],
        out_specs=pl.BlockSpec(memory_space=pl.ANY),
        scratch_shapes=[pltpu.SemaphoreType.DMA((2, n_row)), pltpu.SemaphoreType.DMA((1,))],
        compiler_params=pltpu.CompilerParams(collective_id=0, has_side_effects=True),
    )(sent)
    return out.reshape(cap, total, width)


COL = ("col_0", "col_1", "col_2")


def cut_along(value, dim, size):
    before, after = (value.shape[:dim], value.shape[dim + 1 :])
    return jnp.moveaxis(value.reshape(*before, size, -1, *after), dim, 0)


def laid_out(tiles, dim):
    tiles = jnp.moveaxis(tiles, 0, dim)
    lengths = tiles.shape
    return tiles.reshape(*lengths[:dim], lengths[dim] * lengths[dim + 1], *lengths[dim + 2 :])


def turned_blocks(tiles, axes, turns):
    inside = tiles.shape[1:]
    result = tiles.reshape(*(lax.axis_size(a) for a in axes), *inside)
    for k in turns:
        result = lax.all_to_all(result, axes[k], k, k, tiled=True)
    return result.reshape(-1, *inside)


def exchange_by_chip(value, groups, turns, split_dim, concat_dim):
    size = lax.axis_size(groups[0]) * lax.axis_size(groups[1])
    tiles = cut_along(value, split_dim, size)
    return laid_out(turned_blocks(tiles, groups, turns), concat_dim)


def piece_ends(length, count):
    unit = 8 if length >= 8 * count else 1
    return [length // unit * k // count * unit for k in range(1, count)]


def cut_exchange(value, axis, pieces, split_dim, concat_dim):
    tiles = cut_along(value, split_dim, lax.axis_size(axis))
    cut = max(range(1, max(2, tiles.ndim - 1)), key=lambda d: tiles.shape[d])
    gathered = []
    for share in jnp.split(tiles, piece_ends(tiles.shape[cut], pieces), axis=cut):
        if share.size:
            gathered.append(lax.all_to_all(share, axis, split_axis=0, concat_axis=0, tiled=True))
    return laid_out(jnp.concatenate(gathered, axis=cut), concat_dim)


def compress_batch(panel_tiles, tile_ranks, sketch_cols):
    keep_cols = jnp.arange(sketch_cols.shape[1])[None, :] < tile_ranks[:, None]
    masked = jnp.where(keep_cols[:, None, :], sketch_cols[None], jnp.zeros_like(sketch_cols)[None])
    sketched = jnp.einsum("bij,bjk->bik", panel_tiles, masked, preferred_element_type=jnp.float32)
    padding = jnp.where(keep_cols, 0.0, 1.0).astype(jnp.float32)
    gram = jnp.einsum("bij,bik->bjk", sketched, sketched, precision=HI)
    gram = gram + padding[:, :, None] * jnp.eye(gram.shape[1], dtype=jnp.float32)[None]
    gram = (gram + jnp.swapaxes(gram, 1, 2)) * 0.5
    inverse = chol_inv(gram)
    basis = jnp.einsum(
        "bij,bkj->bik", sketched, inverse, precision=HI, preferred_element_type=jnp.float32
    ).astype(jnp.bfloat16)
    coeffs = jnp.einsum(
        "bij,bik->bjk", panel_tiles, basis, preferred_element_type=jnp.float32
    ).astype(jnp.bfloat16)
    return jnp.concatenate([basis, coeffs], axis=2)


def slot_numbers(helpers):
    total = helpers.shape[0]
    same_helper = helpers[:, None] == helpers[None, :]
    earlier = jnp.arange(total)[None, :] < jnp.arange(total)[:, None]
    return jnp.sum(jnp.logical_and(same_helper, earlier).astype(jnp.int32), axis=1)


def pack_slabs(slabs, helpers, slots, owners, capacity):
    target = slots * owners + helpers
    table = (jnp.arange(capacity * owners)[:, None] == target[None, :]).astype(jnp.bfloat16)
    packed = jnp.einsum("sk,kab->sab", table, slabs, preferred_element_type=jnp.float32).astype(
        jnp.bfloat16
    )
    return packed.reshape(capacity, owners * slabs.shape[1], slabs.shape[2])


def slot_ranks(ranks, helpers, slots, myself, capacity):
    chosen = jnp.logical_and(
        helpers[None, :] == myself, slots[None, :] == jnp.arange(capacity)[:, None]
    )
    return jnp.sum(jnp.where(chosen, ranks[None, :], 0), axis=1)


def pick_mine(returned, helpers, slots, capacity):
    target = helpers * capacity + slots
    table = (target[:, None] == jnp.arange(returned.shape[0])[None, :]).astype(jnp.bfloat16)
    return jnp.einsum("kn,nab->kab", table, returned, preferred_element_type=jnp.float32).astype(
        jnp.bfloat16
    )


def local(trailing, raw_l, raw_u, sketch, helper_l, helper_u, ranks_l, ranks_u):
    depth = raw_l.shape[1]
    width_r = sketch.shape[3]
    own_sketch = sketch[0, 0]
    compress_all = compress_batch
    col_count = lax.axis_size(COL)
    row_count = lax.axis_size("row")
    cap_row = 2 * depth // col_count
    cap_col = 2 * depth // row_count
    helpers_row = helper_l[0]
    slots_row = slot_numbers(helpers_row)
    sent_row = pack_slabs(raw_l[0], helpers_row, slots_row, col_count, cap_row)
    tiles_row = exchange_by_chip(sent_row, (("col_0", "col_1"), "col_2"), (1, 0), 1, 1)
    made_row = compress_all(
        tiles_row,
        slot_ranks(ranks_l[0], helpers_row, slots_row, lax.axis_index(COL), cap_row),
        own_sketch,
    )
    helpers_col = helper_u[:, 0]
    slots_col = slot_numbers(helpers_col)
    sent_col = pack_slabs(raw_u[:, 0], helpers_col, slots_col, row_count, cap_col)
    tiles_col = exchange_rows(sent_col, row_count)
    made_col = compress_all(
        tiles_col,
        slot_ranks(ranks_u[:, 0], helpers_col, slots_col, lax.axis_index("row"), cap_col),
        own_sketch,
    )
    back_row = lax.all_to_all(made_row, COL, split_axis=1, concat_axis=0, tiled=True)
    full_row = lax.all_gather(
        pick_mine(back_row, helpers_row, slots_row, cap_row), COL, axis=1, tiled=True
    )
    back_col = cut_exchange(made_col, "row", 2, 1, 0)
    full_col = lax.all_gather(
        pick_mine(back_col, helpers_col, slots_col, cap_col), "row", axis=1, tiled=True
    )
    return trailing_update(full_row, full_col, trailing)


def solution(mesh):
    torus = Mesh(
        mesh.devices.reshape(mesh.shape["row"], 2, 4, 2), ("row", "col_0", "col_1", "col_2")
    )
    in_specs = (
        P("row", COL),
        P("row", None, COL, None),
        P(None, COL, "row", None),
        P("row", COL, None, None),
        P("row", None),
        P(None, COL),
        P("row", None),
        P(None, COL),
    )
    out_specs = P("row", COL)
    return jax.shard_map(local, mesh=torus, in_specs=in_specs, out_specs=out_specs, check_vma=False)
```

```python
import jax
import jax.numpy as jnp
from jax import lax
from jax.sharding import Mesh
from jax.sharding import PartitionSpec as P
from jax.experimental import pallas as pl
from jax.experimental.pallas import tpu as pltpu

HI = lax.Precision.HIGHEST


def _eliminate(a, n):
    rows = lax.broadcasted_iota(jnp.int32, (1, n, 1), 1)
    cols = lax.broadcasted_iota(jnp.int32, (1, 1, n), 2)
    ident = jnp.broadcast_to((rows == cols).astype(jnp.float32), a.shape)

    def step(j, carry):
        xa, xb = carry
        at_row = rows == j
        at_col = cols == j
        row_a = jnp.sum(jnp.where(at_row, xa, 0.0), axis=1, keepdims=True)
        row_b = jnp.sum(jnp.where(at_row, xb, 0.0), axis=1, keepdims=True)
        col = jnp.sum(jnp.where(at_col, xa, 0.0), axis=2, keepdims=True)
        pivot = jnp.sum(jnp.where(at_col, row_a, 0.0), axis=2, keepdims=True)
        scale = 1.0 / jnp.sqrt(pivot)
        ra = row_a * scale
        rb = row_b * scale
        mult = jnp.where(rows > j, col * scale, 0.0)
        xa = jnp.where(at_row, ra, xa - mult * ra)
        xb = jnp.where(at_row, rb, xb - mult * rb)
        return xa, xb

    _, xb = lax.fori_loop(0, n, step, (a, ident), unroll=4)
    return xb


def _chol_inv_kernel(g_ref, e_ref):
    count, m, _ = g_ref.shape
    h = 128
    e0 = _eliminate(g_ref[:, :h, :h], h)
    for t in range(count):
        g21 = g_ref[t, h:, :h]
        v = lax.dot_general(g21, e0[t], (((1,), (1,)), ((), ())), precision=HI,
                            preferred_element_type=jnp.float32)
        s = g_ref[t, h:, h:] - lax.dot_general(v, v, (((1,), (1,)), ((), ())), precision=HI,
                                               preferred_element_type=jnp.float32)
        e_ref[t, h:, h:] = s
        e_ref[t, :h, :h] = e0[t]
        e_ref[t, :h, h:] = jnp.zeros((h, m - h), jnp.float32)
        e_ref[t, h:, :h] = jnp.dot(v, e0[t], precision=HI, preferred_element_type=jnp.float32)
    e1 = _eliminate(e_ref[:, h:, h:], m - h)
    for t in range(count):
        e_ref[t, h:, h:] = e1[t]
        e_ref[t, h:, :h] = -jnp.dot(e1[t], e_ref[t, h:, :h], precision=HI,
                                    preferred_element_type=jnp.float32)


def chol_inv(gram):
    return pl.pallas_call(
        _chol_inv_kernel,
        out_shape=jax.ShapeDtypeStruct(gram.shape, jnp.float32),
        in_specs=[pl.BlockSpec(memory_space=pltpu.VMEM)],
        out_specs=pl.BlockSpec(memory_space=pltpu.VMEM),
    )(gram)


def _update_kernel(row_ref, col_ref, t_ref, o_ref):
    k = pl.program_id(0)
    width = row_ref.shape[2] // 2
    term = None
    for part in range(row_ref.shape[0]):
        x = row_ref[part]
        y = col_ref[part]
        middle = lax.dot_general(x[:, width:], y[:, :width], (((0,), (0,)), ((), ())),
                                 preferred_element_type=jnp.float32).astype(jnp.bfloat16)
        left = jnp.dot(x[:, :width], middle, preferred_element_type=jnp.float32).astype(jnp.bfloat16)
        piece = lax.dot_general(left, y[:, width:], (((1,), (1,)), ((), ())),
                                preferred_element_type=jnp.float32)
        term = piece if term is None else term + piece

    @pl.when(k == 0)
    def _():
        o_ref[...] = t_ref[...].astype(jnp.float32) - term

    @pl.when(k > 0)
    def _():
        o_ref[...] -= term


def trailing_update(full_row, full_col, trailing):
    depth, rows, both = full_row.shape
    cols = full_col.shape[1]
    return pl.pallas_call(
        _update_kernel,
        out_shape=jax.ShapeDtypeStruct((rows, cols), jnp.float32),
        grid=(depth // 4,),
        in_specs=[
            pl.BlockSpec((4, rows, both), lambda k: (k, 0, 0)),
            pl.BlockSpec((4, cols, both), lambda k: (k, 0, 0)),
            pl.BlockSpec((rows, cols), lambda k: (0, 0)),
        ],
        out_specs=pl.BlockSpec((rows, cols), lambda k: (0, 0)),
        compiler_params=pltpu.CompilerParams(
            dimension_semantics=("arbitrary",), vmem_limit_bytes=48 * 1024 * 1024
        ),
    )(full_row, full_col, trailing)


MESH_ID = pl.DeviceIdType.MESH


def _row_exchange_kernel(s_ref, o_ref, sems, own_sem):
    n_row = lax.axis_size("row")
    rows = o_ref.shape[2]
    me = lax.axis_index("row")
    c0 = lax.axis_index("col_0")
    c1 = lax.axis_index("col_1")
    c2 = lax.axis_index("col_2")

    def row_dev(o):
        return (o, c0, c1, c2)

    barrier = pltpu.get_barrier_semaphore()
    for step in range(1, n_row):
        pl.semaphore_signal(barrier, 1, device_id=row_dev(lax.rem(me + step, n_row)),
                            device_id_type=MESH_ID)
    pl.semaphore_wait(barrier, n_row - 1)
    copies = []
    for step in range(1, n_row):
        target = lax.rem(me + step, n_row)
        copies.append(pltpu.make_async_remote_copy(
            src_ref=s_ref.at[:, pl.ds(target * rows, rows)], dst_ref=o_ref.at[:, me],
            send_sem=sems.at[0, step], recv_sem=sems.at[1, step],
            device_id=row_dev(target), device_id_type=MESH_ID))
    for cp in copies:
        cp.start()
    own = pltpu.make_async_copy(s_ref.at[:, pl.ds(me * rows, rows)], o_ref.at[:, me], own_sem.at[0])
    own.start()
    own.wait()
    for cp in copies:
        cp.wait()


def exchange_rows(sent, n_row):
    cap, total, width = sent.shape
    rows = total // n_row
    out = pl.pallas_call(
        _row_exchange_kernel,
        out_shape=jax.ShapeDtypeStruct((cap, n_row, rows, width), sent.dtype),
        in_specs=[pl.BlockSpec(memory_space=pl.ANY)],
        out_specs=pl.BlockSpec(memory_space=pl.ANY),
        scratch_shapes=[pltpu.SemaphoreType.DMA((2, n_row)), pltpu.SemaphoreType.DMA((1,))],
        compiler_params=pltpu.CompilerParams(collective_id=0, has_side_effects=True),
    )(sent)
    return out.reshape(cap, total, width)


COL = ("col_0", "col_1", "col_2")


def cut_along(value, dim, size):
    before, after = (value.shape[:dim], value.shape[dim + 1 :])
    return jnp.moveaxis(value.reshape(*before, size, -1, *after), dim, 0)


def laid_out(tiles, dim):
    tiles = jnp.moveaxis(tiles, 0, dim)
    lengths = tiles.shape
    return tiles.reshape(*lengths[:dim], lengths[dim] * lengths[dim + 1], *lengths[dim + 2 :])


def turned_blocks(tiles, axes, turns):
    inside = tiles.shape[1:]
    result = tiles.reshape(*(lax.axis_size(a) for a in axes), *inside)
    for k in turns:
        result = lax.all_to_all(result, axes[k], k, k, tiled=True)
    return result.reshape(-1, *inside)


def exchange_by_chip(value, groups, turns, split_dim, concat_dim):
    size = lax.axis_size(groups[0]) * lax.axis_size(groups[1])
    tiles = cut_along(value, split_dim, size)
    return laid_out(turned_blocks(tiles, groups, turns), concat_dim)


def piece_ends(length, count):
    unit = 8 if length >= 8 * count else 1
    return [length // unit * k // count * unit for k in range(1, count)]


def cut_exchange(value, axis, pieces, split_dim, concat_dim):
    tiles = cut_along(value, split_dim, lax.axis_size(axis))
    cut = max(range(1, max(2, tiles.ndim - 1)), key=lambda d: tiles.shape[d])
    gathered = []
    for share in jnp.split(tiles, piece_ends(tiles.shape[cut], pieces), axis=cut):
        if share.size:
            gathered.append(lax.all_to_all(share, axis, split_axis=0, concat_axis=0, tiled=True))
    return laid_out(jnp.concatenate(gathered, axis=cut), concat_dim)


def compress_batch(panel_tiles, tile_ranks, sketch_cols):
    keep_cols = jnp.arange(sketch_cols.shape[1])[None, :] < tile_ranks[:, None]
    masked = jnp.where(keep_cols[:, None, :], sketch_cols[None], jnp.zeros_like(sketch_cols)[None])
    sketched = jnp.einsum("bij,bjk->bik", panel_tiles, masked, preferred_element_type=jnp.float32)
    padding = jnp.where(keep_cols, 0.0, 1.0).astype(jnp.float32)
    gram = jnp.einsum("bij,bik->bjk", sketched, sketched, precision=HI)
    gram = gram + padding[:, :, None] * jnp.eye(gram.shape[1], dtype=jnp.float32)[None]
    gram = (gram + jnp.swapaxes(gram, 1, 2)) * 0.5
    inverse = chol_inv(gram)
    basis = jnp.einsum(
        "bij,bkj->bik", sketched, inverse, precision=HI, preferred_element_type=jnp.float32
    ).astype(jnp.bfloat16)
    coeffs = jnp.einsum(
        "bij,bik->bjk", panel_tiles, basis, preferred_element_type=jnp.float32
    ).astype(jnp.bfloat16)
    return jnp.concatenate([basis, coeffs], axis=2)


def slot_numbers(helpers):
    total = helpers.shape[0]
    same_helper = helpers[:, None] == helpers[None, :]
    earlier = jnp.arange(total)[None, :] < jnp.arange(total)[:, None]
    return jnp.sum(jnp.logical_and(same_helper, earlier).astype(jnp.int32), axis=1)


def pack_slabs(slabs, helpers, slots, owners, capacity):
    target = slots * owners + helpers
    hits = jnp.arange(capacity * owners)[:, None] == target[None, :]
    source = jnp.sum(jnp.where(hits, jnp.arange(slabs.shape[0])[None, :], 0), axis=1)
    found = jnp.any(hits, axis=1)
    packed = jnp.where(found[:, None, None], jnp.take(slabs, source, axis=0), jnp.zeros_like(slabs[:1]))
    return packed.reshape(capacity, owners * slabs.shape[1], slabs.shape[2])


def slot_ranks(ranks, helpers, slots, myself, capacity):
    chosen = jnp.logical_and(
        helpers[None, :] == myself, slots[None, :] == jnp.arange(capacity)[:, None]
    )
    return jnp.sum(jnp.where(chosen, ranks[None, :], 0), axis=1)


def pick_mine(returned, helpers, slots, capacity):
    target = helpers * capacity + slots
    table = (target[:, None] == jnp.arange(returned.shape[0])[None, :]).astype(jnp.bfloat16)
    return jnp.einsum("kn,nab->kab", table, returned, preferred_element_type=jnp.float32).astype(
        jnp.bfloat16
    )


def local(trailing, raw_l, raw_u, sketch, helper_l, helper_u, ranks_l, ranks_u):
    depth = raw_l.shape[1]
    width_r = sketch.shape[3]
    own_sketch = sketch[0, 0]
    compress_all = compress_batch
    col_count = lax.axis_size(COL)
    row_count = lax.axis_size("row")
    cap_row = 2 * depth // col_count
    cap_col = 2 * depth // row_count
    helpers_row = helper_l[0]
    slots_row = slot_numbers(helpers_row)
    sent_row = pack_slabs(raw_l[0], helpers_row, slots_row, col_count, cap_row)
    tiles_row = exchange_by_chip(sent_row, (("col_0", "col_1"), "col_2"), (1, 0), 1, 1)
    made_row = compress_all(
        tiles_row,
        slot_ranks(ranks_l[0], helpers_row, slots_row, lax.axis_index(COL), cap_row),
        own_sketch,
    )
    helpers_col = helper_u[:, 0]
    slots_col = slot_numbers(helpers_col)
    sent_col = pack_slabs(raw_u[:, 0], helpers_col, slots_col, row_count, cap_col)
    tiles_col = exchange_rows(sent_col, row_count)
    made_col = compress_all(
        tiles_col,
        slot_ranks(ranks_u[:, 0], helpers_col, slots_col, lax.axis_index("row"), cap_col),
        own_sketch,
    )
    back_row = lax.all_to_all(made_row, COL, split_axis=1, concat_axis=0, tiled=True)
    full_row = lax.all_gather(
        pick_mine(back_row, helpers_row, slots_row, cap_row), COL, axis=1, tiled=True
    )
    back_col = cut_exchange(made_col, "row", 2, 1, 0)
    full_col = lax.all_gather(
        pick_mine(back_col, helpers_col, slots_col, cap_col), "row", axis=1, tiled=True
    )
    return trailing_update(full_row, full_col, trailing)


def solution(mesh):
    torus = Mesh(
        mesh.devices.reshape(mesh.shape["row"], 2, 4, 2), ("row", "col_0", "col_1", "col_2")
    )
    in_specs = (
        P("row", COL),
        P("row", None, COL, None),
        P(None, COL, "row", None),
        P("row", COL, None, None),
        P("row", None),
        P(None, COL),
        P("row", None),
        P(None, COL),
    )
    out_specs = P("row", COL)
    return jax.shard_map(local, mesh=torus, in_specs=in_specs, out_specs=out_specs, check_vma=False)
```

```python
import jax
import jax.numpy as jnp
from jax import lax
from jax.sharding import Mesh
from jax.sharding import PartitionSpec as P
from jax.experimental import pallas as pl
from jax.experimental.pallas import tpu as pltpu

HI = lax.Precision.HIGHEST


def _eliminate(a, n):
    rows = lax.broadcasted_iota(jnp.int32, (1, n, 1), 1)
    cols = lax.broadcasted_iota(jnp.int32, (1, 1, n), 2)
    ident = jnp.broadcast_to((rows == cols).astype(jnp.float32), a.shape)

    def step(j, carry):
        xa, xb = carry
        at_row = rows == j
        at_col = cols == j
        row_a = jnp.sum(jnp.where(at_row, xa, 0.0), axis=1, keepdims=True)
        row_b = jnp.sum(jnp.where(at_row, xb, 0.0), axis=1, keepdims=True)
        col = jnp.sum(jnp.where(at_col, xa, 0.0), axis=2, keepdims=True)
        pivot = jnp.sum(jnp.where(at_col, row_a, 0.0), axis=2, keepdims=True)
        scale = 1.0 / jnp.sqrt(pivot)
        ra = row_a * scale
        rb = row_b * scale
        mult = jnp.where(rows > j, col * scale, 0.0)
        xa = jnp.where(at_row, ra, xa - mult * ra)
        xb = jnp.where(at_row, rb, xb - mult * rb)
        return xa, xb

    _, xb = lax.fori_loop(0, n, step, (a, ident), unroll=4)
    return xb


def _chol_inv_kernel(g_ref, e_ref):
    count, m, _ = g_ref.shape
    h = 128
    e0 = _eliminate(g_ref[:, :h, :h], h)
    for t in range(count):
        g21 = g_ref[t, h:, :h]
        v = lax.dot_general(g21, e0[t], (((1,), (1,)), ((), ())), precision=HI,
                            preferred_element_type=jnp.float32)
        s = g_ref[t, h:, h:] - lax.dot_general(v, v, (((1,), (1,)), ((), ())), precision=HI,
                                               preferred_element_type=jnp.float32)
        e_ref[t, h:, h:] = s
        e_ref[t, :h, :h] = e0[t]
        e_ref[t, :h, h:] = jnp.zeros((h, m - h), jnp.float32)
        e_ref[t, h:, :h] = jnp.dot(v, e0[t], precision=HI, preferred_element_type=jnp.float32)
    e1 = _eliminate(e_ref[:, h:, h:], m - h)
    for t in range(count):
        e_ref[t, h:, h:] = e1[t]
        e_ref[t, h:, :h] = -jnp.dot(e1[t], e_ref[t, h:, :h], precision=HI,
                                    preferred_element_type=jnp.float32)


def chol_inv(gram):
    return pl.pallas_call(
        _chol_inv_kernel,
        out_shape=jax.ShapeDtypeStruct(gram.shape, jnp.float32),
        in_specs=[pl.BlockSpec(memory_space=pltpu.VMEM)],
        out_specs=pl.BlockSpec(memory_space=pltpu.VMEM),
    )(gram)


def _update_kernel(row_ref, col_ref, t_ref, o_ref):
    k = pl.program_id(0)
    width = row_ref.shape[2] // 2
    term = None
    for part in range(row_ref.shape[0]):
        x = row_ref[part]
        y = col_ref[part]
        middle = lax.dot_general(x[:, width:], y[:, :width], (((0,), (0,)), ((), ())),
                                 preferred_element_type=jnp.float32).astype(jnp.bfloat16)
        left = jnp.dot(x[:, :width], middle, preferred_element_type=jnp.float32).astype(jnp.bfloat16)
        piece = lax.dot_general(left, y[:, width:], (((1,), (1,)), ((), ())),
                                preferred_element_type=jnp.float32)
        term = piece if term is None else term + piece

    @pl.when(k == 0)
    def _():
        o_ref[...] = t_ref[...].astype(jnp.float32) - term

    @pl.when(k > 0)
    def _():
        o_ref[...] -= term


def trailing_update(full_row, full_col, trailing):
    depth, rows, both = full_row.shape
    cols = full_col.shape[1]
    return pl.pallas_call(
        _update_kernel,
        out_shape=jax.ShapeDtypeStruct((rows, cols), jnp.float32),
        grid=(depth // 4,),
        in_specs=[
            pl.BlockSpec((4, rows, both), lambda k: (k, 0, 0)),
            pl.BlockSpec((4, cols, both), lambda k: (k, 0, 0)),
            pl.BlockSpec((rows, cols), lambda k: (0, 0)),
        ],
        out_specs=pl.BlockSpec((rows, cols), lambda k: (0, 0)),
        compiler_params=pltpu.CompilerParams(
            dimension_semantics=("arbitrary",), vmem_limit_bytes=48 * 1024 * 1024
        ),
    )(full_row, full_col, trailing)


MESH_ID = pl.DeviceIdType.MESH


def _row_exchange_kernel(s_ref, o_ref, sems, own_sem):
    n_row = lax.axis_size("row")
    rows = o_ref.shape[2]
    me = lax.axis_index("row")
    c0 = lax.axis_index("col_0")
    c1 = lax.axis_index("col_1")
    c2 = lax.axis_index("col_2")

    def row_dev(o):
        return (o, c0, c1, c2)

    barrier = pltpu.get_barrier_semaphore()
    for step in range(1, n_row):
        pl.semaphore_signal(barrier, 1, device_id=row_dev(lax.rem(me + step, n_row)),
                            device_id_type=MESH_ID)
    pl.semaphore_wait(barrier, n_row - 1)
    copies = []
    for step in range(1, n_row):
        target = lax.rem(me + step, n_row)
        copies.append(pltpu.make_async_remote_copy(
            src_ref=s_ref.at[:, pl.ds(target * rows, rows)], dst_ref=o_ref.at[:, me],
            send_sem=sems.at[0, step], recv_sem=sems.at[1, step],
            device_id=row_dev(target), device_id_type=MESH_ID))
    for cp in copies:
        cp.start()
    own = pltpu.make_async_copy(s_ref.at[:, pl.ds(me * rows, rows)], o_ref.at[:, me], own_sem.at[0])
    own.start()
    own.wait()
    for cp in copies:
        cp.wait()


def exchange_rows(sent, n_row, channel):
    cap, total, width = sent.shape
    rows = total // n_row
    out = pl.pallas_call(
        _row_exchange_kernel,
        out_shape=jax.ShapeDtypeStruct((cap, n_row, rows, width), sent.dtype),
        in_specs=[pl.BlockSpec(memory_space=pl.ANY)],
        out_specs=pl.BlockSpec(memory_space=pl.ANY),
        scratch_shapes=[pltpu.SemaphoreType.DMA((2, n_row)), pltpu.SemaphoreType.DMA((1,))],
        compiler_params=pltpu.CompilerParams(collective_id=channel, has_side_effects=True),
    )(sent)
    return out.reshape(cap, total, width)


COL = ("col_0", "col_1", "col_2")


def cut_along(value, dim, size):
    before, after = (value.shape[:dim], value.shape[dim + 1 :])
    return jnp.moveaxis(value.reshape(*before, size, -1, *after), dim, 0)


def laid_out(tiles, dim):
    tiles = jnp.moveaxis(tiles, 0, dim)
    lengths = tiles.shape
    return tiles.reshape(*lengths[:dim], lengths[dim] * lengths[dim + 1], *lengths[dim + 2 :])


def turned_blocks(tiles, axes, turns):
    inside = tiles.shape[1:]
    result = tiles.reshape(*(lax.axis_size(a) for a in axes), *inside)
    for k in turns:
        result = lax.all_to_all(result, axes[k], k, k, tiled=True)
    return result.reshape(-1, *inside)


def exchange_by_chip(value, groups, turns, split_dim, concat_dim):
    size = lax.axis_size(groups[0]) * lax.axis_size(groups[1])
    tiles = cut_along(value, split_dim, size)
    return laid_out(turned_blocks(tiles, groups, turns), concat_dim)


def piece_ends(length, count):
    unit = 8 if length >= 8 * count else 1
    return [length // unit * k // count * unit for k in range(1, count)]


def cut_exchange(value, axis, pieces, split_dim, concat_dim):
    tiles = cut_along(value, split_dim, lax.axis_size(axis))
    cut = max(range(1, max(2, tiles.ndim - 1)), key=lambda d: tiles.shape[d])
    gathered = []
    for share in jnp.split(tiles, piece_ends(tiles.shape[cut], pieces), axis=cut):
        if share.size:
            gathered.append(lax.all_to_all(share, axis, split_axis=0, concat_axis=0, tiled=True))
    return laid_out(jnp.concatenate(gathered, axis=cut), concat_dim)


def compress_batch(panel_tiles, tile_ranks, sketch_cols):
    keep_cols = jnp.arange(sketch_cols.shape[1])[None, :] < tile_ranks[:, None]
    masked = jnp.where(keep_cols[:, None, :], sketch_cols[None], jnp.zeros_like(sketch_cols)[None])
    sketched = jnp.einsum("bij,bjk->bik", panel_tiles, masked, preferred_element_type=jnp.float32)
    padding = jnp.where(keep_cols, 0.0, 1.0).astype(jnp.float32)
    gram = jnp.einsum("bij,bik->bjk", sketched, sketched, precision=HI)
    gram = gram + padding[:, :, None] * jnp.eye(gram.shape[1], dtype=jnp.float32)[None]
    gram = (gram + jnp.swapaxes(gram, 1, 2)) * 0.5
    inverse = chol_inv(gram)
    basis = jnp.einsum(
        "bij,bkj->bik", sketched, inverse, precision=HI, preferred_element_type=jnp.float32
    ).astype(jnp.bfloat16)
    coeffs = jnp.einsum(
        "bij,bik->bjk", panel_tiles, basis, preferred_element_type=jnp.float32
    ).astype(jnp.bfloat16)
    return jnp.concatenate([basis, coeffs], axis=2)


def slot_numbers(helpers):
    total = helpers.shape[0]
    same_helper = helpers[:, None] == helpers[None, :]
    earlier = jnp.arange(total)[None, :] < jnp.arange(total)[:, None]
    return jnp.sum(jnp.logical_and(same_helper, earlier).astype(jnp.int32), axis=1)


def pack_slabs(slabs, helpers, slots, owners, capacity):
    target = slots * owners + helpers
    hits = jnp.arange(capacity * owners)[:, None] == target[None, :]
    source = jnp.sum(jnp.where(hits, jnp.arange(slabs.shape[0])[None, :], 0), axis=1)
    found = jnp.any(hits, axis=1)
    packed = jnp.where(found[:, None, None], jnp.take(slabs, source, axis=0), jnp.zeros_like(slabs[:1]))
    return packed.reshape(capacity, owners * slabs.shape[1], slabs.shape[2])


def slot_ranks(ranks, helpers, slots, myself, capacity):
    chosen = jnp.logical_and(
        helpers[None, :] == myself, slots[None, :] == jnp.arange(capacity)[:, None]
    )
    return jnp.sum(jnp.where(chosen, ranks[None, :], 0), axis=1)


def pick_mine(returned, helpers, slots, capacity):
    target = helpers * capacity + slots
    table = (target[:, None] == jnp.arange(returned.shape[0])[None, :]).astype(jnp.bfloat16)
    return jnp.einsum("kn,nab->kab", table, returned, preferred_element_type=jnp.float32).astype(
        jnp.bfloat16
    )


def local(trailing, raw_l, raw_u, sketch, helper_l, helper_u, ranks_l, ranks_u):
    depth = raw_l.shape[1]
    width_r = sketch.shape[3]
    own_sketch = sketch[0, 0]
    compress_all = compress_batch
    col_count = lax.axis_size(COL)
    row_count = lax.axis_size("row")
    cap_row = 2 * depth // col_count
    cap_col = 2 * depth // row_count
    helpers_row = helper_l[0]
    slots_row = slot_numbers(helpers_row)
    sent_row = pack_slabs(raw_l[0], helpers_row, slots_row, col_count, cap_row)
    tiles_row = exchange_by_chip(sent_row, (("col_0", "col_1"), "col_2"), (1, 0), 1, 1)
    made_row = compress_all(
        tiles_row,
        slot_ranks(ranks_l[0], helpers_row, slots_row, lax.axis_index(COL), cap_row),
        own_sketch,
    )
    helpers_col = helper_u[:, 0]
    slots_col = slot_numbers(helpers_col)
    sent_col = pack_slabs(raw_u[:, 0], helpers_col, slots_col, row_count, cap_col)
    tiles_col = exchange_rows(sent_col, row_count, 0)
    made_col = compress_all(
        tiles_col,
        slot_ranks(ranks_u[:, 0], helpers_col, slots_col, lax.axis_index("row"), cap_col),
        own_sketch,
    )
    back_row = lax.all_to_all(made_row, COL, split_axis=1, concat_axis=0, tiled=True)
    full_row = lax.all_gather(
        pick_mine(back_row, helpers_row, slots_row, cap_row), COL, axis=1, tiled=True
    )
    back_col = exchange_rows(made_col, row_count, 1).reshape(
        cap_col * row_count, -1, made_col.shape[2]
    )
    mine_col = jnp.take(back_col, slots_col * row_count + helpers_col, axis=0)
    full_col = lax.all_gather(mine_col, "row", axis=1, tiled=True)
    return trailing_update(full_row, full_col, trailing)


def solution(mesh):
    torus = Mesh(
        mesh.devices.reshape(mesh.shape["row"], 2, 4, 2), ("row", "col_0", "col_1", "col_2")
    )
    in_specs = (
        P("row", COL),
        P("row", None, COL, None),
        P(None, COL, "row", None),
        P("row", COL, None, None),
        P("row", None),
        P(None, COL),
        P("row", None),
        P(None, COL),
    )
    out_specs = P("row", COL)
    return jax.shard_map(local, mesh=torus, in_specs=in_specs, out_specs=out_specs, check_vma=False)
```

```python
import jax
import jax.numpy as jnp
from jax import lax
from jax.sharding import Mesh
from jax.sharding import PartitionSpec as P
from jax.experimental import pallas as pl
from jax.experimental.pallas import tpu as pltpu

HI = lax.Precision.HIGHEST


def _eliminate(a, n):
    rows = lax.broadcasted_iota(jnp.int32, (1, n, 1), 1)
    cols = lax.broadcasted_iota(jnp.int32, (1, 1, n), 2)
    ident = jnp.broadcast_to((rows == cols).astype(jnp.float32), a.shape)

    def step(j, carry):
        xa, xb = carry
        at_row = rows == j
        at_col = cols == j
        row_a = jnp.sum(jnp.where(at_row, xa, 0.0), axis=1, keepdims=True)
        row_b = jnp.sum(jnp.where(at_row, xb, 0.0), axis=1, keepdims=True)
        col = jnp.sum(jnp.where(at_col, xa, 0.0), axis=2, keepdims=True)
        pivot = jnp.sum(jnp.where(at_col, row_a, 0.0), axis=2, keepdims=True)
        scale = 1.0 / jnp.sqrt(pivot)
        ra = row_a * scale
        rb = row_b * scale
        mult = jnp.where(rows > j, col * scale, 0.0)
        xa = jnp.where(at_row, ra, xa - mult * ra)
        xb = jnp.where(at_row, rb, xb - mult * rb)
        return xa, xb

    _, xb = lax.fori_loop(0, n, step, (a, ident), unroll=4)
    return xb


def _mm(a, b):
    return jnp.dot(a, b, precision=HI, preferred_element_type=jnp.float32)


def _mmt(a, b):
    return lax.dot_general(a, b, (((1,), (1,)), ((), ())), precision=HI,
                           preferred_element_type=jnp.float32)


def _chol_inv_kernel(g_ref, e_ref):
    count = g_ref.shape[0]
    nb = g_ref.shape[3]
    e0 = _eliminate(g_ref[:, 0, 0], nb)
    v1s, v2s, s11s = [], [], []
    for t in range(count):
        v1 = _mmt(g_ref[t, 1, 0], e0[t])
        v2 = _mmt(g_ref[t, 2, 0], e0[t])
        v1s.append(v1)
        v2s.append(v2)
        s11s.append(g_ref[t, 1, 1] - _mmt(v1, v1))
    e1 = _eliminate(jnp.stack(s11s), nb)
    ws, s22s = [], []
    for t in range(count):
        s21 = g_ref[t, 2, 1] - _mmt(v2s[t], v1s[t])
        w = _mmt(s21, e1[t])
        ws.append(w)
        s22s.append(g_ref[t, 2, 2] - _mmt(v2s[t], v2s[t]) - _mmt(w, w))
    e2 = _eliminate(jnp.stack(s22s), nb)
    zero = jnp.zeros((nb, nb), jnp.float32)
    for t in range(count):
        x10 = -_mm(e1[t], _mm(v1s[t], e0[t]))
        x21 = -_mm(e2[t], _mm(ws[t], e1[t]))
        x20 = -_mm(e2[t], _mm(v2s[t], e0[t]) + _mm(ws[t], x10))
        e_ref[t, 0, 0] = e0[t]
        e_ref[t, 0, 1] = zero
        e_ref[t, 0, 2] = zero
        e_ref[t, 1, 0] = x10
        e_ref[t, 1, 1] = e1[t]
        e_ref[t, 1, 2] = zero
        e_ref[t, 2, 0] = x20
        e_ref[t, 2, 1] = x21
        e_ref[t, 2, 2] = e2[t]


def chol_inv(gram):
    count, m, _ = gram.shape
    nb = m // 3
    blocks = gram.reshape(count, 3, nb, 3, nb).transpose(0, 1, 3, 2, 4)
    inverse = pl.pallas_call(
        _chol_inv_kernel,
        out_shape=jax.ShapeDtypeStruct(blocks.shape, jnp.float32),
        in_specs=[pl.BlockSpec(memory_space=pltpu.VMEM)],
        out_specs=pl.BlockSpec(memory_space=pltpu.VMEM),
    )(blocks)
    return inverse.transpose(0, 1, 3, 2, 4).reshape(count, m, m)


def _update_kernel(row_ref, col_ref, t_ref, o_ref):
    k = pl.program_id(0)
    width = row_ref.shape[2] // 2
    term = None
    for part in range(row_ref.shape[0]):
        x = row_ref[part]
        y = col_ref[part]
        middle = lax.dot_general(x[:, width:], y[:, :width], (((0,), (0,)), ((), ())),
                                 preferred_element_type=jnp.float32).astype(jnp.bfloat16)
        left = jnp.dot(x[:, :width], middle, preferred_element_type=jnp.float32).astype(jnp.bfloat16)
        piece = lax.dot_general(left, y[:, width:], (((1,), (1,)), ((), ())),
                                preferred_element_type=jnp.float32)
        term = piece if term is None else term + piece

    @pl.when(k == 0)
    def _():
        o_ref[...] = t_ref[...].astype(jnp.float32) - term

    @pl.when(k > 0)
    def _():
        o_ref[...] -= term


def trailing_update(full_row, full_col, trailing):
    depth, rows, both = full_row.shape
    cols = full_col.shape[1]
    return pl.pallas_call(
        _update_kernel,
        out_shape=jax.ShapeDtypeStruct((rows, cols), jnp.float32),
        grid=(depth // 4,),
        in_specs=[
            pl.BlockSpec((4, rows, both), lambda k: (k, 0, 0)),
            pl.BlockSpec((4, cols, both), lambda k: (k, 0, 0)),
            pl.BlockSpec((rows, cols), lambda k: (0, 0)),
        ],
        out_specs=pl.BlockSpec((rows, cols), lambda k: (0, 0)),
        compiler_params=pltpu.CompilerParams(
            dimension_semantics=("arbitrary",), vmem_limit_bytes=48 * 1024 * 1024
        ),
    )(full_row, full_col, trailing)


MESH_ID = pl.DeviceIdType.MESH


def _row_exchange_kernel(s_ref, o_ref, sems, own_sem):
    n_row = lax.axis_size("row")
    rows = o_ref.shape[2]
    me = lax.axis_index("row")
    c0 = lax.axis_index("col_0")
    c1 = lax.axis_index("col_1")
    c2 = lax.axis_index("col_2")

    def row_dev(o):
        return (o, c0, c1, c2)

    barrier = pltpu.get_barrier_semaphore()
    for step in range(1, n_row):
        pl.semaphore_signal(barrier, 1, device_id=row_dev(lax.rem(me + step, n_row)),
                            device_id_type=MESH_ID)
    pl.semaphore_wait(barrier, n_row - 1)
    copies = []
    for step in range(1, n_row):
        target = lax.rem(me + step, n_row)
        copies.append(pltpu.make_async_remote_copy(
            src_ref=s_ref.at[:, pl.ds(target * rows, rows)], dst_ref=o_ref.at[:, me],
            send_sem=sems.at[0, step], recv_sem=sems.at[1, step],
            device_id=row_dev(target), device_id_type=MESH_ID))
    for cp in copies:
        cp.start()
    own = pltpu.make_async_copy(s_ref.at[:, pl.ds(me * rows, rows)], o_ref.at[:, me], own_sem.at[0])
    own.start()
    own.wait()
    for cp in copies:
        cp.wait()


def exchange_rows(sent, n_row):
    cap, total, width = sent.shape
    rows = total // n_row
    out = pl.pallas_call(
        _row_exchange_kernel,
        out_shape=jax.ShapeDtypeStruct((cap, n_row, rows, width), sent.dtype),
        in_specs=[pl.BlockSpec(memory_space=pl.ANY)],
        out_specs=pl.BlockSpec(memory_space=pl.ANY),
        scratch_shapes=[pltpu.SemaphoreType.DMA((2, n_row)), pltpu.SemaphoreType.DMA((1,))],
        compiler_params=pltpu.CompilerParams(collective_id=0, has_side_effects=True),
    )(sent)
    return out.reshape(cap, total, width)


COL = ("col_0", "col_1", "col_2")


def cut_along(value, dim, size):
    before, after = (value.shape[:dim], value.shape[dim + 1 :])
    return jnp.moveaxis(value.reshape(*before, size, -1, *after), dim, 0)


def laid_out(tiles, dim):
    tiles = jnp.moveaxis(tiles, 0, dim)
    lengths = tiles.shape
    return tiles.reshape(*lengths[:dim], lengths[dim] * lengths[dim + 1], *lengths[dim + 2 :])


def turned_blocks(tiles, axes, turns):
    inside = tiles.shape[1:]
    result = tiles.reshape(*(lax.axis_size(a) for a in axes), *inside)
    for k in turns:
        result = lax.all_to_all(result, axes[k], k, k, tiled=True)
    return result.reshape(-1, *inside)


def exchange_by_chip(value, groups, turns, split_dim, concat_dim):
    size = lax.axis_size(groups[0]) * lax.axis_size(groups[1])
    tiles = cut_along(value, split_dim, size)
    return laid_out(turned_blocks(tiles, groups, turns), concat_dim)


def piece_ends(length, count):
    unit = 8 if length >= 8 * count else 1
    return [length // unit * k // count * unit for k in range(1, count)]


def cut_exchange(value, axis, pieces, split_dim, concat_dim):
    tiles = cut_along(value, split_dim, lax.axis_size(axis))
    cut = max(range(1, max(2, tiles.ndim - 1)), key=lambda d: tiles.shape[d])
    gathered = []
    for share in jnp.split(tiles, piece_ends(tiles.shape[cut], pieces), axis=cut):
        if share.size:
            gathered.append(lax.all_to_all(share, axis, split_axis=0, concat_axis=0, tiled=True))
    return laid_out(jnp.concatenate(gathered, axis=cut), concat_dim)


def compress_batch(panel_tiles, tile_ranks, sketch_cols):
    keep_cols = jnp.arange(sketch_cols.shape[1])[None, :] < tile_ranks[:, None]
    masked = jnp.where(keep_cols[:, None, :], sketch_cols[None], jnp.zeros_like(sketch_cols)[None])
    sketched = jnp.einsum("bij,bjk->bik", panel_tiles, masked, preferred_element_type=jnp.float32)
    padding = jnp.where(keep_cols, 0.0, 1.0).astype(jnp.float32)
    gram = jnp.einsum("bij,bik->bjk", sketched, sketched, precision=HI)
    gram = gram + padding[:, :, None] * jnp.eye(gram.shape[1], dtype=jnp.float32)[None]
    gram = (gram + jnp.swapaxes(gram, 1, 2)) * 0.5
    inverse = chol_inv(gram)
    basis = jnp.einsum(
        "bij,bkj->bik", sketched, inverse, precision=HI, preferred_element_type=jnp.float32
    ).astype(jnp.bfloat16)
    coeffs = jnp.einsum(
        "bij,bik->bjk", panel_tiles, basis, preferred_element_type=jnp.float32
    ).astype(jnp.bfloat16)
    return jnp.concatenate([basis, coeffs], axis=2)


def slot_numbers(helpers):
    total = helpers.shape[0]
    same_helper = helpers[:, None] == helpers[None, :]
    earlier = jnp.arange(total)[None, :] < jnp.arange(total)[:, None]
    return jnp.sum(jnp.logical_and(same_helper, earlier).astype(jnp.int32), axis=1)


def pack_slabs(slabs, helpers, slots, owners, capacity):
    target = slots * owners + helpers
    hits = jnp.arange(capacity * owners)[:, None] == target[None, :]
    source = jnp.sum(jnp.where(hits, jnp.arange(slabs.shape[0])[None, :], 0), axis=1)
    found = jnp.any(hits, axis=1)
    packed = jnp.where(found[:, None, None], jnp.take(slabs, source, axis=0), jnp.zeros_like(slabs[:1]))
    return packed.reshape(capacity, owners * slabs.shape[1], slabs.shape[2])


def slot_ranks(ranks, helpers, slots, myself, capacity):
    chosen = jnp.logical_and(
        helpers[None, :] == myself, slots[None, :] == jnp.arange(capacity)[:, None]
    )
    return jnp.sum(jnp.where(chosen, ranks[None, :], 0), axis=1)


def pick_mine(returned, helpers, slots, capacity):
    target = helpers * capacity + slots
    table = (target[:, None] == jnp.arange(returned.shape[0])[None, :]).astype(jnp.bfloat16)
    return jnp.einsum("kn,nab->kab", table, returned, preferred_element_type=jnp.float32).astype(
        jnp.bfloat16
    )


def local(trailing, raw_l, raw_u, sketch, helper_l, helper_u, ranks_l, ranks_u):
    depth = raw_l.shape[1]
    width_r = sketch.shape[3]
    own_sketch = sketch[0, 0]
    compress_all = compress_batch
    col_count = lax.axis_size(COL)
    row_count = lax.axis_size("row")
    cap_row = 2 * depth // col_count
    cap_col = 2 * depth // row_count
    helpers_row = helper_l[0]
    slots_row = slot_numbers(helpers_row)
    sent_row = pack_slabs(raw_l[0], helpers_row, slots_row, col_count, cap_row)
    tiles_row = exchange_by_chip(sent_row, (("col_0", "col_1"), "col_2"), (1, 0), 1, 1)
    made_row = compress_all(
        tiles_row,
        slot_ranks(ranks_l[0], helpers_row, slots_row, lax.axis_index(COL), cap_row),
        own_sketch,
    )
    helpers_col = helper_u[:, 0]
    slots_col = slot_numbers(helpers_col)
    sent_col = pack_slabs(raw_u[:, 0], helpers_col, slots_col, row_count, cap_col)
    tiles_col = exchange_rows(sent_col, row_count)
    made_col = compress_all(
        tiles_col,
        slot_ranks(ranks_u[:, 0], helpers_col, slots_col, lax.axis_index("row"), cap_col),
        own_sketch,
    )
    back_row = lax.all_to_all(made_row, COL, split_axis=1, concat_axis=0, tiled=True)
    full_row = lax.all_gather(
        pick_mine(back_row, helpers_row, slots_row, cap_row), COL, axis=1, tiled=True
    )
    back_col = cut_exchange(made_col, "row", 2, 1, 0)
    full_col = lax.all_gather(
        pick_mine(back_col, helpers_col, slots_col, cap_col), "row", axis=1, tiled=True
    )
    return trailing_update(full_row, full_col, trailing)


def solution(mesh):
    torus = Mesh(
        mesh.devices.reshape(mesh.shape["row"], 2, 4, 2), ("row", "col_0", "col_1", "col_2")
    )
    in_specs = (
        P("row", COL),
        P("row", None, COL, None),
        P(None, COL, "row", None),
        P("row", COL, None, None),
        P("row", None),
        P(None, COL),
        P("row", None),
        P(None, COL),
    )
    out_specs = P("row", COL)
    return jax.shard_map(local, mesh=torus, in_specs=in_specs, out_specs=out_specs, check_vma=False)
```

```python
import jax
import jax.numpy as jnp
from jax import lax
from jax.sharding import Mesh
from jax.sharding import PartitionSpec as P
from jax.experimental import pallas as pl
from jax.experimental.pallas import tpu as pltpu

HI = lax.Precision.HIGHEST


def _eliminate(a, n):
    rows = lax.broadcasted_iota(jnp.int32, (1, n, 1), 1)
    cols = lax.broadcasted_iota(jnp.int32, (1, 1, n), 2)
    ident = jnp.broadcast_to((rows == cols).astype(jnp.float32), a.shape)

    def step(j, carry):
        xa, xb = carry
        at_row = rows == j
        at_col = cols == j
        row_a = jnp.sum(jnp.where(at_row, xa, 0.0), axis=1, keepdims=True)
        row_b = jnp.sum(jnp.where(at_row, xb, 0.0), axis=1, keepdims=True)
        col = jnp.sum(jnp.where(at_col, xa, 0.0), axis=2, keepdims=True)
        pivot = jnp.sum(jnp.where(at_col, row_a, 0.0), axis=2, keepdims=True)
        scale = 1.0 / jnp.sqrt(pivot)
        ra = row_a * scale
        rb = row_b * scale
        mult = jnp.where(rows > j, col * scale, 0.0)
        xa = jnp.where(at_row, ra, xa - mult * ra)
        xb = jnp.where(at_row, rb, xb - mult * rb)
        return xa, xb

    _, xb = lax.fori_loop(0, n, step, (a, ident), unroll=4)
    return xb


def _mm(a, b):
    return jnp.dot(a, b, precision=HI, preferred_element_type=jnp.float32)


def _mmt(a, b):
    return lax.dot_general(a, b, (((1,), (1,)), ((), ())), precision=HI,
                           preferred_element_type=jnp.float32)


def _chol_inv_kernel(g_ref, e_ref):
    count = g_ref.shape[0]
    nb = g_ref.shape[3]
    e0 = _eliminate(g_ref[:, 0, 0], nb)
    v1s, v2s, s11s = [], [], []
    for t in range(count):
        v1 = _mmt(g_ref[t, 1, 0], e0[t])
        v2 = _mmt(g_ref[t, 2, 0], e0[t])
        v1s.append(v1)
        v2s.append(v2)
        s11s.append(g_ref[t, 1, 1] - _mmt(v1, v1))
    e1 = _eliminate(jnp.stack(s11s), nb)
    ws, s22s = [], []
    for t in range(count):
        s21 = g_ref[t, 2, 1] - _mmt(v2s[t], v1s[t])
        w = _mmt(s21, e1[t])
        ws.append(w)
        s22s.append(g_ref[t, 2, 2] - _mmt(v2s[t], v2s[t]) - _mmt(w, w))
    e2 = _eliminate(jnp.stack(s22s), nb)
    zero = jnp.zeros((nb, nb), jnp.float32)
    for t in range(count):
        x10 = -_mm(e1[t], _mm(v1s[t], e0[t]))
        x21 = -_mm(e2[t], _mm(ws[t], e1[t]))
        x20 = -_mm(e2[t], _mm(v2s[t], e0[t]) + _mm(ws[t], x10))
        e_ref[t, 0, 0] = e0[t]
        e_ref[t, 0, 1] = zero
        e_ref[t, 0, 2] = zero
        e_ref[t, 1, 0] = x10
        e_ref[t, 1, 1] = e1[t]
        e_ref[t, 1, 2] = zero
        e_ref[t, 2, 0] = x20
        e_ref[t, 2, 1] = x21
        e_ref[t, 2, 2] = e2[t]


def chol_inv(gram):
    count, m, _ = gram.shape
    nb = m // 3
    blocks = gram.reshape(count, 3, nb, 3, nb).transpose(0, 1, 3, 2, 4)
    inverse = pl.pallas_call(
        _chol_inv_kernel,
        out_shape=jax.ShapeDtypeStruct(blocks.shape, jnp.float32),
        in_specs=[pl.BlockSpec(memory_space=pltpu.VMEM)],
        out_specs=pl.BlockSpec(memory_space=pltpu.VMEM),
    )(blocks)
    return inverse.transpose(0, 1, 3, 2, 4).reshape(count, m, m)


def _update_kernel(row_ref, col_ref, t_ref, o_ref):
    k = pl.program_id(0)
    width = row_ref.shape[2] // 2
    term = None
    for part in range(row_ref.shape[0]):
        x = row_ref[part]
        y = col_ref[part]
        middle = lax.dot_general(x[:, width:], y[:, :width], (((0,), (0,)), ((), ())),
                                 preferred_element_type=jnp.float32).astype(jnp.bfloat16)
        left = jnp.dot(x[:, :width], middle, preferred_element_type=jnp.float32).astype(jnp.bfloat16)
        piece = lax.dot_general(left, y[:, width:], (((1,), (1,)), ((), ())),
                                preferred_element_type=jnp.float32)
        term = piece if term is None else term + piece

    @pl.when(k == 0)
    def _():
        o_ref[...] = t_ref[...].astype(jnp.float32) - term

    @pl.when(k > 0)
    def _():
        o_ref[...] -= term


def trailing_update(full_row, full_col, trailing):
    depth, rows, both = full_row.shape
    cols = full_col.shape[1]
    return pl.pallas_call(
        _update_kernel,
        out_shape=jax.ShapeDtypeStruct((rows, cols), jnp.float32),
        grid=(depth // 4,),
        in_specs=[
            pl.BlockSpec((4, rows, both), lambda k: (k, 0, 0)),
            pl.BlockSpec((4, cols, both), lambda k: (k, 0, 0)),
            pl.BlockSpec((rows, cols), lambda k: (0, 0)),
        ],
        out_specs=pl.BlockSpec((rows, cols), lambda k: (0, 0)),
        compiler_params=pltpu.CompilerParams(
            dimension_semantics=("arbitrary",), vmem_limit_bytes=48 * 1024 * 1024
        ),
    )(full_row, full_col, trailing)


MESH_ID = pl.DeviceIdType.MESH


def _row_exchange_kernel(s_ref, o_ref, sems, own_sem):
    n_row = lax.axis_size("row")
    rows = o_ref.shape[2]
    me = lax.axis_index("row")
    c0 = lax.axis_index("col_0")
    c1 = lax.axis_index("col_1")
    c2 = lax.axis_index("col_2")

    def row_dev(o):
        return (o, c0, c1, c2)

    barrier = pltpu.get_barrier_semaphore()
    for step in range(1, n_row):
        pl.semaphore_signal(barrier, 1, device_id=row_dev(lax.rem(me + step, n_row)),
                            device_id_type=MESH_ID)
    pl.semaphore_wait(barrier, n_row - 1)
    copies = []
    for step in range(1, n_row):
        target = lax.rem(me + step, n_row)
        copies.append(pltpu.make_async_remote_copy(
            src_ref=s_ref.at[:, pl.ds(target * rows, rows)], dst_ref=o_ref.at[:, me],
            send_sem=sems.at[0, step], recv_sem=sems.at[1, step],
            device_id=row_dev(target), device_id_type=MESH_ID))
    for cp in copies:
        cp.start()
    own = pltpu.make_async_copy(s_ref.at[:, pl.ds(me * rows, rows)], o_ref.at[:, me], own_sem.at[0])
    own.start()
    own.wait()
    for cp in copies:
        cp.wait()


def exchange_rows(sent, n_row):
    cap, total, width = sent.shape
    rows = total // n_row
    out = pl.pallas_call(
        _row_exchange_kernel,
        out_shape=jax.ShapeDtypeStruct((cap, n_row, rows, width), sent.dtype),
        in_specs=[pl.BlockSpec(memory_space=pl.ANY)],
        out_specs=pl.BlockSpec(memory_space=pl.ANY),
        scratch_shapes=[pltpu.SemaphoreType.DMA((2, n_row)), pltpu.SemaphoreType.DMA((1,))],
        compiler_params=pltpu.CompilerParams(collective_id=0, has_side_effects=True),
    )(sent)
    return out.reshape(cap, total, width)


COL = ("col_0", "col_1", "col_2")


def cut_along(value, dim, size):
    before, after = (value.shape[:dim], value.shape[dim + 1 :])
    return jnp.moveaxis(value.reshape(*before, size, -1, *after), dim, 0)


def laid_out(tiles, dim):
    tiles = jnp.moveaxis(tiles, 0, dim)
    lengths = tiles.shape
    return tiles.reshape(*lengths[:dim], lengths[dim] * lengths[dim + 1], *lengths[dim + 2 :])


def turned_blocks(tiles, axes, turns):
    inside = tiles.shape[1:]
    result = tiles.reshape(*(lax.axis_size(a) for a in axes), *inside)
    for k in turns:
        result = lax.all_to_all(result, axes[k], k, k, tiled=True)
    return result.reshape(-1, *inside)


def exchange_by_chip(value, groups, turns, split_dim, concat_dim):
    size = lax.axis_size(groups[0]) * lax.axis_size(groups[1])
    tiles = cut_along(value, split_dim, size)
    return laid_out(turned_blocks(tiles, groups, turns), concat_dim)


def piece_ends(length, count):
    unit = 8 if length >= 8 * count else 1
    return [length // unit * k // count * unit for k in range(1, count)]


def cut_exchange(value, axis, pieces, split_dim, concat_dim):
    tiles = cut_along(value, split_dim, lax.axis_size(axis))
    cut = max(range(1, max(2, tiles.ndim - 1)), key=lambda d: tiles.shape[d])
    gathered = []
    for share in jnp.split(tiles, piece_ends(tiles.shape[cut], pieces), axis=cut):
        if share.size:
            gathered.append(lax.all_to_all(share, axis, split_axis=0, concat_axis=0, tiled=True))
    return laid_out(jnp.concatenate(gathered, axis=cut), concat_dim)


def compress_batch(panel_tiles, tile_ranks, sketch_cols):
    keep_cols = jnp.arange(sketch_cols.shape[1])[None, :] < tile_ranks[:, None]
    masked = jnp.where(keep_cols[:, None, :], sketch_cols[None], jnp.zeros_like(sketch_cols)[None])
    sketched = jnp.einsum("bij,bjk->bik", panel_tiles, masked, preferred_element_type=jnp.float32)
    padding = jnp.where(keep_cols, 0.0, 1.0).astype(jnp.float32)
    gram = jnp.einsum("bij,bik->bjk", sketched, sketched, precision=HI)
    gram = gram + padding[:, :, None] * jnp.eye(gram.shape[1], dtype=jnp.float32)[None]
    gram = (gram + jnp.swapaxes(gram, 1, 2)) * 0.5
    inverse = chol_inv(gram)
    basis = jnp.einsum(
        "bij,bkj->bik", sketched, inverse, precision=HI, preferred_element_type=jnp.float32
    ).astype(jnp.bfloat16)
    coeffs = jnp.einsum(
        "bij,bik->bjk", panel_tiles, basis, preferred_element_type=jnp.float32
    ).astype(jnp.bfloat16)
    return jnp.concatenate([basis, coeffs], axis=2)


def slot_numbers(helpers):
    total = helpers.shape[0]
    same_helper = helpers[:, None] == helpers[None, :]
    earlier = jnp.arange(total)[None, :] < jnp.arange(total)[:, None]
    return jnp.sum(jnp.logical_and(same_helper, earlier).astype(jnp.int32), axis=1)


def pack_slabs(slabs, helpers, slots, owners, capacity):
    target = slots * owners + helpers
    hits = jnp.arange(capacity * owners)[:, None] == target[None, :]
    source = jnp.sum(jnp.where(hits, jnp.arange(slabs.shape[0])[None, :], 0), axis=1)
    found = jnp.any(hits, axis=1)
    packed = jnp.where(found[:, None, None], jnp.take(slabs, source, axis=0), jnp.zeros_like(slabs[:1]))
    return packed.reshape(capacity, owners * slabs.shape[1], slabs.shape[2])


def slot_ranks(ranks, helpers, slots, myself, capacity):
    chosen = jnp.logical_and(
        helpers[None, :] == myself, slots[None, :] == jnp.arange(capacity)[:, None]
    )
    return jnp.sum(jnp.where(chosen, ranks[None, :], 0), axis=1)


def pick_mine(returned, helpers, slots, capacity):
    return jnp.take(returned, helpers * capacity + slots, axis=0)


def local(trailing, raw_l, raw_u, sketch, helper_l, helper_u, ranks_l, ranks_u):
    depth = raw_l.shape[1]
    width_r = sketch.shape[3]
    own_sketch = sketch[0, 0]
    compress_all = compress_batch
    col_count = lax.axis_size(COL)
    row_count = lax.axis_size("row")
    cap_row = 2 * depth // col_count
    cap_col = 2 * depth // row_count
    helpers_row = helper_l[0]
    slots_row = slot_numbers(helpers_row)
    sent_row = pack_slabs(raw_l[0], helpers_row, slots_row, col_count, cap_row)
    tiles_row = exchange_by_chip(sent_row, (("col_0", "col_1"), "col_2"), (1, 0), 1, 1)
    made_row = compress_all(
        tiles_row,
        slot_ranks(ranks_l[0], helpers_row, slots_row, lax.axis_index(COL), cap_row),
        own_sketch,
    )
    helpers_col = helper_u[:, 0]
    slots_col = slot_numbers(helpers_col)
    sent_col = pack_slabs(raw_u[:, 0], helpers_col, slots_col, row_count, cap_col)
    tiles_col = exchange_rows(sent_col, row_count)
    made_col = compress_all(
        tiles_col,
        slot_ranks(ranks_u[:, 0], helpers_col, slots_col, lax.axis_index("row"), cap_col),
        own_sketch,
    )
    back_row = lax.all_to_all(made_row, COL, split_axis=1, concat_axis=0, tiled=True)
    full_row = lax.all_gather(
        pick_mine(back_row, helpers_row, slots_row, cap_row), COL, axis=1, tiled=True
    )
    back_col = cut_exchange(made_col, "row", 2, 1, 0)
    full_col = lax.all_gather(
        pick_mine(back_col, helpers_col, slots_col, cap_col), "row", axis=1, tiled=True
    )
    return trailing_update(full_row, full_col, trailing)


def solution(mesh):
    torus = Mesh(
        mesh.devices.reshape(mesh.shape["row"], 2, 4, 2), ("row", "col_0", "col_1", "col_2")
    )
    in_specs = (
        P("row", COL),
        P("row", None, COL, None),
        P(None, COL, "row", None),
        P("row", COL, None, None),
        P("row", None),
        P(None, COL),
        P("row", None),
        P(None, COL),
    )
    out_specs = P("row", COL)
    return jax.shard_map(local, mesh=torus, in_specs=in_specs, out_specs=out_specs, check_vma=False)
```

```python
import jax
import jax.numpy as jnp
from jax import lax
from jax.sharding import Mesh
from jax.sharding import PartitionSpec as P
from jax.experimental import pallas as pl
from jax.experimental.pallas import tpu as pltpu

HI = lax.Precision.HIGHEST


def _eliminate(a, n):
    rows = lax.broadcasted_iota(jnp.int32, (1, n, 1), 1)
    cols = lax.broadcasted_iota(jnp.int32, (1, 1, n), 2)
    ident = jnp.broadcast_to((rows == cols).astype(jnp.float32), a.shape)

    def step(j, carry):
        xa, xb = carry
        at_row = rows == j
        at_col = cols == j
        row_a = jnp.sum(jnp.where(at_row, xa, 0.0), axis=1, keepdims=True)
        row_b = jnp.sum(jnp.where(at_row, xb, 0.0), axis=1, keepdims=True)
        col = jnp.sum(jnp.where(at_col, xa, 0.0), axis=2, keepdims=True)
        pivot = jnp.sum(jnp.where(at_col, row_a, 0.0), axis=2, keepdims=True)
        scale = 1.0 / jnp.sqrt(pivot)
        ra = row_a * scale
        rb = row_b * scale
        mult = jnp.where(rows > j, col * scale, 0.0)
        xa = jnp.where(at_row, ra, xa - mult * ra)
        xb = jnp.where(at_row, rb, xb - mult * rb)
        return xa, xb

    _, xb = lax.fori_loop(0, n, step, (a, ident), unroll=4)
    return xb


def _chol_inv_kernel(g_ref, e_ref):
    count, m, _ = g_ref.shape
    h = 128
    e0 = _eliminate(g_ref[:, :h, :h], h)
    for t in range(count):
        g21 = g_ref[t, h:, :h]
        v = lax.dot_general(g21, e0[t], (((1,), (1,)), ((), ())), precision=HI,
                            preferred_element_type=jnp.float32)
        s = g_ref[t, h:, h:] - lax.dot_general(v, v, (((1,), (1,)), ((), ())), precision=HI,
                                               preferred_element_type=jnp.float32)
        e_ref[t, h:, h:] = s
        e_ref[t, :h, :h] = e0[t]
        e_ref[t, :h, h:] = jnp.zeros((h, m - h), jnp.float32)
        e_ref[t, h:, :h] = jnp.dot(v, e0[t], precision=HI, preferred_element_type=jnp.float32)
    e1 = _eliminate(e_ref[:, h:, h:], m - h)
    for t in range(count):
        e_ref[t, h:, h:] = e1[t]
        e_ref[t, h:, :h] = -jnp.dot(e1[t], e_ref[t, h:, :h], precision=HI,
                                    preferred_element_type=jnp.float32)


def chol_inv(gram):
    return pl.pallas_call(
        _chol_inv_kernel,
        out_shape=jax.ShapeDtypeStruct(gram.shape, jnp.float32),
        in_specs=[pl.BlockSpec(memory_space=pltpu.VMEM)],
        out_specs=pl.BlockSpec(memory_space=pltpu.VMEM),
    )(gram)


def _update_kernel(row_ref, col_ref, t_ref, o_ref):
    k = pl.program_id(0)
    width = row_ref.shape[2] // 2
    term = None
    for part in range(row_ref.shape[0]):
        x = row_ref[part]
        y = col_ref[part]
        middle = lax.dot_general(x[:, width:], y[:, :width], (((0,), (0,)), ((), ())),
                                 preferred_element_type=jnp.float32).astype(jnp.bfloat16)
        left = jnp.dot(x[:, :width], middle, preferred_element_type=jnp.float32).astype(jnp.bfloat16)
        piece = lax.dot_general(left, y[:, width:], (((1,), (1,)), ((), ())),
                                preferred_element_type=jnp.float32)
        term = piece if term is None else term + piece

    @pl.when(k == 0)
    def _():
        o_ref[...] = t_ref[...].astype(jnp.float32) - term

    @pl.when(k > 0)
    def _():
        o_ref[...] -= term


def trailing_update(full_row, full_col, trailing):
    depth, rows, both = full_row.shape
    cols = full_col.shape[1]
    return pl.pallas_call(
        _update_kernel,
        out_shape=jax.ShapeDtypeStruct((rows, cols), jnp.float32),
        grid=(depth // 4,),
        in_specs=[
            pl.BlockSpec((4, rows, both), lambda k: (k, 0, 0)),
            pl.BlockSpec((4, cols, both), lambda k: (k, 0, 0)),
            pl.BlockSpec((rows, cols), lambda k: (0, 0)),
        ],
        out_specs=pl.BlockSpec((rows, cols), lambda k: (0, 0)),
        compiler_params=pltpu.CompilerParams(
            dimension_semantics=("arbitrary",), vmem_limit_bytes=48 * 1024 * 1024
        ),
    )(full_row, full_col, trailing)


MESH_ID = pl.DeviceIdType.MESH


def _row_exchange_kernel(s_ref, o_ref, sems, own_sem):
    n_row = lax.axis_size("row")
    rows = o_ref.shape[2]
    me = lax.axis_index("row")
    c0 = lax.axis_index("col_0")
    c1 = lax.axis_index("col_1")
    c2 = lax.axis_index("col_2")

    def row_dev(o):
        return (o, c0, c1, c2)

    barrier = pltpu.get_barrier_semaphore()
    for step in range(1, n_row):
        pl.semaphore_signal(barrier, 1, device_id=row_dev(lax.rem(me + step, n_row)),
                            device_id_type=MESH_ID)
    pl.semaphore_wait(barrier, n_row - 1)
    copies = []
    for step in range(1, n_row):
        target = lax.rem(me + step, n_row)
        copies.append(pltpu.make_async_remote_copy(
            src_ref=s_ref.at[:, pl.ds(target * rows, rows)], dst_ref=o_ref.at[:, me],
            send_sem=sems.at[0, step], recv_sem=sems.at[1, step],
            device_id=row_dev(target), device_id_type=MESH_ID))
    for cp in copies:
        cp.start()
    own = pltpu.make_async_copy(s_ref.at[:, pl.ds(me * rows, rows)], o_ref.at[:, me], own_sem.at[0])
    own.start()
    own.wait()
    for cp in copies:
        cp.wait()


def exchange_rows(sent, n_row):
    cap, total, width = sent.shape
    rows = total // n_row
    out = pl.pallas_call(
        _row_exchange_kernel,
        out_shape=jax.ShapeDtypeStruct((cap, n_row, rows, width), sent.dtype),
        in_specs=[pl.BlockSpec(memory_space=pl.ANY)],
        out_specs=pl.BlockSpec(memory_space=pl.ANY),
        scratch_shapes=[pltpu.SemaphoreType.DMA((2, n_row)), pltpu.SemaphoreType.DMA((1,))],
        compiler_params=pltpu.CompilerParams(collective_id=0, has_side_effects=True),
    )(sent)
    return out.reshape(cap, total, width)


COL = ("col_0", "col_1", "col_2")


def cut_along(value, dim, size):
    before, after = (value.shape[:dim], value.shape[dim + 1 :])
    return jnp.moveaxis(value.reshape(*before, size, -1, *after), dim, 0)


def laid_out(tiles, dim):
    tiles = jnp.moveaxis(tiles, 0, dim)
    lengths = tiles.shape
    return tiles.reshape(*lengths[:dim], lengths[dim] * lengths[dim + 1], *lengths[dim + 2 :])


def turned_blocks(tiles, axes, turns):
    inside = tiles.shape[1:]
    result = tiles.reshape(*(lax.axis_size(a) for a in axes), *inside)
    for k in turns:
        result = lax.all_to_all(result, axes[k], k, k, tiled=True)
    return result.reshape(-1, *inside)


def exchange_by_chip(value, groups, turns, split_dim, concat_dim):
    size = lax.axis_size(groups[0]) * lax.axis_size(groups[1])
    tiles = cut_along(value, split_dim, size)
    return laid_out(turned_blocks(tiles, groups, turns), concat_dim)


def piece_ends(length, count):
    unit = 8 if length >= 8 * count else 1
    return [length // unit * k // count * unit for k in range(1, count)]


def cut_exchange(value, axis, pieces, split_dim, concat_dim):
    tiles = cut_along(value, split_dim, lax.axis_size(axis))
    cut = max(range(1, max(2, tiles.ndim - 1)), key=lambda d: tiles.shape[d])
    gathered = []
    for share in jnp.split(tiles, piece_ends(tiles.shape[cut], pieces), axis=cut):
        if share.size:
            gathered.append(lax.all_to_all(share, axis, split_axis=0, concat_axis=0, tiled=True))
    return laid_out(jnp.concatenate(gathered, axis=cut), concat_dim)


def compress_batch(panel_tiles, tile_ranks, sketch_cols):
    keep_cols = jnp.arange(sketch_cols.shape[1])[None, :] < tile_ranks[:, None]
    masked = jnp.where(keep_cols[:, None, :], sketch_cols[None], jnp.zeros_like(sketch_cols)[None])
    sketched = jnp.einsum("bij,bjk->bik", panel_tiles, masked, preferred_element_type=jnp.float32)
    padding = jnp.where(keep_cols, 0.0, 1.0).astype(jnp.float32)
    gram = jnp.einsum("bij,bik->bjk", sketched, sketched, precision=HI)
    gram = gram + padding[:, :, None] * jnp.eye(gram.shape[1], dtype=jnp.float32)[None]
    gram = (gram + jnp.swapaxes(gram, 1, 2)) * 0.5
    inverse = chol_inv(gram)
    basis = jnp.einsum(
        "bij,bkj->bik", sketched, inverse, precision=HI, preferred_element_type=jnp.float32
    ).astype(jnp.bfloat16)
    coeffs = jnp.einsum(
        "bij,bik->bjk", panel_tiles, basis, preferred_element_type=jnp.float32
    ).astype(jnp.bfloat16)
    return jnp.concatenate([basis, coeffs], axis=2)


def slot_numbers(helpers):
    total = helpers.shape[0]
    same_helper = helpers[:, None] == helpers[None, :]
    earlier = jnp.arange(total)[None, :] < jnp.arange(total)[:, None]
    return jnp.sum(jnp.logical_and(same_helper, earlier).astype(jnp.int32), axis=1)


def pack_slabs(slabs, helpers, slots, owners, capacity):
    target = slots * owners + helpers
    hits = jnp.arange(capacity * owners)[:, None] == target[None, :]
    source = jnp.sum(jnp.where(hits, jnp.arange(slabs.shape[0])[None, :], 0), axis=1)
    found = jnp.any(hits, axis=1)
    packed = jnp.where(found[:, None, None], jnp.take(slabs, source, axis=0), jnp.zeros_like(slabs[:1]))
    return packed.reshape(capacity, owners * slabs.shape[1], slabs.shape[2])


def slot_ranks(ranks, helpers, slots, myself, capacity):
    chosen = jnp.logical_and(
        helpers[None, :] == myself, slots[None, :] == jnp.arange(capacity)[:, None]
    )
    return jnp.sum(jnp.where(chosen, ranks[None, :], 0), axis=1)


def pick_mine(returned, helpers, slots, capacity):
    return jnp.take(returned, helpers * capacity + slots, axis=0)


def local(trailing, raw_l, raw_u, sketch, helper_l, helper_u, ranks_l, ranks_u):
    depth = raw_l.shape[1]
    width_r = sketch.shape[3]
    own_sketch = sketch[0, 0]
    compress_all = compress_batch
    col_count = lax.axis_size(COL)
    row_count = lax.axis_size("row")
    cap_row = 2 * depth // col_count
    cap_col = 2 * depth // row_count
    helpers_row = helper_l[0]
    slots_row = slot_numbers(helpers_row)
    sent_row = pack_slabs(raw_l[0], helpers_row, slots_row, col_count, cap_row)
    tiles_row = exchange_by_chip(sent_row, (("col_0", "col_1"), "col_2"), (1, 0), 1, 1)
    made_row = compress_all(
        tiles_row,
        slot_ranks(ranks_l[0], helpers_row, slots_row, lax.axis_index(COL), cap_row),
        own_sketch,
    )
    helpers_col = helper_u[:, 0]
    slots_col = slot_numbers(helpers_col)
    sent_col = pack_slabs(raw_u[:, 0], helpers_col, slots_col, row_count, cap_col)
    tiles_col = exchange_rows(sent_col, row_count)
    made_col = compress_all(
        tiles_col,
        slot_ranks(ranks_u[:, 0], helpers_col, slots_col, lax.axis_index("row"), cap_col),
        own_sketch,
    )
    back_row = lax.all_to_all(made_row, COL, split_axis=1, concat_axis=0, tiled=True)
    full_row = lax.all_gather(
        pick_mine(back_row, helpers_row, slots_row, cap_row), COL, axis=1, tiled=True
    )
    back_col = cut_exchange(made_col, "row", 2, 1, 0)
    full_col = lax.all_gather(
        pick_mine(back_col, helpers_col, slots_col, cap_col), "row", axis=1, tiled=True
    )
    return trailing_update(full_row, full_col, trailing)


def solution(mesh):
    torus = Mesh(
        mesh.devices.reshape(mesh.shape["row"], 2, 4, 2), ("row", "col_0", "col_1", "col_2")
    )
    in_specs = (
        P("row", COL),
        P("row", None, COL, None),
        P(None, COL, "row", None),
        P("row", COL, None, None),
        P("row", None),
        P(None, COL),
        P("row", None),
        P(None, COL),
    )
    out_specs = P("row", COL)
    return jax.shard_map(local, mesh=torus, in_specs=in_specs, out_specs=out_specs, check_vma=False)
```

```python
import jax
import jax.numpy as jnp
from jax import lax
from jax.sharding import Mesh
from jax.sharding import PartitionSpec as P
from jax.experimental import pallas as pl
from jax.experimental.pallas import tpu as pltpu

HI = lax.Precision.HIGHEST


def _eliminate(a, n):
    rows = lax.broadcasted_iota(jnp.int32, (1, n, 1), 1)
    cols = lax.broadcasted_iota(jnp.int32, (1, 1, n), 2)
    ident = jnp.broadcast_to((rows == cols).astype(jnp.float32), a.shape)

    def step(j, carry):
        xa, xb = carry
        at_row = rows == j
        at_col = cols == j
        row_a = jnp.sum(jnp.where(at_row, xa, 0.0), axis=1, keepdims=True)
        row_b = jnp.sum(jnp.where(at_row, xb, 0.0), axis=1, keepdims=True)
        col = jnp.sum(jnp.where(at_col, xa, 0.0), axis=2, keepdims=True)
        pivot = jnp.sum(jnp.where(at_col, row_a, 0.0), axis=2, keepdims=True)
        scale = 1.0 / jnp.sqrt(pivot)
        ra = row_a * scale
        rb = row_b * scale
        mult = jnp.where(rows > j, col * scale, 0.0)
        xa = jnp.where(at_row, ra, xa - mult * ra)
        xb = jnp.where(at_row, rb, xb - mult * rb)
        return xa, xb

    _, xb = lax.fori_loop(0, n, step, (a, ident), unroll=4)
    return xb


def _chol_inv_kernel(g_ref, e_ref):
    count, m, _ = g_ref.shape
    h = 128
    e0 = _eliminate(g_ref[:, :h, :h], h)
    for t in range(count):
        g21 = g_ref[t, h:, :h]
        v = lax.dot_general(g21, e0[t], (((1,), (1,)), ((), ())), precision=HI,
                            preferred_element_type=jnp.float32)
        s = g_ref[t, h:, h:] - lax.dot_general(v, v, (((1,), (1,)), ((), ())), precision=HI,
                                               preferred_element_type=jnp.float32)
        e_ref[t, h:, h:] = s
        e_ref[t, :h, :h] = e0[t]
        e_ref[t, :h, h:] = jnp.zeros((h, m - h), jnp.float32)
        e_ref[t, h:, :h] = jnp.dot(v, e0[t], precision=HI, preferred_element_type=jnp.float32)
    e1 = _eliminate(e_ref[:, h:, h:], m - h)
    for t in range(count):
        e_ref[t, h:, h:] = e1[t]
        e_ref[t, h:, :h] = -jnp.dot(e1[t], e_ref[t, h:, :h], precision=HI,
                                    preferred_element_type=jnp.float32)


def chol_inv(gram):
    return pl.pallas_call(
        _chol_inv_kernel,
        out_shape=jax.ShapeDtypeStruct(gram.shape, jnp.float32),
        in_specs=[pl.BlockSpec(memory_space=pltpu.VMEM)],
        out_specs=pl.BlockSpec(memory_space=pltpu.VMEM),
    )(gram)


def _update_kernel(row_ref, col_ref, t_ref, o_ref):
    k = pl.program_id(0)
    width = row_ref.shape[2] // 2
    term = None
    for part in range(row_ref.shape[0]):
        x = row_ref[part]
        y = col_ref[part]
        middle = lax.dot_general(x[:, width:], y[:, :width], (((0,), (0,)), ((), ())),
                                 preferred_element_type=jnp.float32).astype(jnp.bfloat16)
        left = jnp.dot(x[:, :width], middle, preferred_element_type=jnp.float32).astype(jnp.bfloat16)
        piece = lax.dot_general(left, y[:, width:], (((1,), (1,)), ((), ())),
                                preferred_element_type=jnp.float32)
        term = piece if term is None else term + piece

    @pl.when(k == 0)
    def _():
        o_ref[...] = t_ref[...].astype(jnp.float32) - term

    @pl.when(k > 0)
    def _():
        o_ref[...] -= term


def trailing_update(full_row, full_col, trailing):
    depth, rows, both = full_row.shape
    cols = full_col.shape[1]
    return pl.pallas_call(
        _update_kernel,
        out_shape=jax.ShapeDtypeStruct((rows, cols), jnp.float32),
        grid=(depth // 4,),
        in_specs=[
            pl.BlockSpec((4, rows, both), lambda k: (k, 0, 0)),
            pl.BlockSpec((4, cols, both), lambda k: (k, 0, 0)),
            pl.BlockSpec((rows, cols), lambda k: (0, 0)),
        ],
        out_specs=pl.BlockSpec((rows, cols), lambda k: (0, 0)),
        compiler_params=pltpu.CompilerParams(
            dimension_semantics=("arbitrary",), vmem_limit_bytes=48 * 1024 * 1024
        ),
    )(full_row, full_col, trailing)


MESH_ID = pl.DeviceIdType.MESH


def _row_exchange_kernel(s_ref, o_ref, sems, own_sem):
    n_row = lax.axis_size("row")
    rows = o_ref.shape[2]
    me = lax.axis_index("row")
    c0 = lax.axis_index("col_0")
    c1 = lax.axis_index("col_1")
    c2 = lax.axis_index("col_2")

    def row_dev(o):
        return (o, c0, c1, c2)

    barrier = pltpu.get_barrier_semaphore()
    for step in range(1, n_row):
        pl.semaphore_signal(barrier, 1, device_id=row_dev(lax.rem(me + step, n_row)),
                            device_id_type=MESH_ID)
    pl.semaphore_wait(barrier, n_row - 1)
    copies = []
    for step in range(1, n_row):
        target = lax.rem(me + step, n_row)
        copies.append(pltpu.make_async_remote_copy(
            src_ref=s_ref.at[:, pl.ds(target * rows, rows)], dst_ref=o_ref.at[:, me],
            send_sem=sems.at[0, step], recv_sem=sems.at[1, step],
            device_id=row_dev(target), device_id_type=MESH_ID))
    for cp in copies:
        cp.start()
    own = pltpu.make_async_copy(s_ref.at[:, pl.ds(me * rows, rows)], o_ref.at[:, me], own_sem.at[0])
    own.start()
    own.wait()
    for cp in copies:
        cp.wait()


def exchange_rows(sent, n_row, channel):
    cap, total, width = sent.shape
    rows = total // n_row
    out = pl.pallas_call(
        _row_exchange_kernel,
        out_shape=jax.ShapeDtypeStruct((cap, n_row, rows, width), sent.dtype),
        in_specs=[pl.BlockSpec(memory_space=pl.ANY)],
        out_specs=pl.BlockSpec(memory_space=pl.ANY),
        scratch_shapes=[pltpu.SemaphoreType.DMA((2, n_row)), pltpu.SemaphoreType.DMA((1,))],
        compiler_params=pltpu.CompilerParams(collective_id=channel, has_side_effects=True),
    )(sent)
    return out.reshape(cap, total, width)


COL = ("col_0", "col_1", "col_2")


def cut_along(value, dim, size):
    before, after = (value.shape[:dim], value.shape[dim + 1 :])
    return jnp.moveaxis(value.reshape(*before, size, -1, *after), dim, 0)


def laid_out(tiles, dim):
    tiles = jnp.moveaxis(tiles, 0, dim)
    lengths = tiles.shape
    return tiles.reshape(*lengths[:dim], lengths[dim] * lengths[dim + 1], *lengths[dim + 2 :])


def turned_blocks(tiles, axes, turns):
    inside = tiles.shape[1:]
    result = tiles.reshape(*(lax.axis_size(a) for a in axes), *inside)
    for k in turns:
        result = lax.all_to_all(result, axes[k], k, k, tiled=True)
    return result.reshape(-1, *inside)


def exchange_by_chip(value, groups, turns, split_dim, concat_dim):
    size = lax.axis_size(groups[0]) * lax.axis_size(groups[1])
    tiles = cut_along(value, split_dim, size)
    return laid_out(turned_blocks(tiles, groups, turns), concat_dim)


def piece_ends(length, count):
    unit = 8 if length >= 8 * count else 1
    return [length // unit * k // count * unit for k in range(1, count)]


def cut_exchange(value, axis, pieces, split_dim, concat_dim):
    tiles = cut_along(value, split_dim, lax.axis_size(axis))
    cut = max(range(1, max(2, tiles.ndim - 1)), key=lambda d: tiles.shape[d])
    gathered = []
    for share in jnp.split(tiles, piece_ends(tiles.shape[cut], pieces), axis=cut):
        if share.size:
            gathered.append(lax.all_to_all(share, axis, split_axis=0, concat_axis=0, tiled=True))
    return laid_out(jnp.concatenate(gathered, axis=cut), concat_dim)


def compress_batch(panel_tiles, tile_ranks, sketch_cols):
    keep_cols = jnp.arange(sketch_cols.shape[1])[None, :] < tile_ranks[:, None]
    masked = jnp.where(keep_cols[:, None, :], sketch_cols[None], jnp.zeros_like(sketch_cols)[None])
    sketched = jnp.einsum("bij,bjk->bik", panel_tiles, masked, preferred_element_type=jnp.float32)
    padding = jnp.where(keep_cols, 0.0, 1.0).astype(jnp.float32)
    gram = jnp.einsum("bij,bik->bjk", sketched, sketched, precision=HI)
    gram = gram + padding[:, :, None] * jnp.eye(gram.shape[1], dtype=jnp.float32)[None]
    gram = (gram + jnp.swapaxes(gram, 1, 2)) * 0.5
    inverse = chol_inv(gram)
    basis = jnp.einsum(
        "bij,bkj->bik", sketched, inverse, precision=HI, preferred_element_type=jnp.float32
    ).astype(jnp.bfloat16)
    coeffs = jnp.einsum(
        "bij,bik->bjk", panel_tiles, basis, preferred_element_type=jnp.float32
    ).astype(jnp.bfloat16)
    return jnp.concatenate([basis, coeffs], axis=2)


def slot_numbers(helpers):
    total = helpers.shape[0]
    same_helper = helpers[:, None] == helpers[None, :]
    earlier = jnp.arange(total)[None, :] < jnp.arange(total)[:, None]
    return jnp.sum(jnp.logical_and(same_helper, earlier).astype(jnp.int32), axis=1)


def pack_slabs(slabs, helpers, slots, owners, capacity):
    target = slots * owners + helpers
    hits = jnp.arange(capacity * owners)[:, None] == target[None, :]
    source = jnp.sum(jnp.where(hits, jnp.arange(slabs.shape[0])[None, :], 0), axis=1)
    found = jnp.any(hits, axis=1)
    packed = jnp.where(found[:, None, None], jnp.take(slabs, source, axis=0), jnp.zeros_like(slabs[:1]))
    return packed.reshape(capacity, owners * slabs.shape[1], slabs.shape[2])


def slot_ranks(ranks, helpers, slots, myself, capacity):
    chosen = jnp.logical_and(
        helpers[None, :] == myself, slots[None, :] == jnp.arange(capacity)[:, None]
    )
    return jnp.sum(jnp.where(chosen, ranks[None, :], 0), axis=1)


def pick_mine(returned, helpers, slots, capacity):
    return jnp.take(returned, helpers * capacity + slots, axis=0)


def local(trailing, raw_l, raw_u, sketch, helper_l, helper_u, ranks_l, ranks_u):
    depth = raw_l.shape[1]
    width_r = sketch.shape[3]
    own_sketch = sketch[0, 0]
    compress_all = compress_batch
    col_count = lax.axis_size(COL)
    row_count = lax.axis_size("row")
    cap_row = 2 * depth // col_count
    cap_col = 2 * depth // row_count
    helpers_row = helper_l[0]
    slots_row = slot_numbers(helpers_row)
    sent_row = pack_slabs(raw_l[0], helpers_row, slots_row, col_count, cap_row)
    tiles_row = exchange_by_chip(sent_row, (("col_0", "col_1"), "col_2"), (1, 0), 1, 1)
    made_row = compress_all(
        tiles_row,
        slot_ranks(ranks_l[0], helpers_row, slots_row, lax.axis_index(COL), cap_row),
        own_sketch,
    )
    helpers_col = helper_u[:, 0]
    slots_col = slot_numbers(helpers_col)
    sent_col = pack_slabs(raw_u[:, 0], helpers_col, slots_col, row_count, cap_col)
    tiles_col = exchange_rows(sent_col, row_count, 0)
    made_col = compress_all(
        tiles_col,
        slot_ranks(ranks_u[:, 0], helpers_col, slots_col, lax.axis_index("row"), cap_col),
        own_sketch,
    )
    back_row = lax.all_to_all(made_row, COL, split_axis=1, concat_axis=0, tiled=True)
    full_row = lax.all_gather(
        pick_mine(back_row, helpers_row, slots_row, cap_row), COL, axis=1, tiled=True
    )
    back_col = exchange_rows(made_col, row_count, 1).reshape(
        cap_col * row_count, -1, made_col.shape[2]
    )
    mine_col = jnp.take(back_col, slots_col * row_count + helpers_col, axis=0)
    full_col = lax.all_gather(mine_col, "row", axis=1, tiled=True)
    return trailing_update(full_row, full_col, trailing)


def solution(mesh):
    torus = Mesh(
        mesh.devices.reshape(mesh.shape["row"], 2, 4, 2), ("row", "col_0", "col_1", "col_2")
    )
    in_specs = (
        P("row", COL),
        P("row", None, COL, None),
        P(None, COL, "row", None),
        P("row", COL, None, None),
        P("row", None),
        P(None, COL),
        P("row", None),
        P(None, COL),
    )
    out_specs = P("row", COL)
    return jax.shard_map(local, mesh=torus, in_specs=in_specs, out_specs=out_specs, check_vma=False)
```

```python
import jax
import jax.numpy as jnp
from jax import lax
from jax.sharding import Mesh
from jax.sharding import PartitionSpec as P
from jax.experimental import pallas as pl
from jax.experimental.pallas import tpu as pltpu

HI = lax.Precision.HIGHEST


def _eliminate(a, n):
    rows = lax.broadcasted_iota(jnp.int32, (1, n, 1), 1)
    cols = lax.broadcasted_iota(jnp.int32, (1, 1, n), 2)
    ident = jnp.broadcast_to((rows == cols).astype(jnp.float32), a.shape)

    def step(j, carry):
        xa, xb = carry
        at_row = rows == j
        at_col = cols == j
        row_a = jnp.sum(jnp.where(at_row, xa, 0.0), axis=1, keepdims=True)
        row_b = jnp.sum(jnp.where(at_row, xb, 0.0), axis=1, keepdims=True)
        col = jnp.sum(jnp.where(at_col, xa, 0.0), axis=2, keepdims=True)
        pivot = jnp.sum(jnp.where(at_col, row_a, 0.0), axis=2, keepdims=True)
        scale = 1.0 / jnp.sqrt(pivot)
        ra = row_a * scale
        rb = row_b * scale
        mult = jnp.where(rows > j, col * scale, 0.0)
        xa = jnp.where(at_row, ra, xa - mult * ra)
        xb = jnp.where(at_row, rb, xb - mult * rb)
        return xa, xb

    _, xb = lax.fori_loop(0, n, step, (a, ident), unroll=4)
    return xb


def _chol_inv_kernel(g_ref, e_ref):
    count, m, _ = g_ref.shape
    h = 128
    e0 = _eliminate(g_ref[:, :h, :h], h)
    for t in range(count):
        g21 = g_ref[t, h:, :h]
        v = lax.dot_general(g21, e0[t], (((1,), (1,)), ((), ())), precision=HI,
                            preferred_element_type=jnp.float32)
        s = g_ref[t, h:, h:] - lax.dot_general(v, v, (((1,), (1,)), ((), ())), precision=HI,
                                               preferred_element_type=jnp.float32)
        e_ref[t, h:, h:] = s
        e_ref[t, :h, :h] = e0[t]
        e_ref[t, :h, h:] = jnp.zeros((h, m - h), jnp.float32)
        e_ref[t, h:, :h] = jnp.dot(v, e0[t], precision=HI, preferred_element_type=jnp.float32)
    e1 = _eliminate(e_ref[:, h:, h:], m - h)
    for t in range(count):
        e_ref[t, h:, h:] = e1[t]
        e_ref[t, h:, :h] = -jnp.dot(e1[t], e_ref[t, h:, :h], precision=HI,
                                    preferred_element_type=jnp.float32)


def chol_inv(gram):
    return pl.pallas_call(
        _chol_inv_kernel,
        out_shape=jax.ShapeDtypeStruct(gram.shape, jnp.float32),
        in_specs=[pl.BlockSpec(memory_space=pltpu.VMEM)],
        out_specs=pl.BlockSpec(memory_space=pltpu.VMEM),
    )(gram)


def _update_kernel(row_ref, col_ref, t_ref, o_ref):
    k = pl.program_id(0)
    width = row_ref.shape[2] // 2
    term = None
    for part in range(row_ref.shape[0]):
        x = row_ref[part]
        y = col_ref[part]
        middle = lax.dot_general(x[:, width:], y[:, :width], (((0,), (0,)), ((), ())),
                                 preferred_element_type=jnp.float32).astype(jnp.bfloat16)
        left = jnp.dot(x[:, :width], middle, preferred_element_type=jnp.float32).astype(jnp.bfloat16)
        piece = lax.dot_general(left, y[:, width:], (((1,), (1,)), ((), ())),
                                preferred_element_type=jnp.float32)
        term = piece if term is None else term + piece

    @pl.when(k == 0)
    def _():
        o_ref[...] = t_ref[...].astype(jnp.float32) - term

    @pl.when(k > 0)
    def _():
        o_ref[...] -= term


def trailing_update(full_row, full_col, trailing):
    depth, rows, both = full_row.shape
    cols = full_col.shape[1]
    return pl.pallas_call(
        _update_kernel,
        out_shape=jax.ShapeDtypeStruct((rows, cols), jnp.float32),
        grid=(depth // 4,),
        in_specs=[
            pl.BlockSpec((4, rows, both), lambda k: (k, 0, 0)),
            pl.BlockSpec((4, cols, both), lambda k: (k, 0, 0)),
            pl.BlockSpec((rows, cols), lambda k: (0, 0)),
        ],
        out_specs=pl.BlockSpec((rows, cols), lambda k: (0, 0)),
        compiler_params=pltpu.CompilerParams(
            dimension_semantics=("arbitrary",), vmem_limit_bytes=48 * 1024 * 1024
        ),
    )(full_row, full_col, trailing)


MESH_ID = pl.DeviceIdType.MESH


def _row_exchange_kernel(s_ref, o_ref, sems, own_sem):
    n_row = lax.axis_size("row")
    rows = o_ref.shape[2]
    me = lax.axis_index("row")
    c0 = lax.axis_index("col_0")
    c1 = lax.axis_index("col_1")
    c2 = lax.axis_index("col_2")

    def row_dev(o):
        return (o, c0, c1, c2)

    barrier = pltpu.get_barrier_semaphore()
    for step in range(1, n_row):
        pl.semaphore_signal(barrier, 1, device_id=row_dev(lax.rem(me + step, n_row)),
                            device_id_type=MESH_ID)
    pl.semaphore_wait(barrier, n_row - 1)
    copies = []
    for step in range(1, n_row):
        target = lax.rem(me + step, n_row)
        copies.append(pltpu.make_async_remote_copy(
            src_ref=s_ref.at[:, pl.ds(target * rows, rows)], dst_ref=o_ref.at[:, me],
            send_sem=sems.at[0, step], recv_sem=sems.at[1, step],
            device_id=row_dev(target), device_id_type=MESH_ID))
    for cp in copies:
        cp.start()
    own = pltpu.make_async_copy(s_ref.at[:, pl.ds(me * rows, rows)], o_ref.at[:, me], own_sem.at[0])
    own.start()
    own.wait()
    for cp in copies:
        cp.wait()


def exchange_rows(sent, n_row, channel):
    cap, total, width = sent.shape
    rows = total // n_row
    out = pl.pallas_call(
        _row_exchange_kernel,
        out_shape=jax.ShapeDtypeStruct((cap, n_row, rows, width), sent.dtype),
        in_specs=[pl.BlockSpec(memory_space=pl.ANY)],
        out_specs=pl.BlockSpec(memory_space=pl.ANY),
        scratch_shapes=[pltpu.SemaphoreType.DMA((2, n_row)), pltpu.SemaphoreType.DMA((1,))],
        compiler_params=pltpu.CompilerParams(collective_id=channel, has_side_effects=True),
    )(sent)
    return out.reshape(cap, total, width)


def _col_exchange_kernel(s_ref, o_ref, sems, own_sem):
    n1 = lax.axis_size("col_1")
    n2 = lax.axis_size("col_2")
    n_col = lax.axis_size("col_0") * n1 * n2
    rows = o_ref.shape[2]
    me_r = lax.axis_index("row")
    me = (lax.axis_index("col_0") * n1 + lax.axis_index("col_1")) * n2 + lax.axis_index("col_2")

    def col_dev(d):
        return (me_r, d // (n1 * n2), (d // n2) % n1, d % n2)

    barrier = pltpu.get_barrier_semaphore()
    for step in range(1, n_col):
        pl.semaphore_signal(barrier, 1, device_id=col_dev(lax.rem(me + step, n_col)),
                            device_id_type=MESH_ID)
    pl.semaphore_wait(barrier, n_col - 1)
    copies = []
    for step in range(1, n_col):
        target = lax.rem(me + step, n_col)
        copies.append(pltpu.make_async_remote_copy(
            src_ref=s_ref.at[:, pl.ds(target * rows, rows)], dst_ref=o_ref.at[:, me],
            send_sem=sems.at[0, step], recv_sem=sems.at[1, step],
            device_id=col_dev(target), device_id_type=MESH_ID))
    for cp in copies:
        cp.start()
    own = pltpu.make_async_copy(s_ref.at[:, pl.ds(me * rows, rows)], o_ref.at[:, me], own_sem.at[0])
    own.start()
    own.wait()
    for cp in copies:
        cp.wait()


def exchange_cols(sent, n_col, channel):
    cap, total, width = sent.shape
    rows = total // n_col
    out = pl.pallas_call(
        _col_exchange_kernel,
        out_shape=jax.ShapeDtypeStruct((cap, n_col, rows, width), sent.dtype),
        in_specs=[pl.BlockSpec(memory_space=pl.ANY)],
        out_specs=pl.BlockSpec(memory_space=pl.ANY),
        scratch_shapes=[pltpu.SemaphoreType.DMA((2, n_col)), pltpu.SemaphoreType.DMA((1,))],
        compiler_params=pltpu.CompilerParams(collective_id=channel, has_side_effects=True),
    )(sent)
    return out.reshape(cap, total, width)


COL = ("col_0", "col_1", "col_2")


def cut_along(value, dim, size):
    before, after = (value.shape[:dim], value.shape[dim + 1 :])
    return jnp.moveaxis(value.reshape(*before, size, -1, *after), dim, 0)


def laid_out(tiles, dim):
    tiles = jnp.moveaxis(tiles, 0, dim)
    lengths = tiles.shape
    return tiles.reshape(*lengths[:dim], lengths[dim] * lengths[dim + 1], *lengths[dim + 2 :])


def turned_blocks(tiles, axes, turns):
    inside = tiles.shape[1:]
    result = tiles.reshape(*(lax.axis_size(a) for a in axes), *inside)
    for k in turns:
        result = lax.all_to_all(result, axes[k], k, k, tiled=True)
    return result.reshape(-1, *inside)


def exchange_by_chip(value, groups, turns, split_dim, concat_dim):
    size = lax.axis_size(groups[0]) * lax.axis_size(groups[1])
    tiles = cut_along(value, split_dim, size)
    return laid_out(turned_blocks(tiles, groups, turns), concat_dim)


def piece_ends(length, count):
    unit = 8 if length >= 8 * count else 1
    return [length // unit * k // count * unit for k in range(1, count)]


def cut_exchange(value, axis, pieces, split_dim, concat_dim):
    tiles = cut_along(value, split_dim, lax.axis_size(axis))
    cut = max(range(1, max(2, tiles.ndim - 1)), key=lambda d: tiles.shape[d])
    gathered = []
    for share in jnp.split(tiles, piece_ends(tiles.shape[cut], pieces), axis=cut):
        if share.size:
            gathered.append(lax.all_to_all(share, axis, split_axis=0, concat_axis=0, tiled=True))
    return laid_out(jnp.concatenate(gathered, axis=cut), concat_dim)


def compress_batch(panel_tiles, tile_ranks, sketch_cols):
    keep_cols = jnp.arange(sketch_cols.shape[1])[None, :] < tile_ranks[:, None]
    masked = jnp.where(keep_cols[:, None, :], sketch_cols[None], jnp.zeros_like(sketch_cols)[None])
    sketched = jnp.einsum("bij,bjk->bik", panel_tiles, masked, preferred_element_type=jnp.float32)
    padding = jnp.where(keep_cols, 0.0, 1.0).astype(jnp.float32)
    gram = jnp.einsum("bij,bik->bjk", sketched, sketched, precision=HI)
    gram = gram + padding[:, :, None] * jnp.eye(gram.shape[1], dtype=jnp.float32)[None]
    gram = (gram + jnp.swapaxes(gram, 1, 2)) * 0.5
    inverse = chol_inv(gram)
    basis = jnp.einsum(
        "bij,bkj->bik", sketched, inverse, precision=HI, preferred_element_type=jnp.float32
    ).astype(jnp.bfloat16)
    coeffs = jnp.einsum(
        "bij,bik->bjk", panel_tiles, basis, preferred_element_type=jnp.float32
    ).astype(jnp.bfloat16)
    return jnp.concatenate([basis, coeffs], axis=2)


def slot_numbers(helpers):
    total = helpers.shape[0]
    same_helper = helpers[:, None] == helpers[None, :]
    earlier = jnp.arange(total)[None, :] < jnp.arange(total)[:, None]
    return jnp.sum(jnp.logical_and(same_helper, earlier).astype(jnp.int32), axis=1)


def pack_slabs(slabs, helpers, slots, owners, capacity):
    target = slots * owners + helpers
    hits = jnp.arange(capacity * owners)[:, None] == target[None, :]
    source = jnp.sum(jnp.where(hits, jnp.arange(slabs.shape[0])[None, :], 0), axis=1)
    found = jnp.any(hits, axis=1)
    packed = jnp.where(found[:, None, None], jnp.take(slabs, source, axis=0), jnp.zeros_like(slabs[:1]))
    return packed.reshape(capacity, owners * slabs.shape[1], slabs.shape[2])


def slot_ranks(ranks, helpers, slots, myself, capacity):
    chosen = jnp.logical_and(
        helpers[None, :] == myself, slots[None, :] == jnp.arange(capacity)[:, None]
    )
    return jnp.sum(jnp.where(chosen, ranks[None, :], 0), axis=1)


def pick_mine(returned, helpers, slots, capacity):
    return jnp.take(returned, helpers * capacity + slots, axis=0)


def local(trailing, raw_l, raw_u, sketch, helper_l, helper_u, ranks_l, ranks_u):
    depth = raw_l.shape[1]
    width_r = sketch.shape[3]
    own_sketch = sketch[0, 0]
    compress_all = compress_batch
    col_count = lax.axis_size(COL)
    row_count = lax.axis_size("row")
    cap_row = 2 * depth // col_count
    cap_col = 2 * depth // row_count
    helpers_row = helper_l[0]
    slots_row = slot_numbers(helpers_row)
    sent_row = pack_slabs(raw_l[0], helpers_row, slots_row, col_count, cap_row)
    tiles_row = exchange_cols(sent_row, col_count, 2)
    made_row = compress_all(
        tiles_row,
        slot_ranks(ranks_l[0], helpers_row, slots_row, lax.axis_index(COL), cap_row),
        own_sketch,
    )
    helpers_col = helper_u[:, 0]
    slots_col = slot_numbers(helpers_col)
    sent_col = pack_slabs(raw_u[:, 0], helpers_col, slots_col, row_count, cap_col)
    tiles_col = exchange_rows(sent_col, row_count, 0)
    made_col = compress_all(
        tiles_col,
        slot_ranks(ranks_u[:, 0], helpers_col, slots_col, lax.axis_index("row"), cap_col),
        own_sketch,
    )
    back_row = exchange_cols(made_row, col_count, 3).reshape(
        cap_row * col_count, -1, made_row.shape[2]
    )
    mine_row = jnp.take(back_row, slots_row * col_count + helpers_row, axis=0)
    full_row = lax.all_gather(mine_row, COL, axis=1, tiled=True)
    back_col = exchange_rows(made_col, row_count, 1).reshape(
        cap_col * row_count, -1, made_col.shape[2]
    )
    mine_col = jnp.take(back_col, slots_col * row_count + helpers_col, axis=0)
    full_col = lax.all_gather(mine_col, "row", axis=1, tiled=True)
    return trailing_update(full_row, full_col, trailing)


def solution(mesh):
    torus = Mesh(
        mesh.devices.reshape(mesh.shape["row"], 2, 4, 2), ("row", "col_0", "col_1", "col_2")
    )
    in_specs = (
        P("row", COL),
        P("row", None, COL, None),
        P(None, COL, "row", None),
        P("row", COL, None, None),
        P("row", None),
        P(None, COL),
        P("row", None),
        P(None, COL),
    )
    out_specs = P("row", COL)
    return jax.shard_map(local, mesh=torus, in_specs=in_specs, out_specs=out_specs, check_vma=False)
```

```python
import jax
import jax.numpy as jnp
from jax import lax
from jax.sharding import Mesh
from jax.sharding import PartitionSpec as P
from jax.experimental import pallas as pl
from jax.experimental.pallas import tpu as pltpu

HI = lax.Precision.HIGHEST


def _eliminate(a, n):
    rows = lax.broadcasted_iota(jnp.int32, (1, n, 1), 1)
    cols = lax.broadcasted_iota(jnp.int32, (1, 1, n), 2)
    ident = jnp.broadcast_to((rows == cols).astype(jnp.float32), a.shape)

    def step(j, carry):
        xa, xb = carry
        at_row = rows == j
        at_col = cols == j
        row_a = jnp.sum(jnp.where(at_row, xa, 0.0), axis=1, keepdims=True)
        row_b = jnp.sum(jnp.where(at_row, xb, 0.0), axis=1, keepdims=True)
        col = jnp.sum(jnp.where(at_col, xa, 0.0), axis=2, keepdims=True)
        pivot = jnp.sum(jnp.where(at_col, row_a, 0.0), axis=2, keepdims=True)
        scale = 1.0 / jnp.sqrt(pivot)
        ra = row_a * scale
        rb = row_b * scale
        mult = jnp.where(rows > j, col * scale, 0.0)
        xa = jnp.where(at_row, ra, xa - mult * ra)
        xb = jnp.where(at_row, rb, xb - mult * rb)
        return xa, xb

    _, xb = lax.fori_loop(0, n, step, (a, ident), unroll=4)
    return xb


def _chol_inv_kernel(g_ref, e_ref):
    count, m, _ = g_ref.shape
    h = 128
    e0 = _eliminate(g_ref[:, :h, :h], h)
    for t in range(count):
        g21 = g_ref[t, h:, :h]
        v = lax.dot_general(g21, e0[t], (((1,), (1,)), ((), ())), precision=HI,
                            preferred_element_type=jnp.float32)
        s = g_ref[t, h:, h:] - lax.dot_general(v, v, (((1,), (1,)), ((), ())), precision=HI,
                                               preferred_element_type=jnp.float32)
        e_ref[t, h:, h:] = s
        e_ref[t, :h, :h] = e0[t]
        e_ref[t, :h, h:] = jnp.zeros((h, m - h), jnp.float32)
        e_ref[t, h:, :h] = jnp.dot(v, e0[t], precision=HI, preferred_element_type=jnp.float32)
    e1 = _eliminate(e_ref[:, h:, h:], m - h)
    for t in range(count):
        e_ref[t, h:, h:] = e1[t]
        e_ref[t, h:, :h] = -jnp.dot(e1[t], e_ref[t, h:, :h], precision=HI,
                                    preferred_element_type=jnp.float32)


def chol_inv(gram):
    return pl.pallas_call(
        _chol_inv_kernel,
        out_shape=jax.ShapeDtypeStruct(gram.shape, jnp.float32),
        in_specs=[pl.BlockSpec(memory_space=pltpu.VMEM)],
        out_specs=pl.BlockSpec(memory_space=pltpu.VMEM),
    )(gram)


def _update_kernel(row_ref, col_ref, t_ref, o_ref):
    k = pl.program_id(0)
    width = row_ref.shape[2] // 2
    term = None
    for part in range(row_ref.shape[0]):
        x = row_ref[part]
        y = col_ref[part]
        middle = lax.dot_general(x[:, width:], y[:, :width], (((0,), (0,)), ((), ())),
                                 preferred_element_type=jnp.float32).astype(jnp.bfloat16)
        left = jnp.dot(x[:, :width], middle, preferred_element_type=jnp.float32).astype(jnp.bfloat16)
        piece = lax.dot_general(left, y[:, width:], (((1,), (1,)), ((), ())),
                                preferred_element_type=jnp.float32)
        term = piece if term is None else term + piece

    @pl.when(k == 0)
    def _():
        o_ref[...] = t_ref[...].astype(jnp.float32) - term

    @pl.when(k > 0)
    def _():
        o_ref[...] -= term


def trailing_update(full_row, full_col, trailing):
    depth, rows, both = full_row.shape
    cols = full_col.shape[1]
    return pl.pallas_call(
        _update_kernel,
        out_shape=jax.ShapeDtypeStruct((rows, cols), jnp.float32),
        grid=(depth // 4,),
        in_specs=[
            pl.BlockSpec((4, rows, both), lambda k: (k, 0, 0)),
            pl.BlockSpec((4, cols, both), lambda k: (k, 0, 0)),
            pl.BlockSpec((rows, cols), lambda k: (0, 0)),
        ],
        out_specs=pl.BlockSpec((rows, cols), lambda k: (0, 0)),
        compiler_params=pltpu.CompilerParams(
            dimension_semantics=("arbitrary",), vmem_limit_bytes=48 * 1024 * 1024
        ),
    )(full_row, full_col, trailing)


MESH_ID = pl.DeviceIdType.MESH


def _row_exchange_kernel(s_ref, o_ref, sems, own_sem):
    n_row = lax.axis_size("row")
    rows = o_ref.shape[2]
    me = lax.axis_index("row")
    c0 = lax.axis_index("col_0")
    c1 = lax.axis_index("col_1")
    c2 = lax.axis_index("col_2")

    def row_dev(o):
        return (o, c0, c1, c2)

    barrier = pltpu.get_barrier_semaphore()
    for step in range(1, n_row):
        pl.semaphore_signal(barrier, 1, device_id=row_dev(lax.rem(me + step, n_row)),
                            device_id_type=MESH_ID)
    pl.semaphore_wait(barrier, n_row - 1)
    copies = []
    for step in range(1, n_row):
        target = lax.rem(me + step, n_row)
        copies.append(pltpu.make_async_remote_copy(
            src_ref=s_ref.at[:, pl.ds(target * rows, rows)], dst_ref=o_ref.at[:, me],
            send_sem=sems.at[0, step], recv_sem=sems.at[1, step],
            device_id=row_dev(target), device_id_type=MESH_ID))
    for cp in copies:
        cp.start()
    own = pltpu.make_async_copy(s_ref.at[:, pl.ds(me * rows, rows)], o_ref.at[:, me], own_sem.at[0])
    own.start()
    own.wait()
    for cp in copies:
        cp.wait()


def exchange_rows(sent, n_row, channel):
    cap, total, width = sent.shape
    rows = total // n_row
    out = pl.pallas_call(
        _row_exchange_kernel,
        out_shape=jax.ShapeDtypeStruct((cap, n_row, rows, width), sent.dtype),
        in_specs=[pl.BlockSpec(memory_space=pl.ANY)],
        out_specs=pl.BlockSpec(memory_space=pl.ANY),
        scratch_shapes=[pltpu.SemaphoreType.DMA((2, n_row)), pltpu.SemaphoreType.DMA((1,))],
        compiler_params=pltpu.CompilerParams(collective_id=channel, has_side_effects=True),
    )(sent)
    return out.reshape(cap, total, width)


COL = ("col_0", "col_1", "col_2")


def cut_along(value, dim, size):
    before, after = (value.shape[:dim], value.shape[dim + 1 :])
    return jnp.moveaxis(value.reshape(*before, size, -1, *after), dim, 0)


def laid_out(tiles, dim):
    tiles = jnp.moveaxis(tiles, 0, dim)
    lengths = tiles.shape
    return tiles.reshape(*lengths[:dim], lengths[dim] * lengths[dim + 1], *lengths[dim + 2 :])


def turned_blocks(tiles, axes, turns):
    inside = tiles.shape[1:]
    result = tiles.reshape(*(lax.axis_size(a) for a in axes), *inside)
    for k in turns:
        result = lax.all_to_all(result, axes[k], k, k, tiled=True)
    return result.reshape(-1, *inside)


def exchange_by_chip(value, groups, turns, split_dim, concat_dim):
    size = lax.axis_size(groups[0]) * lax.axis_size(groups[1])
    tiles = cut_along(value, split_dim, size)
    return laid_out(turned_blocks(tiles, groups, turns), concat_dim)


def piece_ends(length, count):
    unit = 8 if length >= 8 * count else 1
    return [length // unit * k // count * unit for k in range(1, count)]


def cut_exchange(value, axis, pieces, split_dim, concat_dim):
    tiles = cut_along(value, split_dim, lax.axis_size(axis))
    cut = max(range(1, max(2, tiles.ndim - 1)), key=lambda d: tiles.shape[d])
    gathered = []
    for share in jnp.split(tiles, piece_ends(tiles.shape[cut], pieces), axis=cut):
        if share.size:
            gathered.append(lax.all_to_all(share, axis, split_axis=0, concat_axis=0, tiled=True))
    return laid_out(jnp.concatenate(gathered, axis=cut), concat_dim)


def compress_batch(panel_tiles, tile_ranks, sketch_cols):
    keep_cols = jnp.arange(sketch_cols.shape[1])[None, :] < tile_ranks[:, None]
    masked = jnp.where(keep_cols[:, None, :], sketch_cols[None], jnp.zeros_like(sketch_cols)[None])
    sketched = jnp.einsum("bij,bjk->bik", panel_tiles, masked, preferred_element_type=jnp.float32)
    padding = jnp.where(keep_cols, 0.0, 1.0).astype(jnp.float32)
    gram = jnp.einsum("bij,bik->bjk", sketched, sketched, precision=lax.Precision.HIGH)
    gram = gram + padding[:, :, None] * jnp.eye(gram.shape[1], dtype=jnp.float32)[None]
    gram = (gram + jnp.swapaxes(gram, 1, 2)) * 0.5
    inverse = chol_inv(gram)
    basis = jnp.einsum(
        "bij,bkj->bik", sketched, inverse, precision=lax.Precision.HIGH,
        preferred_element_type=jnp.float32,
    ).astype(jnp.bfloat16)
    coeffs = jnp.einsum(
        "bij,bik->bjk", panel_tiles, basis, preferred_element_type=jnp.float32
    ).astype(jnp.bfloat16)
    return jnp.concatenate([basis, coeffs], axis=2)


def slot_numbers(helpers):
    total = helpers.shape[0]
    same_helper = helpers[:, None] == helpers[None, :]
    earlier = jnp.arange(total)[None, :] < jnp.arange(total)[:, None]
    return jnp.sum(jnp.logical_and(same_helper, earlier).astype(jnp.int32), axis=1)


def pack_slabs(slabs, helpers, slots, owners, capacity):
    target = slots * owners + helpers
    hits = jnp.arange(capacity * owners)[:, None] == target[None, :]
    source = jnp.sum(jnp.where(hits, jnp.arange(slabs.shape[0])[None, :], 0), axis=1)
    found = jnp.any(hits, axis=1)
    packed = jnp.where(found[:, None, None], jnp.take(slabs, source, axis=0), jnp.zeros_like(slabs[:1]))
    return packed.reshape(capacity, owners * slabs.shape[1], slabs.shape[2])


def slot_ranks(ranks, helpers, slots, myself, capacity):
    chosen = jnp.logical_and(
        helpers[None, :] == myself, slots[None, :] == jnp.arange(capacity)[:, None]
    )
    return jnp.sum(jnp.where(chosen, ranks[None, :], 0), axis=1)


def pick_mine(returned, helpers, slots, capacity):
    return jnp.take(returned, helpers * capacity + slots, axis=0)


def local(trailing, raw_l, raw_u, sketch, helper_l, helper_u, ranks_l, ranks_u):
    depth = raw_l.shape[1]
    width_r = sketch.shape[3]
    own_sketch = sketch[0, 0]
    compress_all = compress_batch
    col_count = lax.axis_size(COL)
    row_count = lax.axis_size("row")
    cap_row = 2 * depth // col_count
    cap_col = 2 * depth // row_count
    helpers_row = helper_l[0]
    slots_row = slot_numbers(helpers_row)
    sent_row = pack_slabs(raw_l[0], helpers_row, slots_row, col_count, cap_row)
    tiles_row = exchange_by_chip(sent_row, (("col_0", "col_1"), "col_2"), (1, 0), 1, 1)
    made_row = compress_all(
        tiles_row,
        slot_ranks(ranks_l[0], helpers_row, slots_row, lax.axis_index(COL), cap_row),
        own_sketch,
    )
    helpers_col = helper_u[:, 0]
    slots_col = slot_numbers(helpers_col)
    sent_col = pack_slabs(raw_u[:, 0], helpers_col, slots_col, row_count, cap_col)
    tiles_col = exchange_rows(sent_col, row_count, 0)
    made_col = compress_all(
        tiles_col,
        slot_ranks(ranks_u[:, 0], helpers_col, slots_col, lax.axis_index("row"), cap_col),
        own_sketch,
    )
    back_row = lax.all_to_all(made_row, COL, split_axis=1, concat_axis=0, tiled=True)
    full_row = lax.all_gather(
        pick_mine(back_row, helpers_row, slots_row, cap_row), COL, axis=1, tiled=True
    )
    back_col = exchange_rows(made_col, row_count, 1).reshape(
        cap_col * row_count, -1, made_col.shape[2]
    )
    mine_col = jnp.take(back_col, slots_col * row_count + helpers_col, axis=0)
    full_col = lax.all_gather(mine_col, "row", axis=1, tiled=True)
    return trailing_update(full_row, full_col, trailing)


def solution(mesh):
    torus = Mesh(
        mesh.devices.reshape(mesh.shape["row"], 2, 4, 2), ("row", "col_0", "col_1", "col_2")
    )
    in_specs = (
        P("row", COL),
        P("row", None, COL, None),
        P(None, COL, "row", None),
        P("row", COL, None, None),
        P("row", None),
        P(None, COL),
        P("row", None),
        P(None, COL),
    )
    out_specs = P("row", COL)
    return jax.shard_map(local, mesh=torus, in_specs=in_specs, out_specs=out_specs, check_vma=False)
```

```python
import jax
import jax.numpy as jnp
from jax import lax
from jax.sharding import Mesh
from jax.sharding import PartitionSpec as P
from jax.experimental import pallas as pl
from jax.experimental.pallas import tpu as pltpu

HI = lax.Precision.HIGHEST


def _eliminate(a, n):
    rows = lax.broadcasted_iota(jnp.int32, (1, n, 1), 1)
    cols = lax.broadcasted_iota(jnp.int32, (1, 1, n), 2)
    ident = jnp.broadcast_to((rows == cols).astype(jnp.float32), a.shape)

    def step(j, carry):
        xa, xb = carry
        at_row = rows == j
        at_col = cols == j
        row_a = jnp.sum(jnp.where(at_row, xa, 0.0), axis=1, keepdims=True)
        row_b = jnp.sum(jnp.where(at_row, xb, 0.0), axis=1, keepdims=True)
        col = jnp.sum(jnp.where(at_col, xa, 0.0), axis=2, keepdims=True)
        pivot = jnp.sum(jnp.where(at_col, row_a, 0.0), axis=2, keepdims=True)
        scale = 1.0 / jnp.sqrt(pivot)
        ra = row_a * scale
        rb = row_b * scale
        mult = jnp.where(rows > j, col * scale, 0.0)
        xa = jnp.where(at_row, ra, xa - mult * ra)
        xb = jnp.where(at_row, rb, xb - mult * rb)
        return xa, xb

    _, xb = lax.fori_loop(0, n, step, (a, ident), unroll=8 if a.shape[0] >= 4 else 4)
    return xb


def _chol_inv_kernel(g_ref, e_ref):
    count, m, _ = g_ref.shape
    h = 128
    e0 = _eliminate(g_ref[:, :h, :h], h)
    for t in range(count):
        g21 = g_ref[t, h:, :h]
        v = lax.dot_general(g21, e0[t], (((1,), (1,)), ((), ())), precision=HI,
                            preferred_element_type=jnp.float32)
        s = g_ref[t, h:, h:] - lax.dot_general(v, v, (((1,), (1,)), ((), ())), precision=HI,
                                               preferred_element_type=jnp.float32)
        e_ref[t, h:, h:] = s
        e_ref[t, :h, :h] = e0[t]
        e_ref[t, :h, h:] = jnp.zeros((h, m - h), jnp.float32)
        e_ref[t, h:, :h] = jnp.dot(v, e0[t], precision=HI, preferred_element_type=jnp.float32)
    e1 = _eliminate(e_ref[:, h:, h:], m - h)
    for t in range(count):
        e_ref[t, h:, h:] = e1[t]
        e_ref[t, h:, :h] = -jnp.dot(e1[t], e_ref[t, h:, :h], precision=HI,
                                    preferred_element_type=jnp.float32)


def chol_inv(gram):
    return pl.pallas_call(
        _chol_inv_kernel,
        out_shape=jax.ShapeDtypeStruct(gram.shape, jnp.float32),
        in_specs=[pl.BlockSpec(memory_space=pltpu.VMEM)],
        out_specs=pl.BlockSpec(memory_space=pltpu.VMEM),
    )(gram)


def _update_kernel(row_ref, col_ref, t_ref, o_ref):
    k = pl.program_id(0)
    width = row_ref.shape[2] // 2
    term = None
    for part in range(row_ref.shape[0]):
        x = row_ref[part]
        y = col_ref[part]
        middle = lax.dot_general(x[:, width:], y[:, :width], (((0,), (0,)), ((), ())),
                                 preferred_element_type=jnp.float32).astype(jnp.bfloat16)
        left = jnp.dot(x[:, :width], middle, preferred_element_type=jnp.float32).astype(jnp.bfloat16)
        piece = lax.dot_general(left, y[:, width:], (((1,), (1,)), ((), ())),
                                preferred_element_type=jnp.float32)
        term = piece if term is None else term + piece

    @pl.when(k == 0)
    def _():
        o_ref[...] = t_ref[...].astype(jnp.float32) - term

    @pl.when(k > 0)
    def _():
        o_ref[...] -= term


def trailing_update(full_row, full_col, trailing):
    depth, rows, both = full_row.shape
    cols = full_col.shape[1]
    return pl.pallas_call(
        _update_kernel,
        out_shape=jax.ShapeDtypeStruct((rows, cols), jnp.float32),
        grid=(depth // 4,),
        in_specs=[
            pl.BlockSpec((4, rows, both), lambda k: (k, 0, 0)),
            pl.BlockSpec((4, cols, both), lambda k: (k, 0, 0)),
            pl.BlockSpec((rows, cols), lambda k: (0, 0)),
        ],
        out_specs=pl.BlockSpec((rows, cols), lambda k: (0, 0)),
        compiler_params=pltpu.CompilerParams(
            dimension_semantics=("arbitrary",), vmem_limit_bytes=48 * 1024 * 1024
        ),
    )(full_row, full_col, trailing)


MESH_ID = pl.DeviceIdType.MESH


def _row_exchange_kernel(s_ref, o_ref, sems, own_sem):
    n_row = lax.axis_size("row")
    rows = o_ref.shape[2]
    me = lax.axis_index("row")
    c0 = lax.axis_index("col_0")
    c1 = lax.axis_index("col_1")
    c2 = lax.axis_index("col_2")

    def row_dev(o):
        return (o, c0, c1, c2)

    barrier = pltpu.get_barrier_semaphore()
    for step in range(1, n_row):
        pl.semaphore_signal(barrier, 1, device_id=row_dev(lax.rem(me + step, n_row)),
                            device_id_type=MESH_ID)
    pl.semaphore_wait(barrier, n_row - 1)
    copies = []
    for step in range(1, n_row):
        target = lax.rem(me + step, n_row)
        copies.append(pltpu.make_async_remote_copy(
            src_ref=s_ref.at[:, pl.ds(target * rows, rows)], dst_ref=o_ref.at[:, me],
            send_sem=sems.at[0, step], recv_sem=sems.at[1, step],
            device_id=row_dev(target), device_id_type=MESH_ID))
    for cp in copies:
        cp.start()
    own = pltpu.make_async_copy(s_ref.at[:, pl.ds(me * rows, rows)], o_ref.at[:, me], own_sem.at[0])
    own.start()
    own.wait()
    for cp in copies:
        cp.wait()


def exchange_rows(sent, n_row, channel):
    cap, total, width = sent.shape
    rows = total // n_row
    out = pl.pallas_call(
        _row_exchange_kernel,
        out_shape=jax.ShapeDtypeStruct((cap, n_row, rows, width), sent.dtype),
        in_specs=[pl.BlockSpec(memory_space=pl.ANY)],
        out_specs=pl.BlockSpec(memory_space=pl.ANY),
        scratch_shapes=[pltpu.SemaphoreType.DMA((2, n_row)), pltpu.SemaphoreType.DMA((1,))],
        compiler_params=pltpu.CompilerParams(collective_id=channel, has_side_effects=True),
    )(sent)
    return out.reshape(cap, total, width)


COL = ("col_0", "col_1", "col_2")


def cut_along(value, dim, size):
    before, after = (value.shape[:dim], value.shape[dim + 1 :])
    return jnp.moveaxis(value.reshape(*before, size, -1, *after), dim, 0)


def laid_out(tiles, dim):
    tiles = jnp.moveaxis(tiles, 0, dim)
    lengths = tiles.shape
    return tiles.reshape(*lengths[:dim], lengths[dim] * lengths[dim + 1], *lengths[dim + 2 :])


def turned_blocks(tiles, axes, turns):
    inside = tiles.shape[1:]
    result = tiles.reshape(*(lax.axis_size(a) for a in axes), *inside)
    for k in turns:
        result = lax.all_to_all(result, axes[k], k, k, tiled=True)
    return result.reshape(-1, *inside)


def exchange_by_chip(value, groups, turns, split_dim, concat_dim):
    size = lax.axis_size(groups[0]) * lax.axis_size(groups[1])
    tiles = cut_along(value, split_dim, size)
    return laid_out(turned_blocks(tiles, groups, turns), concat_dim)


def piece_ends(length, count):
    unit = 8 if length >= 8 * count else 1
    return [length // unit * k // count * unit for k in range(1, count)]


def cut_exchange(value, axis, pieces, split_dim, concat_dim):
    tiles = cut_along(value, split_dim, lax.axis_size(axis))
    cut = max(range(1, max(2, tiles.ndim - 1)), key=lambda d: tiles.shape[d])
    gathered = []
    for share in jnp.split(tiles, piece_ends(tiles.shape[cut], pieces), axis=cut):
        if share.size:
            gathered.append(lax.all_to_all(share, axis, split_axis=0, concat_axis=0, tiled=True))
    return laid_out(jnp.concatenate(gathered, axis=cut), concat_dim)


def compress_batch(panel_tiles, tile_ranks, sketch_cols):
    keep_cols = jnp.arange(sketch_cols.shape[1])[None, :] < tile_ranks[:, None]
    masked = jnp.where(keep_cols[:, None, :], sketch_cols[None], jnp.zeros_like(sketch_cols)[None])
    sketched = jnp.einsum("bij,bjk->bik", panel_tiles, masked, preferred_element_type=jnp.float32)
    padding = jnp.where(keep_cols, 0.0, 1.0).astype(jnp.float32)
    gram = jnp.einsum("bij,bik->bjk", sketched, sketched, precision=lax.Precision.HIGH)
    gram = gram + padding[:, :, None] * jnp.eye(gram.shape[1], dtype=jnp.float32)[None]
    gram = (gram + jnp.swapaxes(gram, 1, 2)) * 0.5
    inverse = chol_inv(gram)
    basis = jnp.einsum(
        "bij,bkj->bik", sketched, inverse, precision=lax.Precision.HIGH,
        preferred_element_type=jnp.float32,
    ).astype(jnp.bfloat16)
    coeffs = jnp.einsum(
        "bij,bik->bjk", panel_tiles, basis, preferred_element_type=jnp.float32
    ).astype(jnp.bfloat16)
    return jnp.concatenate([basis, coeffs], axis=2)


def slot_numbers(helpers):
    total = helpers.shape[0]
    same_helper = helpers[:, None] == helpers[None, :]
    earlier = jnp.arange(total)[None, :] < jnp.arange(total)[:, None]
    return jnp.sum(jnp.logical_and(same_helper, earlier).astype(jnp.int32), axis=1)


def pack_slabs(slabs, helpers, slots, owners, capacity):
    target = slots * owners + helpers
    hits = jnp.arange(capacity * owners)[:, None] == target[None, :]
    source = jnp.sum(jnp.where(hits, jnp.arange(slabs.shape[0])[None, :], 0), axis=1)
    found = jnp.any(hits, axis=1)
    packed = jnp.where(found[:, None, None], jnp.take(slabs, source, axis=0), jnp.zeros_like(slabs[:1]))
    return packed.reshape(capacity, owners * slabs.shape[1], slabs.shape[2])


def slot_ranks(ranks, helpers, slots, myself, capacity):
    chosen = jnp.logical_and(
        helpers[None, :] == myself, slots[None, :] == jnp.arange(capacity)[:, None]
    )
    return jnp.sum(jnp.where(chosen, ranks[None, :], 0), axis=1)


def pick_mine(returned, helpers, slots, capacity):
    return jnp.take(returned, helpers * capacity + slots, axis=0)


def local(trailing, raw_l, raw_u, sketch, helper_l, helper_u, ranks_l, ranks_u):
    depth = raw_l.shape[1]
    width_r = sketch.shape[3]
    own_sketch = sketch[0, 0]
    compress_all = compress_batch
    col_count = lax.axis_size(COL)
    row_count = lax.axis_size("row")
    cap_row = 2 * depth // col_count
    cap_col = 2 * depth // row_count
    helpers_row = helper_l[0]
    slots_row = slot_numbers(helpers_row)
    sent_row = pack_slabs(raw_l[0], helpers_row, slots_row, col_count, cap_row)
    tiles_row = exchange_by_chip(sent_row, (("col_0", "col_1"), "col_2"), (1, 0), 1, 1)
    made_row = compress_all(
        tiles_row,
        slot_ranks(ranks_l[0], helpers_row, slots_row, lax.axis_index(COL), cap_row),
        own_sketch,
    )
    helpers_col = helper_u[:, 0]
    slots_col = slot_numbers(helpers_col)
    sent_col = pack_slabs(raw_u[:, 0], helpers_col, slots_col, row_count, cap_col)
    tiles_col = exchange_rows(sent_col, row_count, 0)
    made_col = compress_all(
        tiles_col,
        slot_ranks(ranks_u[:, 0], helpers_col, slots_col, lax.axis_index("row"), cap_col),
        own_sketch,
    )
    back_row = lax.all_to_all(made_row, COL, split_axis=1, concat_axis=0, tiled=True)
    full_row = lax.all_gather(
        pick_mine(back_row, helpers_row, slots_row, cap_row), COL, axis=1, tiled=True
    )
    back_col = exchange_rows(made_col, row_count, 1).reshape(
        cap_col * row_count, -1, made_col.shape[2]
    )
    mine_col = jnp.take(back_col, slots_col * row_count + helpers_col, axis=0)
    full_col = lax.all_gather(mine_col, "row", axis=1, tiled=True)
    return trailing_update(full_row, full_col, trailing)


def solution(mesh):
    torus = Mesh(
        mesh.devices.reshape(mesh.shape["row"], 2, 4, 2), ("row", "col_0", "col_1", "col_2")
    )
    in_specs = (
        P("row", COL),
        P("row", None, COL, None),
        P(None, COL, "row", None),
        P("row", COL, None, None),
        P("row", None),
        P(None, COL),
        P("row", None),
        P(None, COL),
    )
    out_specs = P("row", COL)
    return jax.shard_map(local, mesh=torus, in_specs=in_specs, out_specs=out_specs, check_vma=False)
```
